128 devices in a mesh: dp: 4 (over y), row: 8 (over x, core), col: 4 (over z).
Axes of the slice: x: 4, y: 4, z: 4, core: 2. Of those that a mesh axis runs over, the one named last changes fastest.
Arguments:
- patches: bfloat16 [8, 128, 128, 768], P('dp', 'row', 'col'), may hold values from -64 to 64
- keep_mask: int32 [8, 128, 128], P('dp', 'row', 'col'), may hold values from 0 to 1, as said below
- mask_token: bfloat16 [768], replicated, may hold values from -6 to 6
- qkv_weight: bfloat16 [768, 2304], replicated, may hold values from -2 to 2
- out_weight: bfloat16 [768, 768], replicated, may hold values from -0.21875 to 0.21875
- up_weight: bfloat16 [768, 3072], P(None, 'dp'), may hold values from -0.21875 to 0.21875
- down_weight: bfloat16 [3072, 768], P('dp'), may hold values from -0.109375 to 0.109375
- dec_proj: bfloat16 [768, 256], replicated, may hold values from -0.21875 to 0.21875
- conv_weight: bfloat16 [2, 9, 256, 256], replicated, may hold values from -0.125 to 0.125
- head_weight: bfloat16 [256, 128], replicated, may hold values from -0.375 to 0.375
Outputs:
- recon: bfloat16 [8, 128, 128, 128], P('dp', 'row', 'col')
The draws below stay inside these ranges and needn't reach their ends.
Inputs may be any that keep to these rules, and one draw needn't show every extreme that they name: `keep_mask`: each sample has exactly 4096 ones; in every sample the 16 x 32 tile of some device is all ones.
All inputs are finite; a program needn't handle non-finite values.
Results may differ from the reference program's by a relative error of at most 0.015.
Values may be sent and summed in bfloat16 or wider, within the bound.
No kernel may reach another device: no remote copies, remote signals or barrier semaphores. Data moves between devices by JAX's collectives and lax.ppermute only.
A program may use at most 192 MiB of HBM per device.

```python
import math
import jax
import jax.numpy as jnp
from jax import lax

D = 768
HEADS = 12
HD = 64
FFN = 3072
DEC = 256
OUT = 128
TH = 16
TW = 32
SAMPLES = 8
GH = 128
GW = 128
TOKENS = 16384
KEEP = 4096


def draw_keep_mask(key, part):
    tiles_w = GW // TW
    tiles_all = GH // TH * tiles_w
    cells = GH * GW

    def one_sample(sample_key):
        first_key, second_key, third_key, fourth_key = jax.random.split(sample_key, 4)
        bias = jax.random.randint(first_key, (tiles_all,), 0, 3) * 2
        chosen = jax.random.randint(second_key, (), 0, tiles_all)
        bias = jnp.where(jnp.arange(tiles_all) == chosen, 64, bias)
        noise = jax.random.randint(third_key, (GH, GW), 0, 16)
        breaker = jax.random.permutation(fourth_key, cells).astype(jnp.int32).reshape(GH, GW)
        tile_id = jnp.arange(GH)[:, None] // TH * tiles_w + jnp.arange(GW)[None, :] // TW
        score = ((noise + bias[tile_id]) * cells + breaker).reshape(-1)
        order = jnp.argsort(-score, stable=True)
        ranks = jnp.zeros((cells,), jnp.int32).at[order].set(jnp.arange(cells, dtype=jnp.int32))
        return (ranks < KEEP).astype(jnp.int32).reshape(GH, GW)
    return jax.vmap(one_sample)(jax.random.split(key, SAMPLES))


def draw_patches(key, part):
    first_key = jax.random.fold_in(key, 0)
    shape = (SAMPLES, GH, GW, D)
    values = jnp.clip(jax.random.normal(first_key, shape, jnp.float32), -6.0, 6.0)
    return values.astype(jnp.bfloat16)


def draw_qkv_weight(key, part):
    first_key = jax.random.fold_in(key, 0)
    base = jnp.clip(jax.random.normal(first_key, (D, 3 * D), jnp.float32), -4.0, 4.0)
    root = math.sqrt(D)
    query = base[:, :D] * (1.7 / root)
    keys = base[:, D:2 * D] * (1.7 / root)
    values = base[:, 2 * D:] / root
    return jnp.concatenate([query, keys, values], axis=1).astype(jnp.bfloat16)


def block_scale(key, dims, shards, low, high):
    gain, own = 1.0, jax.random.fold_in(key, 6)
    for axis_at, blocks in shards:
        steps = jnp.exp(jax.random.uniform(jax.random.fold_in(own, axis_at), (blocks,), jnp.float32, low / len(shards), high / len(shards)))
        gain = gain * jnp.repeat(steps, dims[axis_at] // blocks).reshape([-1 if axis == axis_at else 1 for axis in range(len(dims))])
    return gain


def gaussian(rng, extent, deviation, most, pieces=(), kind=jnp.bfloat16):
    entries = deviation * jax.random.normal(rng, extent, jnp.float32)
    if pieces:
        entries = entries * block_scale(rng, extent, pieces, -0.22, 0.18)
    return jnp.clip(entries, -most, most).astype(kind)


def setup_inputs(seed: int = 0) -> dict:
    seeds = jax.random.split(jax.random.key(seed), 11)
    patches = draw_patches(jax.random.fold_in(seeds[10], 71), 0)
    keep_mask = draw_keep_mask(jax.random.fold_in(seeds[10], 71), 0)
    mask_token = gaussian(seeds[2], (D,), 1.0, 6.0)
    qkv_weight = draw_qkv_weight(jax.random.fold_in(seeds[10], 71), 0)
    out_weight = gaussian(seeds[4], (D, D), D ** -0.5, 0.21875)
    up_weight = gaussian(seeds[5], (D, FFN), D ** -0.5, 0.21875, ((1, 4),))
    down_weight = gaussian(seeds[6], (FFN, D), FFN ** -0.5, 0.109375, ((0, 4),))
    dec_proj = gaussian(seeds[7], (D, DEC), D ** -0.5, 0.21875)
    conv_weight = gaussian(seeds[8], (2, 9, DEC, DEC), (9 * DEC) ** -0.5, 0.125)
    head_weight = gaussian(seeds[9], (DEC, OUT), DEC ** -0.5, 0.375)
    return dict(patches=patches, keep_mask=keep_mask, mask_token=mask_token, qkv_weight=qkv_weight, out_weight=out_weight, up_weight=up_weight, down_weight=down_weight, dec_proj=dec_proj, conv_weight=conv_weight, head_weight=head_weight)


EPS = 1e-06

def normalize(rows):
    wide = rows.astype(jnp.float32)
    mean = lax.optimization_barrier(jnp.mean(wide, -1, keepdims=True))
    centred = wide - mean
    var = lax.optimization_barrier(jnp.mean(centred * centred, -1, keepdims=True))
    return (centred * lax.rsqrt(var + EPS)).astype(jnp.bfloat16)

def encode(x, qkv_weight, out_weight, up_weight, down_weight):
    y = normalize(x)
    qkv = jnp.dot(y, qkv_weight, preferred_element_type=jnp.float32).astype(jnp.bfloat16)
    query = qkv[:, :D].reshape(KEEP, HEADS, HD).transpose(1, 0, 2)
    keys = qkv[:, D:2 * D].reshape(KEEP, HEADS, HD).transpose(1, 0, 2)
    values = qkv[:, 2 * D:].reshape(KEEP, HEADS, HD).transpose(1, 0, 2)

    def one_head(group):
        q_head, k_head, v_head = group
        scores = jnp.dot(q_head, k_head.T, preferred_element_type=jnp.float32) * 0.125
        top = lax.optimization_barrier(jnp.max(scores, -1, keepdims=True))
        expo = jnp.exp(scores - top)
        total = lax.optimization_barrier(jnp.sum(expo, -1, keepdims=True))
        mixed = jnp.dot(expo.astype(jnp.bfloat16), v_head, preferred_element_type=jnp.float32)
        return (mixed / total).astype(jnp.bfloat16)
    attn = lax.map(one_head, (query, keys, values)).transpose(1, 0, 2).reshape(KEEP, D)
    x1 = (x.astype(jnp.float32) + jnp.dot(attn, out_weight, preferred_element_type=jnp.float32)).astype(jnp.bfloat16)
    y2 = normalize(x1)
    hidden = jax.nn.gelu(jnp.dot(y2, up_weight, preferred_element_type=jnp.float32), approximate=False).astype(jnp.bfloat16)
    return (x1.astype(jnp.float32) + jnp.dot(hidden, down_weight, preferred_element_type=jnp.float32)).astype(jnp.bfloat16)

def convolve(field, taps):
    padded = jnp.pad(field, ((1, 1), (1, 1), (0, 0)))
    total = jnp.zeros((GH * GW, DEC), jnp.float32)
    for first in range(3):
        for second in range(3):
            window = padded[first:first + GH, second:second + GW].reshape(GH * GW, DEC)
            total = total + jnp.dot(window, taps[first * 3 + second], preferred_element_type=jnp.float32)
    return total.reshape(GH, GW, DEC)

def reference(patches, keep_mask, mask_token, qkv_weight, out_weight, up_weight, down_weight, dec_proj, conv_weight, head_weight):

    def one_sample(group):
        tokens, mask = group
        flat = tokens.reshape(TOKENS, D)
        mask_flat = mask.reshape(TOKENS)
        index = jnp.nonzero(mask_flat, size=KEEP)[0].astype(jnp.int32)
        x = flat[index]
        encoded = encode(x, qkv_weight, out_weight, up_weight, down_weight)
        placed = jnp.zeros((TOKENS, D), jnp.bfloat16).at[index].set(encoded)
        filled = jnp.where(mask_flat[:, None] == 1, placed, mask_token[None, :])
        h0 = jnp.dot(filled, dec_proj, preferred_element_type=jnp.float32).astype(jnp.bfloat16).reshape(GH, GW, DEC)
        h1 = (h0.astype(jnp.float32) + jax.nn.gelu(convolve(h0, conv_weight[0]), approximate=False)).astype(jnp.bfloat16)
        h2 = (h1.astype(jnp.float32) + jax.nn.gelu(convolve(h1, conv_weight[1]), approximate=False)).astype(jnp.bfloat16)
        return jnp.dot(h2.reshape(TOKENS, DEC), head_weight, preferred_element_type=jnp.float32).astype(jnp.bfloat16).reshape(GH, GW, OUT)
    return lax.map(one_sample, (patches, keep_mask))
```

```python
import jax
import jax.numpy as jnp
from jax import lax
from jax.experimental import pallas as pl
from jax.experimental.pallas import tpu as pltpu
from jax.sharding import PartitionSpec as P

HEADS = 12
HD = 64
EPS = 1e-06
LOG2E = 1.4426950408889634
ROOT_HALF = 0.7071067811865476
PLANE = ("row", "col")
MIB = 1 << 20


def extended_2(cells, sides, width):
    for axis, dim in sides:
        count = lax.axis_size(axis)
        ends = count - 1
        head = lax.slice_in_dim(cells, 0, width, axis=dim)
        tail = lax.slice_in_dim(cells, cells.shape[dim] - width, cells.shape[dim], axis=dim)
        cells = jnp.concatenate(
            [
                lax.ppermute(tail, axis, [(i, (i + 1) % count) for i in range(ends)]),
                cells,
                lax.ppermute(head, axis, [((i + 1) % count, i) for i in range(ends)]),
            ],
            axis=dim,
        )
    return cells


def normalize(wide):
    mean = jnp.mean(wide, -1, keepdims=True)
    centred = wide - mean
    var = jnp.mean(centred * centred, -1, keepdims=True)
    return (centred * lax.rsqrt(var + EPS)).astype(jnp.bfloat16)


def gelu(value):
    return 0.5 * value * (1.0 + lax.erf(value * ROOT_HALF))


def dot(left, right):
    return jnp.dot(left, right, preferred_element_type=jnp.float32)


def one_hot(left, right):
    return jnp.where(left == right, 1.0, 0.0).astype(jnp.bfloat16)


def convolve(extended, taps, out_h, out_w):
    total = None
    for first in range(3):
        for second in range(3):
            term = jnp.einsum(
                "shwc,cd->shwd",
                extended[:, first : first + out_h, second : second + out_w],
                taps[first * 3 + second],
                preferred_element_type=jnp.float32,
            )
            total = term if total is None else total + term
    return total


def params(limit):
    return pltpu.CompilerParams(vmem_limit_bytes=limit * MIB)


def dispatch(my_start, cell_rank, tokens, peers):
    samples, tile, width = tokens.shape
    cap = tile // peers

    def kernel(start_ref, rank_ref, token_ref, out_ref):
        start = start_ref[pl.program_id(0)]
        slot = lax.broadcasted_iota(jnp.int32, (tile, 1), 0)
        rank = (slot % cap) * peers + ((slot // cap - start) & (peers - 1))
        chosen = one_hot(rank, rank_ref[...].reshape(1, tile))
        rows = dot(chosen, token_ref[...].reshape(tile, width)).astype(jnp.bfloat16)
        out_ref[...] = rows.reshape(peers, 1, cap, width)

    return pl.pallas_call(
        kernel,
        grid_spec=pltpu.PrefetchScalarGridSpec(
            num_scalar_prefetch=1,
            grid=(samples,),
            in_specs=[
                pl.BlockSpec((1, 1, tile), lambda s, _: (s, 0, 0)),
                pl.BlockSpec((1, tile, width), lambda s, _: (s, 0, 0)),
            ],
            out_specs=pl.BlockSpec((peers, 1, cap, width), lambda s, _: (0, s, 0, 0)),
        ),
        out_shape=jax.ShapeDtypeStruct((peers, samples, cap, width), jnp.bfloat16),
        compiler_params=params(32),
        name="dispatch",
    )(my_start, cell_rank, tokens)


def project(arrived, token_col, qkv_weight, kept):
    peers, samples, cap, width = arrived.shape
    tile = peers * cap
    lanes = 2 * HD
    groups = width // lanes
    places = peers // samples
    half = kept // 2

    def kernel(col_ref, arrived_ref, weight_ref, x_ref, out_ref):
        token = lax.broadcasted_iota(jnp.int32, (kept, 1), 0)
        chosen = one_hot(token, col_ref[...].reshape(1, tile))
        x = dot(chosen, arrived_ref[...].reshape(tile, width))
        x_ref[...] = x.astype(jnp.bfloat16).reshape(1, kept, width)
        normed = normalize(x)
        qkv = dot(normed, weight_ref[...])
        low = lax.broadcasted_iota(jnp.int32, (kept, lanes), 1) < HD
        low_half = lax.broadcasted_iota(jnp.int32, (half, lanes), 1) < HD
        for group in range(groups):
            at = group * lanes
            q = qkv[:, at : at + lanes] * (0.125 * LOG2E)
            k = qkv[:, width + at : width + at + lanes]
            v = qkv[:, 2 * width + at : 2 * width + at + lanes]
            top, bottom = v[:half], v[half:]
            first = jnp.where(low, q, pltpu.roll(k, HD, 1))
            second = jnp.where(low, pltpu.roll(q, HD, 1), k)
            first_v = jnp.where(low_half, top, pltpu.roll(bottom, HD, 1))
            second_v = jnp.where(low_half, pltpu.roll(top, HD, 1), bottom)
            out_ref[2 * group, :kept] = first.astype(jnp.bfloat16)
            out_ref[2 * group, kept:] = first_v.astype(jnp.bfloat16)
            out_ref[2 * group + 1, :kept] = second.astype(jnp.bfloat16)
            out_ref[2 * group + 1, kept:] = second_v.astype(jnp.bfloat16)
        for place in range(2 * groups, places):
            out_ref[place] = jnp.zeros((kept + half, lanes), jnp.bfloat16)

    return pl.pallas_call(
        kernel,
        grid=(samples,),
        in_specs=[
            pl.BlockSpec((1, 1, tile), lambda s: (s, 0, 0)),
            pl.BlockSpec((peers, 1, cap, width), lambda s: (0, s, 0, 0)),
            pl.BlockSpec((width, 3 * width), lambda s: (0, 0)),
        ],
        out_specs=[
            pl.BlockSpec((1, kept, width), lambda s: (s, 0, 0)),
            pl.BlockSpec((places, kept + half, lanes), lambda s: (s, 0, 0)),
        ],
        out_shape=[
            jax.ShapeDtypeStruct((samples, kept, width), jnp.bfloat16),
            jax.ShapeDtypeStruct((peers, kept + half, lanes), jnp.bfloat16),
        ],
        compiler_params=params(48),
        name="project",
    )(token_col, arrived, qkv_weight)


def attention(packed, kept):
    peers, _, lanes = packed.shape
    half = kept // 2
    keys = peers * half
    step = 2

    def kernel(packed_ref, out_ref, low_key, high_key, value):
        at = pl.program_id(0)

        @pl.when(at == 0)
        def _():
            for peer in range(peers):
                rows = pl.ds(peer * half, half)
                both = pltpu.roll(packed_ref[peer, :kept].astype(jnp.float32), HD, 1)
                both = both.astype(jnp.bfloat16)
                low_key[rows] = both[:half]
                high_key[rows] = both[half:]
                value[rows, :lanes] = packed_ref[peer, kept:]
            value[:, lanes:] = jnp.ones((keys, lanes), jnp.bfloat16)

        query = packed_ref[pl.ds(at * step, step), :kept].reshape(step * kept, lanes)
        lane = lax.broadcasted_iota(jnp.int32, query.shape, 1)
        query = jnp.where(lane < HD, query, jnp.zeros_like(query))
        contract = (((1,), (1,)), ((), ()))
        low = lax.dot_general(query, low_key[...], contract, preferred_element_type=jnp.float32)
        high = lax.dot_general(query, high_key[...], contract, preferred_element_type=jnp.float32)
        top = jnp.maximum(jnp.max(low, -1, keepdims=True), jnp.max(high, -1, keepdims=True))
        low = jnp.exp2(low - top).astype(jnp.bfloat16)
        high = jnp.exp2(high - top).astype(jnp.bfloat16)
        low = dot(low, value[...])
        high = dot(high, value[...])
        total = low[:, lanes:] + high[:, lanes:]
        mixed = (low[:, :lanes] + pltpu.roll(high[:, :lanes], HD, 1)) / total
        mixed = mixed.reshape(step, 2, half, lanes)
        lane = lax.broadcasted_iota(jnp.int32, (half, lanes), 1)
        for one in range(step):
            both = jnp.where(lane < HD, mixed[one, 0], pltpu.roll(mixed[one, 1], HD, 1))
            out_ref[one] = both.astype(jnp.bfloat16)

    return pl.pallas_call(
        kernel,
        grid=(peers // step,),
        in_specs=[pl.BlockSpec(packed.shape, lambda i: (0, 0, 0))],
        out_specs=pl.BlockSpec((step, half, lanes), lambda i: (i, 0, 0)),
        out_shape=jax.ShapeDtypeStruct((peers, half, lanes), jnp.bfloat16),
        scratch_shapes=[
            pltpu.VMEM((keys, lanes), jnp.bfloat16),
            pltpu.VMEM((keys, lanes), jnp.bfloat16),
            pltpu.VMEM((keys, 2 * lanes), jnp.bfloat16),
        ],
        compiler_params=params(48),
        name="attention",
    )(packed)


def feed_forward(mixed, x, token_col, out_weight, up, down, dec_proj, cap):
    peers, half, lanes = mixed.shape
    samples, kept, width = x.shape
    places = peers // samples
    rows = samples * kept
    blocks, _, hidden = up.shape
    narrow = dec_proj.shape[1]
    tile = peers * cap

    def kernel(mixed_ref, x_ref, col_ref, out_w, up_ref, down_ref, dec_ref, out_ref, x_one, normed, total):
        at = pl.program_id(0)

        @pl.when(at == 0)
        def _():
            low = lax.broadcasted_iota(jnp.int32, (half, lanes), 1) < HD
            for sample in range(samples):
                parts = []
                for group in range(width // lanes):
                    one = mixed_ref[sample * places + 2 * group].astype(jnp.float32)
                    two = mixed_ref[sample * places + 2 * group + 1].astype(jnp.float32)
                    top = jnp.where(low, one, pltpu.roll(two, HD, 1))
                    bottom = jnp.where(low, pltpu.roll(one, HD, 1), two)
                    parts.append(jnp.concatenate([top, bottom], 0).astype(jnp.bfloat16))
                attn = jnp.concatenate(parts, 1)
                here = pl.ds(sample * kept, kept)
                added = x_ref[sample].astype(jnp.float32) + dot(attn, out_w[...])
                added = added.astype(jnp.bfloat16)
                x_one[here] = added
                normed[here] = normalize(added.astype(jnp.float32))
            total[...] = jnp.zeros_like(total)

        inner = gelu(dot(normed[...], up_ref[0])).astype(jnp.bfloat16)
        total[...] += dot(inner, down_ref[0])

        @pl.when(at == blocks - 1)
        def _():
            encoded = (x_one[...].astype(jnp.float32) + total[...]).astype(jnp.bfloat16)
            field = dot(encoded, dec_ref[...]).astype(jnp.bfloat16)
            for sample in range(samples):
                token = lax.broadcasted_iota(jnp.int32, (1, kept), 1)
                chosen = one_hot(col_ref[sample], token)
                sent = dot(chosen, field[sample * kept : (sample + 1) * kept])
                out_ref[:, sample] = sent.astype(jnp.bfloat16).reshape(peers, cap, narrow)

    def whole(shape):
        return pl.BlockSpec(shape, lambda i: (0,) * len(shape))

    return pl.pallas_call(
        kernel,
        grid=(blocks,),
        in_specs=[
            whole(mixed.shape),
            whole(x.shape),
            whole((samples, tile, 1)),
            whole(out_weight.shape),
            pl.BlockSpec((1, width, hidden), lambda i: (i, 0, 0)),
            pl.BlockSpec((1, hidden, width), lambda i: (i, 0, 0)),
            whole(dec_proj.shape),
        ],
        out_specs=whole((peers, samples, cap, narrow)),
        out_shape=jax.ShapeDtypeStruct((peers, samples, cap, narrow), jnp.bfloat16),
        scratch_shapes=[
            pltpu.VMEM((rows, width), jnp.bfloat16),
            pltpu.VMEM((rows, width), jnp.bfloat16),
            pltpu.VMEM((rows, width), jnp.float32),
        ],
        compiler_params=params(48),
        name="feed_forward",
    )(mixed, x, token_col, out_weight, up, down, dec_proj)


def place(home, cell_slot, mask_token, dec_proj):
    peers, samples, cap, narrow = home.shape
    tile = peers * cap
    width = dec_proj.shape[0]

    def kernel(slot_ref, home_ref, token_ref, dec_ref, out_ref):
        slot = slot_ref[0]
        chosen = one_hot(slot, lax.broadcasted_iota(jnp.int32, (1, tile), 1))
        rows = dot(chosen, home_ref[...].reshape(tile, narrow))
        blank = dot(jnp.broadcast_to(token_ref[...], (8, width)), dec_ref[...])[:1]
        out_ref[0] = jnp.where(slot < 0, blank, rows).astype(jnp.bfloat16)

    return pl.pallas_call(
        kernel,
        grid=(samples,),
        in_specs=[
            pl.BlockSpec((1, tile, 1), lambda s: (s, 0, 0)),
            pl.BlockSpec((peers, 1, cap, narrow), lambda s: (0, s, 0, 0)),
            pl.BlockSpec((1, width), lambda s: (0, 0)),
            pl.BlockSpec((width, narrow), lambda s: (0, 0)),
        ],
        out_specs=pl.BlockSpec((1, tile, narrow), lambda s: (s, 0, 0)),
        out_shape=jax.ShapeDtypeStruct((samples, tile, narrow), jnp.bfloat16),
        compiler_params=params(32),
        name="place",
    )(cell_slot, home, mask_token.reshape(1, width), dec_proj)


def inside(height, width, out_h, out_w, reach):
    row = lax.axis_index("row") * height - reach + jnp.arange(out_h, dtype=jnp.int32)
    col = lax.axis_index("col") * width - reach + jnp.arange(out_w, dtype=jnp.int32)
    row_in = (row >= 0) & (row < lax.axis_size("row") * height)
    col_in = (col >= 0) & (col < lax.axis_size("col") * width)
    return row_in[:, None] & col_in[None, :]


def shards(
    patches,
    keep_mask,
    mask_token,
    qkv_weight,
    out_weight,
    up_weight,
    down_weight,
    dec_proj,
    conv_weight,
    head_weight,
):
    peers = lax.axis_size(PLANE)
    me = lax.axis_index(PLANE)
    samples, tile_h, tile_w, width = patches.shape
    tile = tile_h * tile_w
    cap = tile // peers
    kept = tile // 4
    up = lax.all_gather(up_weight, "dp", axis=0)
    down = lax.all_gather(down_weight, "dp", axis=0)

    flat_mask = keep_mask.reshape(samples, tile)
    counts = jnp.sum(flat_mask, 1)
    told = lax.all_to_all(
        jnp.broadcast_to(counts[None, None, :], (peers, 1, samples)),
        PLANE,
        split_axis=0,
        concat_axis=0,
        tiled=True,
    ).reshape(peers, samples)
    before = jnp.arange(tile)[:, None] < jnp.arange(tile)[None, :]
    running = dot(flat_mask.astype(jnp.bfloat16), before.astype(jnp.bfloat16)).astype(jnp.int32)
    cell_rank = jnp.where(flat_mask == 1, running, -1)

    ids = jnp.arange(peers, dtype=jnp.int32)
    earlier = ids[:, None] < ids[None, :]
    starts = jnp.sum(jnp.where(earlier[:, :, None], told[:, None, :], 0), 0)
    my_start = jnp.sum(jnp.where((ids < me)[:, None], told, 0), 0)

    outgoing = dispatch(
        my_start, cell_rank.reshape(samples, 1, tile), patches.reshape(samples, tile, width), peers
    )
    arrived = lax.all_to_all(outgoing, PLANE, split_axis=0, concat_axis=0, tiled=True)

    slot = jnp.arange(cap, dtype=jnp.int32)[None, None, :]
    local = slot * peers + ((me - starts.T[:, :, None]) & (peers - 1))
    token = (starts.T[:, :, None] + local - me) // peers
    token = jnp.where(local < told.T[:, :, None], token, -1)

    x, packed = project(arrived, token.reshape(samples, 1, tile), qkv_weight, kept)
    packed = lax.all_to_all(packed, PLANE, split_axis=0, concat_axis=0, tiled=True)
    mixed = attention(packed, kept)
    mixed = lax.all_to_all(mixed, PLANE, split_axis=0, concat_axis=0, tiled=True)
    returning = feed_forward(
        mixed, x, token.reshape(samples, tile, 1), out_weight, up, down, dec_proj, cap
    )
    home = lax.all_to_all(returning, PLANE, split_axis=0, concat_axis=0, tiled=True)

    cell_slot = ((my_start[:, None] + running) & (peers - 1)) * cap + running // peers
    cell_slot = jnp.where(flat_mask == 1, cell_slot, -1)
    h_zero = place(home, cell_slot.reshape(samples, tile, 1), mask_token, dec_proj)
    h_zero = h_zero.reshape(samples, tile_h, tile_w, h_zero.shape[-1])
    h_zero = extended_2(h_zero, (("row", 1), ("col", 2)), 2)
    conv_one = convolve(h_zero, conv_weight[0], tile_h + 2, tile_w + 2)
    h_one = h_zero[:, 1:-1, 1:-1].astype(jnp.float32) + gelu(conv_one)
    within = inside(tile_h, tile_w, tile_h + 2, tile_w + 2, 1)
    h_one = jnp.where(within[None, :, :, None], h_one, 0.0).astype(jnp.bfloat16)
    conv_two = convolve(h_one, conv_weight[1], tile_h, tile_w)
    h_two = (h_one[:, 1:-1, 1:-1].astype(jnp.float32) + gelu(conv_two)).astype(jnp.bfloat16)
    return dot(h_two, head_weight).astype(jnp.bfloat16)


def solution(mesh):
    return jax.shard_map(
        shards,
        mesh=mesh,
        in_specs=(
            P("dp", "row", "col", None),
            P("dp", "row", "col"),
            P(),
            P(),
            P(),
            P(None, "dp"),
            P("dp", None),
            P(),
            P(),
            P(),
        ),
        out_specs=P("dp", "row", "col", None),
        check_vma=False,
    )
```

```python
import jax
import jax.numpy as jnp
from jax import lax
from jax.experimental import pallas as pl
from jax.experimental.pallas import tpu as pltpu
from jax.sharding import PartitionSpec as P


HD = 64
EPS = 1e-06
LOG2E = 1.4426950408889634
ROOT_HALF = 0.7071067811865476
PLANE = ("row", "col")
MIB = 1 << 20
ATTENTION_MIB = 40
SAFE = 96.0


def extended_2(cells, sides, width):
    for axis, dim in sides:
        count = lax.axis_size(axis)
        ends = count - 1
        head = lax.slice_in_dim(cells, 0, width, axis=dim)
        tail = lax.slice_in_dim(cells, cells.shape[dim] - width, cells.shape[dim], axis=dim)
        cells = jnp.concatenate(
            [
                lax.ppermute(tail, axis, [(i, (i + 1) % count) for i in range(ends)]),
                cells,
                lax.ppermute(head, axis, [((i + 1) % count, i) for i in range(ends)]),
            ],
            axis=dim,
        )
    return cells


def normalize(wide):
    mean = jnp.mean(wide, -1, keepdims=True)
    centred = wide - mean
    var = jnp.mean(centred * centred, -1, keepdims=True)
    return (centred * lax.rsqrt(var + EPS)).astype(jnp.bfloat16)


def gelu(value):
    return 0.5 * value * (1.0 + lax.erf(value * ROOT_HALF))


def dot(left, right):
    return jnp.dot(left, right, preferred_element_type=jnp.float32)


def one_hot(left, right):
    return jnp.where(left == right, 1.0, 0.0).astype(jnp.bfloat16)


def convolve(extended, taps, out_h, out_w):
    total = None
    for first in range(3):
        for second in range(3):
            term = jnp.einsum(
                "shwc,cd->shwd",
                extended[:, first : first + out_h, second : second + out_w],
                taps[first * 3 + second],
                preferred_element_type=jnp.float32,
            )
            total = term if total is None else total + term
    return total


def params(limit):
    return pltpu.CompilerParams(vmem_limit_bytes=limit * MIB)


def dispatch(my_start, cell_rank, tokens, peers):
    samples, tile, width = tokens.shape
    cap = tile // peers

    def kernel(start_ref, rank_ref, token_ref, out_ref):
        start = start_ref[pl.program_id(0)]
        slot = lax.broadcasted_iota(jnp.int32, (tile, 1), 0)
        rank = (slot % cap) * peers + ((slot // cap - start) & (peers - 1))
        chosen = one_hot(rank, rank_ref[...].reshape(1, tile))
        rows = dot(chosen, token_ref[...].reshape(tile, width)).astype(jnp.bfloat16)
        out_ref[...] = rows.reshape(peers, 1, cap, width)

    return pl.pallas_call(
        kernel,
        grid_spec=pltpu.PrefetchScalarGridSpec(
            num_scalar_prefetch=1,
            grid=(samples,),
            in_specs=[
                pl.BlockSpec((1, 1, tile), lambda s, _: (s, 0, 0)),
                pl.BlockSpec((1, tile, width), lambda s, _: (s, 0, 0)),
            ],
            out_specs=pl.BlockSpec((peers, 1, cap, width), lambda s, _: (0, s, 0, 0)),
        ),
        out_shape=jax.ShapeDtypeStruct((peers, samples, cap, width), jnp.bfloat16),
        compiler_params=params(32),
        name="dispatch",
    )(my_start, cell_rank, tokens)


def project(arrived, token_col, qkv_weight, kept):
    peers, samples, cap, width = arrived.shape
    tile = peers * cap
    lanes = 2 * HD
    groups = width // lanes
    places = peers // samples
    half = kept // 2

    def kernel(col_ref, arrived_ref, weight_ref, x_ref, out_ref):
        token = lax.broadcasted_iota(jnp.int32, (kept, 1), 0)
        chosen = one_hot(token, col_ref[...].reshape(1, tile))
        x = dot(chosen, arrived_ref[...].reshape(tile, width))
        x_ref[...] = x.astype(jnp.bfloat16).reshape(1, kept, width)
        normed = normalize(x)
        qkv = dot(normed, weight_ref[...])
        low = lax.broadcasted_iota(jnp.int32, (kept, lanes), 1) < HD
        low_half = lax.broadcasted_iota(jnp.int32, (half, lanes), 1) < HD
        for group in range(groups):
            at = group * lanes
            q = qkv[:, at : at + lanes] * (0.125 * LOG2E)
            k = qkv[:, width + at : width + at + lanes]
            v = qkv[:, 2 * width + at : 2 * width + at + lanes]
            top, bottom = v[:half], v[half:]
            first = jnp.where(low, q, pltpu.roll(k, HD, 1))
            second = jnp.where(low, pltpu.roll(q, HD, 1), k)
            first_v = jnp.where(low_half, top, pltpu.roll(bottom, HD, 1))
            second_v = jnp.where(low_half, pltpu.roll(top, HD, 1), bottom)
            out_ref[2 * group, :kept] = first.astype(jnp.bfloat16)
            out_ref[2 * group, kept:] = first_v.astype(jnp.bfloat16)
            out_ref[2 * group + 1, :kept] = second.astype(jnp.bfloat16)
            out_ref[2 * group + 1, kept:] = second_v.astype(jnp.bfloat16)
        for place in range(2 * groups, places):
            out_ref[place] = jnp.zeros((kept + half, lanes), jnp.bfloat16)

    return pl.pallas_call(
        kernel,
        grid=(samples,),
        in_specs=[
            pl.BlockSpec((1, 1, tile), lambda s: (s, 0, 0)),
            pl.BlockSpec((peers, 1, cap, width), lambda s: (0, s, 0, 0)),
            pl.BlockSpec((width, 3 * width), lambda s: (0, 0)),
        ],
        out_specs=[
            pl.BlockSpec((1, kept, width), lambda s: (s, 0, 0)),
            pl.BlockSpec((places, kept + half, lanes), lambda s: (s, 0, 0)),
        ],
        out_shape=[
            jax.ShapeDtypeStruct((samples, kept, width), jnp.bfloat16),
            jax.ShapeDtypeStruct((peers, kept + half, lanes), jnp.bfloat16),
        ],
        compiler_params=params(48),
        name="project",
    )(token_col, arrived, qkv_weight)


def attention(packed, kept):
    peers, _, lanes = packed.shape
    half = kept // 2
    keys = peers * half
    step = 8
    contract = (((1,), (1,)), ((), ()))

    def kernel(packed_ref, out_ref, low_key, high_key, value, bound):
        at = pl.program_id(0)

        @pl.when(at == 0)
        def _():
            lane = lax.broadcasted_iota(jnp.int32, (kept, lanes), 1)
            most_q = jnp.zeros((kept, 1), jnp.float32)
            most_k = jnp.zeros((kept, 1), jnp.float32)
            for peer in range(peers):
                rows = pl.ds(peer * half, half)
                wide = packed_ref[peer, :kept].astype(jnp.float32)
                both = pltpu.roll(wide, HD, 1).astype(jnp.bfloat16)
                low_key[rows] = both[:half]
                high_key[rows] = both[half:]
                value[rows, :lanes] = packed_ref[peer, kept:]
                square = wide * wide
                size_q = jnp.sum(jnp.where(lane < HD, square, 0.0), -1, keepdims=True)
                size_k = jnp.sum(jnp.where(lane < HD, 0.0, square), -1, keepdims=True)
                most_q = jnp.maximum(most_q, size_q)
                most_k = jnp.maximum(most_k, size_k)
            value[:, lanes:] = jnp.ones((keys, lanes), jnp.bfloat16)
            bound[0] = jnp.max(most_q) * jnp.max(most_k)

        def finish(low, high, first, count):
            total = low[:, lanes:] + high[:, lanes:]
            mixed = (low[:, :lanes] + pltpu.roll(high[:, :lanes], HD, 1)) / total
            mixed = mixed.reshape(count, 2, half, lanes)
            lane = lax.broadcasted_iota(jnp.int32, (half, lanes), 1)
            for one in range(count):
                both = jnp.where(lane < HD, mixed[one, 0], pltpu.roll(mixed[one, 1], HD, 1))
                out_ref[first + one] = both.astype(jnp.bfloat16)

        def queries(first, count):
            query = packed_ref[pl.ds(at * step + first, count), :kept].reshape(count * kept, lanes)
            lane = lax.broadcasted_iota(jnp.int32, query.shape, 1)
            return jnp.where(lane < HD, query, jnp.zeros_like(query))

        def score(query, key):
            return lax.dot_general(query, key[...], contract, preferred_element_type=jnp.float32)

        narrow = bound[0] < SAFE * SAFE

        @pl.when(narrow)
        def _():
            query = queries(0, step)
            low = jnp.exp2(score(query, low_key)).astype(jnp.bfloat16)
            high = jnp.exp2(score(query, high_key)).astype(jnp.bfloat16)
            finish(dot(low, value[...]), dot(high, value[...]), 0, step)

        @pl.when(jnp.logical_not(narrow))
        def _():
            @pl.loop(0, step)
            def _(one):
                query = queries(one, 1)
                low, high = score(query, low_key), score(query, high_key)
                top = jnp.maximum(jnp.max(low, -1, keepdims=True), jnp.max(high, -1, keepdims=True))
                low = jnp.exp2(low - top).astype(jnp.bfloat16)
                high = jnp.exp2(high - top).astype(jnp.bfloat16)
                finish(dot(low, value[...]), dot(high, value[...]), one, 1)

    return pl.pallas_call(
        kernel,
        grid=(peers // step,),
        in_specs=[pl.BlockSpec(packed.shape, lambda i: (0, 0, 0))],
        out_specs=pl.BlockSpec((step, half, lanes), lambda i: (i, 0, 0)),
        out_shape=jax.ShapeDtypeStruct((peers, half, lanes), jnp.bfloat16),
        scratch_shapes=[
            pltpu.VMEM((keys, lanes), jnp.bfloat16),
            pltpu.VMEM((keys, lanes), jnp.bfloat16),
            pltpu.VMEM((keys, 2 * lanes), jnp.bfloat16),
            pltpu.SMEM((1,), jnp.float32),
        ],
        compiler_params=params(ATTENTION_MIB),
        name="attention",
    )(packed)


def feed_forward(mixed, x, token_col, out_weight, up, down, dec_proj, pieces, cap):
    peers, half, lanes = mixed.shape
    samples, kept, width = x.shape
    places = peers // samples
    narrow = dec_proj.shape[1]

    def kernel(mixed_ref, x_ref, col_ref, out_w, up_ref, down_ref, dec_ref, *rest):
        *piece_refs, out_ref = rest
        low = lax.broadcasted_iota(jnp.int32, (half, lanes), 1) < HD
        attn = []
        for sample in range(samples):
            parts = []
            for group in range(width // lanes):
                one = mixed_ref[sample * places + 2 * group].astype(jnp.float32)
                two = mixed_ref[sample * places + 2 * group + 1].astype(jnp.float32)
                top = jnp.where(low, one, pltpu.roll(two, HD, 1))
                bottom = jnp.where(low, pltpu.roll(one, HD, 1), two)
                parts.append(jnp.concatenate([top, bottom], 0).astype(jnp.bfloat16))
            attn.append(jnp.concatenate(parts, 1))
        attn = jnp.concatenate(attn, 0)
        rows = x_ref[...].reshape(samples * kept, width)
        x_one = (rows.astype(jnp.float32) + dot(attn, out_w[...])).astype(jnp.bfloat16)
        normed = normalize(x_one.astype(jnp.float32))
        total = dot(gelu(dot(normed, up_ref[...])).astype(jnp.bfloat16), down_ref[...])
        for piece in piece_refs:
            part = piece.shape[1]
            inner = gelu(dot(normed, piece[:width])).astype(jnp.bfloat16)
            added = [dot(inner, piece[pl.ds(at, part)]) for at in range(width, piece.shape[0], part)]
            total = total + jnp.concatenate(added, 1)
        encoded = (x_one.astype(jnp.float32) + total).astype(jnp.bfloat16)
        field = dot(encoded, dec_ref[...]).astype(jnp.bfloat16)
        for sample in range(samples):
            token = lax.broadcasted_iota(jnp.int32, (1, kept), 1)
            chosen = one_hot(col_ref[sample], token)
            sent = dot(chosen, field[sample * kept : (sample + 1) * kept])
            out_ref[:, sample] = sent.astype(jnp.bfloat16).reshape(peers, cap, narrow)

    operands = (mixed, x, token_col, out_weight, up, down, dec_proj, *pieces)
    return pl.pallas_call(
        kernel,
        in_specs=[pl.BlockSpec(memory_space=pltpu.VMEM)] * len(operands),
        out_specs=pl.BlockSpec(memory_space=pltpu.VMEM),
        out_shape=jax.ShapeDtypeStruct((peers, samples, cap, narrow), jnp.bfloat16),
        compiler_params=params(40),
        name="feed_forward",
    )(*operands)


def share(up_weight, down_weight):
    width, hidden = up_weight.shape
    part = hidden // 2
    at = (lax.axis_index("row") % 2) * part
    up = lax.dynamic_slice_in_dim(up_weight, at, part, axis=1)
    down = lax.dynamic_slice_in_dim(down_weight, at, part, axis=0)
    return jnp.concatenate([up] + [down[:, i : i + part] for i in range(0, width, part)], 0)


def from_dp(piece):
    count = lax.axis_size("dp")
    return [
        lax.ppermute(piece, "dp", [(i, (i + hop) % count) for i in range(count)])
        for hop in range(1, count)
    ]


def from_partner(piece):
    return lax.ppermute(piece, "row", [(i, i ^ 1) for i in range(lax.axis_size("row"))])


def place(home, cell_slot, mask_token, dec_proj):
    peers, samples, cap, narrow = home.shape
    tile = peers * cap
    width = dec_proj.shape[0]

    def kernel(slot_ref, home_ref, token_ref, dec_ref, out_ref):
        slot = slot_ref[0]
        chosen = one_hot(slot, lax.broadcasted_iota(jnp.int32, (1, tile), 1))
        rows = dot(chosen, home_ref[...].reshape(tile, narrow))
        blank = dot(jnp.broadcast_to(token_ref[...], (8, width)), dec_ref[...])[:1]
        out_ref[0] = jnp.where(slot < 0, blank, rows).astype(jnp.bfloat16)

    return pl.pallas_call(
        kernel,
        grid=(samples,),
        in_specs=[
            pl.BlockSpec((1, tile, 1), lambda s: (s, 0, 0)),
            pl.BlockSpec((peers, 1, cap, narrow), lambda s: (0, s, 0, 0)),
            pl.BlockSpec((1, width), lambda s: (0, 0)),
            pl.BlockSpec((width, narrow), lambda s: (0, 0)),
        ],
        out_specs=pl.BlockSpec((1, tile, narrow), lambda s: (s, 0, 0)),
        out_shape=jax.ShapeDtypeStruct((samples, tile, narrow), jnp.bfloat16),
        compiler_params=params(32),
        name="place",
    )(cell_slot, home, mask_token.reshape(1, width), dec_proj)


def inside(height, width, out_h, out_w, reach):
    row = lax.axis_index("row") * height - reach + jnp.arange(out_h, dtype=jnp.int32)
    col = lax.axis_index("col") * width - reach + jnp.arange(out_w, dtype=jnp.int32)
    row_in = (row >= 0) & (row < lax.axis_size("row") * height)
    col_in = (col >= 0) & (col < lax.axis_size("col") * width)
    return row_in[:, None] & col_in[None, :]


def shards(
    patches,
    keep_mask,
    mask_token,
    qkv_weight,
    out_weight,
    up_weight,
    down_weight,
    dec_proj,
    conv_weight,
    head_weight,
):
    peers = lax.axis_size(PLANE)
    me = lax.axis_index(PLANE)
    samples, tile_h, tile_w, width = patches.shape
    tile = tile_h * tile_w
    cap = tile // peers
    kept = tile // 4
    piece = share(up_weight, down_weight)

    flat_mask = keep_mask.reshape(samples, tile)
    counts = jnp.sum(flat_mask, 1)
    told = lax.all_to_all(
        jnp.broadcast_to(counts[None, None, :], (peers, 1, samples)),
        PLANE,
        split_axis=0,
        concat_axis=0,
        tiled=True,
    ).reshape(peers, samples)
    before = jnp.arange(tile)[:, None] < jnp.arange(tile)[None, :]
    running = dot(flat_mask.astype(jnp.bfloat16), before.astype(jnp.bfloat16)).astype(jnp.int32)
    cell_rank = jnp.where(flat_mask == 1, running, -1)

    ids = jnp.arange(peers, dtype=jnp.int32)
    earlier = ids[:, None] < ids[None, :]
    starts = jnp.sum(jnp.where(earlier[:, :, None], told[:, None, :], 0), 0)
    my_start = jnp.sum(jnp.where((ids < me)[:, None], told, 0), 0)

    outgoing = dispatch(
        my_start, cell_rank.reshape(samples, 1, tile), patches.reshape(samples, tile, width), peers
    )
    outgoing, piece = lax.optimization_barrier((outgoing, piece))
    pieces = from_dp(piece)
    arrived = lax.all_to_all(outgoing, PLANE, split_axis=0, concat_axis=0, tiled=True)

    slot = jnp.arange(cap, dtype=jnp.int32)[None, None, :]
    local = slot * peers + ((me - starts.T[:, :, None]) & (peers - 1))
    token = (starts.T[:, :, None] + local - me) // peers
    token = jnp.where(local < told.T[:, :, None], token, -1)

    x, packed = project(arrived, token.reshape(samples, 1, tile), qkv_weight, kept)
    packed = lax.all_to_all(packed, PLANE, split_axis=0, concat_axis=0, tiled=True)
    mixed = attention(packed, kept)
    mixed, *pieces = lax.optimization_barrier((mixed, *pieces))
    pieces = pieces + [from_partner(one) for one in pieces]
    mixed = lax.all_to_all(mixed, PLANE, split_axis=0, concat_axis=0, tiled=True)
    returning = feed_forward(
        mixed,
        x,
        token.reshape(samples, tile, 1),
        out_weight,
        up_weight,
        down_weight,
        dec_proj,
        pieces,
        cap,
    )
    home = lax.all_to_all(returning, PLANE, split_axis=0, concat_axis=0, tiled=True)

    cell_slot = ((my_start[:, None] + running) & (peers - 1)) * cap + running // peers
    cell_slot = jnp.where(flat_mask == 1, cell_slot, -1)
    h_zero = place(home, cell_slot.reshape(samples, tile, 1), mask_token, dec_proj)
    h_zero = h_zero.reshape(samples, tile_h, tile_w, h_zero.shape[-1])
    h_zero = extended_2(h_zero, (("row", 1), ("col", 2)), 2)
    conv_one = convolve(h_zero, conv_weight[0], tile_h + 2, tile_w + 2)
    h_one = h_zero[:, 1:-1, 1:-1].astype(jnp.float32) + gelu(conv_one)
    within = inside(tile_h, tile_w, tile_h + 2, tile_w + 2, 1)
    h_one = jnp.where(within[None, :, :, None], h_one, 0.0).astype(jnp.bfloat16)
    conv_two = convolve(h_one, conv_weight[1], tile_h, tile_w)
    h_two = (h_one[:, 1:-1, 1:-1].astype(jnp.float32) + gelu(conv_two)).astype(jnp.bfloat16)
    return dot(h_two, head_weight).astype(jnp.bfloat16)


def solution(mesh):
    return jax.shard_map(
        shards,
        mesh=mesh,
        in_specs=(
            P("dp", "row", "col", None),
            P("dp", "row", "col"),
            P(),
            P(),
            P(),
            P(None, "dp"),
            P("dp", None),
            P(),
            P(),
            P(),
        ),
        out_specs=P("dp", "row", "col", None),
        check_vma=False,
    )
```

```python
import jax
import jax.numpy as jnp
import numpy as np
from jax import lax
from jax.experimental import pallas as pl
from jax.experimental.pallas import tpu as pltpu
from jax.sharding import PartitionSpec as P


HD = 64
EPS = 1e-06
LOG2E = 1.4426950408889634
ROOT_HALF = 0.7071067811865476
PLANE = ("row", "col")
MIB = 1 << 20
ATTENTION_MIB = 34
SAFE = 96.0


def extended_2(cells, sides, width):
    for axis, dim in sides:
        count = lax.axis_size(axis)
        ends = count - 1
        head = lax.slice_in_dim(cells, 0, width, axis=dim)
        tail = lax.slice_in_dim(cells, cells.shape[dim] - width, cells.shape[dim], axis=dim)
        cells = jnp.concatenate(
            [
                lax.ppermute(tail, axis, [(i, (i + 1) % count) for i in range(ends)]),
                cells,
                lax.ppermute(head, axis, [((i + 1) % count, i) for i in range(ends)]),
            ],
            axis=dim,
        )
    return cells


def ring(height, width):
    low, high = slice(0, REACH), slice(-REACH, None)
    mid = slice(REACH, -REACH)
    order = np.zeros((height, width), np.int32)
    ends = [0]
    for rows, cols in (
        (low, low),
        (low, mid),
        (low, high),
        (mid, high),
        (high, high),
        (high, mid),
        (high, low),
        (mid, low),
        (mid, mid),
    ):
        block = order[rows, cols]
        block[...] = ends[-1] + np.arange(block.size, dtype=np.int32).reshape(block.shape)
        ends.append(ends[-1] + block.size)
    return order, np.array(ends, np.int32)


PIECES = (
    (0, 0, 0, 9, 16),
    (-1, 0, 4, 7, 2),
    (1, 0, 0, 3, 2),
    (0, -1, 2, 5, 1),
    (0, 1, 6, 8, 1),
    (0, 1, 0, 1, 1),
    (-1, -1, 4, 5, 1),
    (-1, 1, 6, 7, 1),
    (1, -1, 2, 3, 1),
    (1, 1, 0, 1, 1),
)
REACH = 2
SLOTS = 32


def normalize(wide):
    mean = jnp.mean(wide, -1, keepdims=True)
    centred = wide - mean
    var = jnp.mean(centred * centred, -1, keepdims=True)
    return (centred * lax.rsqrt(var + EPS)).astype(jnp.bfloat16)


def gelu(value):
    return 0.5 * value * (1.0 + lax.erf(value * ROOT_HALF))


def dot(left, right):
    return jnp.dot(left, right, preferred_element_type=jnp.float32)


def one_hot(left, right):
    return jnp.where(left == right, 1.0, 0.0).astype(jnp.bfloat16)


def convolve(extended, taps, out_h, out_w):
    total = None
    for first in range(3):
        for second in range(3):
            term = jnp.einsum(
                "shwc,cd->shwd",
                extended[:, first : first + out_h, second : second + out_w],
                taps[first * 3 + second],
                preferred_element_type=jnp.float32,
            )
            total = term if total is None else total + term
    return total


def in_hbm(array):
    return pltpu.with_memory_space_constraint(array, pltpu.HBM)


def params(limit):
    return pltpu.CompilerParams(vmem_limit_bytes=limit * MIB)


def dispatch(my_start, cell_rank, tokens, peers):
    samples, tile, width = tokens.shape
    cap = tile // peers

    def kernel(start_ref, rank_ref, token_ref, out_ref):
        start = start_ref[pl.program_id(0)]
        slot = lax.broadcasted_iota(jnp.int32, (tile, 1), 0)
        rank = (slot % cap) * peers + ((slot // cap - start) & (peers - 1))
        chosen = one_hot(rank, rank_ref[...].reshape(1, tile))
        rows = dot(chosen, token_ref[...].reshape(tile, width)).astype(jnp.bfloat16)
        out_ref[...] = rows.reshape(peers, 1, cap, width)

    return pl.pallas_call(
        kernel,
        grid_spec=pltpu.PrefetchScalarGridSpec(
            num_scalar_prefetch=1,
            grid=(samples,),
            in_specs=[
                pl.BlockSpec((1, 1, tile), lambda s, _: (s, 0, 0)),
                pl.BlockSpec((1, tile, width), lambda s, _: (s, 0, 0)),
            ],
            out_specs=pl.BlockSpec((peers, 1, cap, width), lambda s, _: (0, s, 0, 0)),
        ),
        out_shape=jax.ShapeDtypeStruct((peers, samples, cap, width), jnp.bfloat16),
        compiler_params=params(32),
        name="dispatch",
    )(my_start, cell_rank, tokens)


def project(arrived, token_col, qkv_weight, kept):
    peers, samples, cap, width = arrived.shape
    tile = peers * cap
    lanes = 2 * HD
    groups = width // lanes
    places = peers // samples
    half = kept // 2

    def kernel(col_ref, arrived_ref, weight_hbm, x_ref, out_ref, weight, sems):
        copies = []
        for third in range(3):
            cols = pl.ds(third * width, width)
            copies.append(
                pltpu.make_async_copy(weight_hbm.at[:, cols], weight.at[third], sems.at[third])
            )
            copies[-1].start()
        token = lax.broadcasted_iota(jnp.int32, (kept, 1), 0)
        rows = []
        for sample in range(samples):
            chosen = one_hot(token, col_ref[sample])
            rows.append(dot(chosen, arrived_ref[:, sample].reshape(tile, width)))
            x_ref[sample] = rows[-1].astype(jnp.bfloat16)
        normed = normalize(jnp.concatenate(rows, 0))
        qkv = []
        for third in range(3):
            copies[third].wait()
            qkv.append(dot(normed, weight[third]))
        low = lax.broadcasted_iota(jnp.int32, (kept, lanes), 1) < HD
        low_half = lax.broadcasted_iota(jnp.int32, (half, lanes), 1) < HD
        for sample in range(samples):
            q_all, k_all, v_all = (one[sample * kept : (sample + 1) * kept] for one in qkv)
            for group in range(groups):
                at = group * lanes
                to = sample * places + 2 * group
                q = q_all[:, at : at + lanes] * (0.125 * LOG2E)
                k = k_all[:, at : at + lanes]
                v = v_all[:, at : at + lanes]
                top, bottom = v[:half], v[half:]
                first = jnp.where(low, q, pltpu.roll(k, HD, 1))
                second = jnp.where(low, pltpu.roll(q, HD, 1), k)
                first_v = jnp.where(low_half, top, pltpu.roll(bottom, HD, 1))
                second_v = jnp.where(low_half, pltpu.roll(top, HD, 1), bottom)
                out_ref[to, :kept] = first.astype(jnp.bfloat16)
                out_ref[to, kept:] = first_v.astype(jnp.bfloat16)
                out_ref[to + 1, :kept] = second.astype(jnp.bfloat16)
                out_ref[to + 1, kept:] = second_v.astype(jnp.bfloat16)
            for place in range(2 * groups, places):
                out_ref[sample * places + place] = jnp.zeros((kept + half, lanes), jnp.bfloat16)

    return pl.pallas_call(
        kernel,
        in_specs=[pl.BlockSpec(memory_space=pltpu.VMEM)] * 2 + [pl.BlockSpec(memory_space=pltpu.HBM)],
        out_specs=[pl.BlockSpec(memory_space=pltpu.VMEM)] * 2,
        out_shape=[
            jax.ShapeDtypeStruct((samples, kept, width), jnp.bfloat16),
            jax.ShapeDtypeStruct((peers, kept + half, lanes), jnp.bfloat16),
        ],
        scratch_shapes=[
            pltpu.VMEM((3, width, width), jnp.bfloat16),
            pltpu.SemaphoreType.DMA((3,)),
        ],
        compiler_params=params(20),
        name="project",
    )(token_col, arrived, in_hbm(qkv_weight))


def attention(packed, kept):
    peers, _, lanes = packed.shape
    half = kept // 2
    keys = peers * half
    step = 8
    contract = (((1,), (1,)), ((), ()))

    def kernel(packed_ref, out_ref, low_key, high_key, value, bound):
        at = pl.program_id(0)

        @pl.when(at == 0)
        def _():
            lane = lax.broadcasted_iota(jnp.int32, (kept, lanes), 1)
            most_q = jnp.zeros((kept, 1), jnp.float32)
            most_k = jnp.zeros((kept, 1), jnp.float32)
            for peer in range(peers):
                rows = pl.ds(peer * half, half)
                wide = packed_ref[peer, :kept].astype(jnp.float32)
                both = pltpu.roll(wide, HD, 1).astype(jnp.bfloat16)
                low_key[rows] = both[:half]
                high_key[rows] = both[half:]
                value[rows, :lanes] = packed_ref[peer, kept:]
                square = wide * wide
                size_q = jnp.sum(jnp.where(lane < HD, square, 0.0), -1, keepdims=True)
                size_k = jnp.sum(jnp.where(lane < HD, 0.0, square), -1, keepdims=True)
                most_q = jnp.maximum(most_q, size_q)
                most_k = jnp.maximum(most_k, size_k)
            value[:, lanes:] = jnp.ones((keys, lanes), jnp.bfloat16)
            bound[0] = jnp.max(most_q) * jnp.max(most_k)

        def finish(low, high, first, count):
            total = low[:, lanes:] + high[:, lanes:]
            mixed = (low[:, :lanes] + pltpu.roll(high[:, :lanes], HD, 1)) / total
            mixed = mixed.reshape(count, 2, half, lanes)
            lane = lax.broadcasted_iota(jnp.int32, (half, lanes), 1)
            for one in range(count):
                both = jnp.where(lane < HD, mixed[one, 0], pltpu.roll(mixed[one, 1], HD, 1))
                out_ref[first + one] = both.astype(jnp.bfloat16)

        def queries(first, count):
            query = packed_ref[pl.ds(at * step + first, count), :kept].reshape(count * kept, lanes)
            lane = lax.broadcasted_iota(jnp.int32, query.shape, 1)
            return jnp.where(lane < HD, query, jnp.zeros_like(query))

        def score(query, key):
            return lax.dot_general(query, key[...], contract, preferred_element_type=jnp.float32)

        narrow = bound[0] < SAFE * SAFE

        @pl.when(narrow)
        def _():
            query = queries(0, step)
            low = jnp.exp2(score(query, low_key)).astype(jnp.bfloat16)
            high = jnp.exp2(score(query, high_key)).astype(jnp.bfloat16)
            finish(dot(low, value[...]), dot(high, value[...]), 0, step)

        @pl.when(jnp.logical_not(narrow))
        def _():
            @pl.loop(0, step)
            def _(one):
                query = queries(one, 1)
                low, high = score(query, low_key), score(query, high_key)
                top = jnp.maximum(jnp.max(low, -1, keepdims=True), jnp.max(high, -1, keepdims=True))
                low = jnp.exp2(low - top).astype(jnp.bfloat16)
                high = jnp.exp2(high - top).astype(jnp.bfloat16)
                finish(dot(low, value[...]), dot(high, value[...]), one, 1)

    return pl.pallas_call(
        kernel,
        grid=(peers // step,),
        in_specs=[pl.BlockSpec(packed.shape, lambda i: (0, 0, 0))],
        out_specs=pl.BlockSpec((step, half, lanes), lambda i: (i, 0, 0)),
        out_shape=jax.ShapeDtypeStruct((peers, half, lanes), jnp.bfloat16),
        scratch_shapes=[
            pltpu.VMEM((keys, lanes), jnp.bfloat16),
            pltpu.VMEM((keys, lanes), jnp.bfloat16),
            pltpu.VMEM((keys, 2 * lanes), jnp.bfloat16),
            pltpu.SMEM((1,), jnp.float32),
        ],
        compiler_params=params(ATTENTION_MIB),
        name="attention",
    )(packed)


def feed_forward(mixed, x, token_col, out_weight, up, down, dec_proj, pieces, slots):
    peers, half, lanes = mixed.shape
    samples, kept, width = x.shape
    places = peers // samples
    narrow = dec_proj.shape[1]

    weights = [in_hbm(one) for one in (out_weight, up, down, *pieces, dec_proj)]
    count = len(weights)

    def kernel(mixed_ref, x_ref, col_ref, *rest):
        sources, out_ref, held, sems = rest[:count], rest[count], rest[count + 1 : -1], rest[-1]
        copies = [
            pltpu.make_async_copy(source, held[at], sems.at[at])
            for at, source in enumerate(sources)
        ]
        for copy in copies:
            copy.start()

        def ready(at):
            copies[at].wait()
            return held[at]

        low = lax.broadcasted_iota(jnp.int32, (half, lanes), 1) < HD
        attn = []
        for sample in range(samples):
            parts = []
            for group in range(width // lanes):
                one = mixed_ref[sample * places + 2 * group].astype(jnp.float32)
                two = mixed_ref[sample * places + 2 * group + 1].astype(jnp.float32)
                top = jnp.where(low, one, pltpu.roll(two, HD, 1))
                bottom = jnp.where(low, pltpu.roll(one, HD, 1), two)
                parts.append(jnp.concatenate([top, bottom], 0).astype(jnp.bfloat16))
            attn.append(jnp.concatenate(parts, 1))
        attn = jnp.concatenate(attn, 0)
        rows = x_ref[...].reshape(samples * kept, width)
        x_one = (rows.astype(jnp.float32) + dot(attn, ready(0)[...])).astype(jnp.bfloat16)
        normed = normalize(x_one.astype(jnp.float32))
        inner = gelu(dot(normed, ready(1)[...])).astype(jnp.bfloat16)
        total = dot(inner, ready(2)[...])
        for at in range(3, count - 1):
            piece = ready(at)
            part = piece.shape[1]
            inner = gelu(dot(normed, piece[:width])).astype(jnp.bfloat16)
            added = [dot(inner, piece[pl.ds(at, part)]) for at in range(width, piece.shape[0], part)]
            total = total + jnp.concatenate(added, 1)
        encoded = (x_one.astype(jnp.float32) + total).astype(jnp.bfloat16)
        field = dot(encoded, ready(count - 1)[...]).astype(jnp.bfloat16)
        for sample in range(samples):
            token = lax.broadcasted_iota(jnp.int32, (1, kept), 1)
            chosen = one_hot(col_ref[sample], token)
            sent = dot(chosen, field[sample * kept : (sample + 1) * kept])
            out_ref[:, sample] = sent.astype(jnp.bfloat16).reshape(peers, slots, narrow)

    return pl.pallas_call(
        kernel,
        in_specs=[pl.BlockSpec(memory_space=pltpu.VMEM)] * 3
        + [pl.BlockSpec(memory_space=pltpu.HBM)] * count,
        out_specs=pl.BlockSpec(memory_space=pltpu.VMEM),
        out_shape=jax.ShapeDtypeStruct((peers, samples, slots, narrow), jnp.bfloat16),
        scratch_shapes=[pltpu.VMEM(one.shape, one.dtype) for one in weights]
        + [pltpu.SemaphoreType.DMA((count,))],
        compiler_params=params(32),
        name="feed_forward",
    )(mixed, x, token_col, *weights)


def share(up_weight, down_weight):
    width, hidden = up_weight.shape
    part = hidden // 2
    at = (lax.axis_index("row") % 2) * part
    up = lax.dynamic_slice_in_dim(up_weight, at, part, axis=1)
    down = lax.dynamic_slice_in_dim(down_weight, at, part, axis=0)
    return jnp.concatenate([up] + [down[:, i : i + part] for i in range(0, width, part)], 0)


def from_dp(piece):
    count = lax.axis_size("dp")
    return [
        lax.ppermute(piece, "dp", [(i, (i + hop) % count) for i in range(count)])
        for hop in range(1, count)
    ]


def from_partner(piece):
    return lax.ppermute(piece, "row", [(i, i ^ 1) for i in range(lax.axis_size("row"))])


def place(home, cell_slot, mask_token, dec_proj, cells):
    peers, samples, slots, narrow = home.shape
    width = dec_proj.shape[0]

    def kernel(slot_ref, home_ref, token_ref, dec_ref, out_ref):
        slot = slot_ref[0]
        chosen = one_hot(slot, lax.broadcasted_iota(jnp.int32, (1, peers * slots), 1))
        rows = dot(chosen, home_ref[...].reshape(peers * slots, narrow))
        blank = dot(jnp.broadcast_to(token_ref[...], (8, width)), dec_ref[...])[:1]
        out_ref[0] = jnp.where(slot == -1, blank, rows).astype(jnp.bfloat16)

    return pl.pallas_call(
        kernel,
        grid=(samples,),
        in_specs=[
            pl.BlockSpec((1, cells, 1), lambda s: (s, 0, 0)),
            pl.BlockSpec((peers, 1, slots, narrow), lambda s: (0, s, 0, 0)),
            pl.BlockSpec((1, width), lambda s: (0, 0)),
            pl.BlockSpec((width, narrow), lambda s: (0, 0)),
        ],
        out_specs=pl.BlockSpec((1, cells, narrow), lambda s: (s, 0, 0)),
        out_shape=jax.ShapeDtypeStruct((samples, cells, narrow), jnp.bfloat16),
        compiler_params=params(16),
        name="place",
    )(cell_slot, home, mask_token.reshape(1, width), dec_proj)


def pick(which, table):
    lane = lax.broadcasted_iota(jnp.int32, (1, table.shape[1]), 1)
    found = jnp.sum(jnp.where(which == lane, table, 0.0), -1, keepdims=True)
    return found.astype(jnp.int32)


def index(me, told, rank, tiles, tile_h, tile_w, wide):
    samples, peers, marks = told.shape
    tiles_h, tiles_w = tiles
    cells = rank.shape[1]
    bases = [sum(piece[4] for piece in PIECES[:number]) for number in range(len(PIECES))]

    def kernel(me_ref, told_ref, rank_ref, back_ref, slot_ref):
        me = me_ref[0]
        ahead = told_ref[0].astype(jnp.float32)
        tile = lax.broadcasted_iota(jnp.int32, (peers, 1), 0)
        other = lax.broadcasted_iota(jnp.int32, (1, peers), 1)
        earlier = jnp.where(other < tile, 1.0, 0.0)
        totals = jnp.broadcast_to(ahead[:, marks - 1 :], (peers, 128))
        starts = jnp.dot(
            earlier, totals, precision=lax.Precision.HIGHEST, preferred_element_type=jnp.float32
        )
        lane = lax.broadcasted_iota(jnp.int32, (1, 128), 1)
        begins = jnp.zeros((peers, 128), jnp.float32)
        ends = jnp.zeros((peers, 128), jnp.float32)
        for number, (down, right, first, last, _) in enumerate(PIECES):
            row, col = tile // tiles_w + down, tile % tiles_w + right
            there = (row >= 0) & (row < tiles_h) & (col >= 0) & (col < tiles_w) & (lane == number)
            for side, mark in enumerate((first, last)):
                value = ahead[:, mark : mark + 1] + starts
                hop = (-(down * tiles_w + right)) % peers
                if hop:
                    value = pltpu.roll(value, hop, 0)
                if side:
                    ends = jnp.where(there, value, ends)
                else:
                    begins = jnp.where(there, value, begins)

        at = lax.broadcasted_iota(jnp.int32, (peers * SLOTS, 1), 0)
        expand = jnp.where(at // SLOTS == other, 1.0, 0.0)
        at = at % SLOTS
        which = jnp.full(at.shape, len(PIECES), jnp.int32)
        nth = jnp.zeros(at.shape, jnp.int32)
        for number, base in enumerate(bases):
            here = (at >= base) & (at < base + PIECES[number][4])
            which = jnp.where(here, number, which)
            nth = jnp.where(here, at - base, nth)

        def spread(table):
            rows = jnp.dot(
                expand, table, precision=lax.Precision.HIGHEST, preferred_element_type=jnp.float32
            )
            return pick(which, rows)

        position = (spread(begins) - me + peers - 1) // peers + nth
        back_ref[0] = jnp.where(position * peers + me < spread(ends), position, -1)

        cell = lax.broadcasted_iota(jnp.int32, (cells, 1), 0)
        row, col = cell // wide, cell % wide
        side = [(col < REACH), (col >= REACH + tile_w)]
        which = jnp.where(row < REACH, 1, jnp.where(row >= REACH + tile_h, 2, 0))
        right = jnp.where(row < 2 * REACH, 5, 4)
        left = jnp.where(which == 0, 3, jnp.where(which == 1, 6, 8))
        right = jnp.where(which == 0, right, jnp.where(which == 1, 7, 9))
        which = jnp.where(side[0], left, jnp.where(side[1], right, which))
        base = jnp.zeros(cell.shape, jnp.int32)
        for number in range(1, len(bases)):
            base = jnp.where(which == number, bases[number], base)
        mine = jnp.sum(jnp.where(tile == me, begins, 0.0), 0, keepdims=True)
        rank = rank_ref[0] - 1
        peer = rank & (peers - 1)
        nth = rank // peers - (pick(which, mine) - peer + peers - 1) // peers
        row = row + (me // tiles_w) * tile_h - REACH
        col = col + (me % tiles_w) * tile_w - REACH
        within = (row >= 0) & (row < tiles_h * tile_h) & (col >= 0) & (col < tiles_w * tile_w)
        slot = jnp.where(rank >= 0, peer * SLOTS + base + nth, -1)
        slot_ref[0] = jnp.where(within, slot, -2)

    return pl.pallas_call(
        kernel,
        grid_spec=pltpu.PrefetchScalarGridSpec(
            num_scalar_prefetch=1,
            grid=(samples,),
            in_specs=[
                pl.BlockSpec((1, peers, marks), lambda s, _: (s, 0, 0)),
                pl.BlockSpec((1, cells, 1), lambda s, _: (s, 0, 0)),
            ],
            out_specs=[
                pl.BlockSpec((1, peers * SLOTS, 1), lambda s, _: (s, 0, 0)),
                pl.BlockSpec((1, cells, 1), lambda s, _: (s, 0, 0)),
            ],
        ),
        out_shape=[
            jax.ShapeDtypeStruct((samples, peers * SLOTS, 1), jnp.int32),
            jax.ShapeDtypeStruct((samples, cells, 1), jnp.int32),
        ],
        compiler_params=params(16),
        name="index",
    )(me.reshape(1), told, rank)


def inside(height, width, out_h, out_w, reach):
    row = lax.axis_index("row") * height - reach + jnp.arange(out_h, dtype=jnp.int32)
    col = lax.axis_index("col") * width - reach + jnp.arange(out_w, dtype=jnp.int32)
    row_in = (row >= 0) & (row < lax.axis_size("row") * height)
    col_in = (col >= 0) & (col < lax.axis_size("col") * width)
    return row_in[:, None] & col_in[None, :]


def shards(
    patches,
    keep_mask,
    mask_token,
    qkv_weight,
    out_weight,
    up_weight,
    down_weight,
    dec_proj,
    conv_weight,
    head_weight,
):
    peers = lax.axis_size(PLANE)
    me = lax.axis_index(PLANE)
    samples, tile_h, tile_w, width = patches.shape
    tile = tile_h * tile_w
    cap = tile // peers
    kept = tile // 4
    piece = share(up_weight, down_weight)

    flat_mask = keep_mask.reshape(samples, tile)
    order, ends = ring(tile_h, tile_w)
    order = jnp.asarray(order.reshape(-1))
    marks = len(ends)
    earlier = order[:, None] < jnp.asarray(ends)[None, :]
    counts = dot(flat_mask.astype(jnp.bfloat16), earlier.astype(jnp.bfloat16)).astype(jnp.int32)
    told = lax.all_to_all(
        jnp.broadcast_to(counts.reshape(1, 1, samples * marks), (peers, 1, samples * marks)),
        PLANE,
        split_axis=0,
        concat_axis=0,
        tiled=True,
    ).reshape(peers, samples, marks)
    segments = told
    told = told[:, :, -1]
    before = order[:, None] < order[None, :]
    running = dot(flat_mask.astype(jnp.bfloat16), before.astype(jnp.bfloat16)).astype(jnp.int32)
    cell_rank = jnp.where(flat_mask == 1, running, -1)

    ids = jnp.arange(peers, dtype=jnp.int32)
    earlier = ids[:, None] < ids[None, :]
    starts = jnp.sum(jnp.where(earlier[:, :, None], told[:, None, :], 0), 0)
    my_start = jnp.sum(jnp.where((ids < me)[:, None], told, 0), 0)

    outgoing = dispatch(
        my_start, cell_rank.reshape(samples, 1, tile), patches.reshape(samples, tile, width), peers
    )
    outgoing, piece = lax.optimization_barrier((outgoing, piece))
    pieces = from_dp(piece)
    arrived = lax.all_to_all(outgoing, PLANE, split_axis=0, concat_axis=0, tiled=True)

    slot = jnp.arange(cap, dtype=jnp.int32)[None, None, :]
    local = slot * peers + ((me - starts.T[:, :, None]) & (peers - 1))
    token = (starts.T[:, :, None] + local - me) // peers
    token = jnp.where(local < told.T[:, :, None], token, -1)

    rank = jnp.where(flat_mask == 1, my_start[:, None] + running + 1, 0)
    rank = rank.reshape(samples, tile_h, tile_w)
    rank = extended_2(rank, (("row", 1), ("col", 2)), REACH)
    tiles = lax.axis_size("row"), lax.axis_size("col")
    high, wide = tile_h + 2 * REACH, -(-(tile_w + 2 * REACH) // 8) * 8
    rank = jnp.pad(rank, ((0, 0), (0, 0), (0, wide - rank.shape[2])))
    back, cell_slot = index(
        me,
        segments.transpose(1, 0, 2),
        rank.reshape(samples, high * wide, 1),
        tiles,
        tile_h,
        tile_w,
        wide,
    )

    x, packed = project(arrived, token.reshape(samples, 1, tile), qkv_weight, kept)
    packed = lax.all_to_all(packed, PLANE, split_axis=0, concat_axis=0, tiled=True)
    mixed = attention(packed, kept)
    mixed, *pieces = lax.optimization_barrier((mixed, *pieces))
    pieces = pieces + [from_partner(one) for one in pieces]
    mixed = lax.all_to_all(mixed, PLANE, split_axis=0, concat_axis=0, tiled=True)
    returning = feed_forward(
        mixed,
        x,
        back,
        out_weight,
        up_weight,
        down_weight,
        dec_proj,
        pieces,
        SLOTS,
    )
    home = lax.all_to_all(returning, PLANE, split_axis=0, concat_axis=0, tiled=True)

    h_zero = place(home, cell_slot, mask_token, dec_proj, high * wide)
    h_zero = h_zero.reshape(samples, high, wide, h_zero.shape[-1])[:, :, : tile_w + 2 * REACH]
    conv_one = convolve(h_zero, conv_weight[0], tile_h + 2, tile_w + 2)
    h_one = h_zero[:, 1:-1, 1:-1].astype(jnp.float32) + gelu(conv_one)
    within = inside(tile_h, tile_w, tile_h + 2, tile_w + 2, 1)
    h_one = jnp.where(within[None, :, :, None], h_one, 0.0).astype(jnp.bfloat16)
    conv_two = convolve(h_one, conv_weight[1], tile_h, tile_w)
    h_two = (h_one[:, 1:-1, 1:-1].astype(jnp.float32) + gelu(conv_two)).astype(jnp.bfloat16)
    return dot(h_two, head_weight).astype(jnp.bfloat16)


def solution(mesh):
    return jax.shard_map(
        shards,
        mesh=mesh,
        in_specs=(
            P("dp", "row", "col", None),
            P("dp", "row", "col"),
            P(),
            P(),
            P(),
            P(None, "dp"),
            P("dp", None),
            P(),
            P(),
            P(),
        ),
        out_specs=P("dp", "row", "col", None),
        check_vma=False,
    )
```

```python
import jax
import jax.numpy as jnp
import numpy as np
from jax import lax
from jax.experimental import pallas as pl
from jax.experimental.pallas import tpu as pltpu
from jax.sharding import PartitionSpec as P


HD = 64
EPS = 1e-06
LOG2E = 1.4426950408889634
ROOT_HALF = 0.7071067811865476
PLANE = ("row", "col")
MIB = 1 << 20
ATTENTION_MIB = 34
SAFE = 96.0


def ring(height, width):
    bands = (slice(0, REACH), slice(REACH, -REACH), slice(-REACH, None))
    order = np.zeros((height, width), np.int32)
    ends = [0]
    for row, col in CORNERS + ((1, 1),):
        block = order[bands[row], bands[col]]
        block[...] = ends[-1] + np.arange(block.size, dtype=np.int32).reshape(block.shape)
        ends.append(ends[-1] + block.size)
    return order, np.array(ends, np.int32)


PIECES = (
    (0, 0, 0, 9, 16),
    (-1, 0, 4, 7, 2),
    (1, 0, 0, 3, 2),
    (0, -1, 2, 5, 1),
    (0, 1, 6, 8, 1),
    (0, 1, 0, 1, 1),
    (-1, -1, 4, 5, 1),
    (-1, 1, 6, 7, 1),
    (1, -1, 2, 3, 1),
    (1, 1, 0, 1, 1),
)
REACH = 2
SLOTS = 32
SIDES = ((-1, 0), (1, 0), (0, -1), (0, 1), (-1, -1), (-1, 1), (1, -1), (1, 1))
CORNERS = ((0, 0), (0, 1), (0, 2), (1, 2), (2, 2), (2, 1), (2, 0), (1, 0))


def normalize(wide):
    mean = jnp.mean(wide, -1, keepdims=True)
    centred = wide - mean
    var = jnp.mean(centred * centred, -1, keepdims=True)
    return (centred * lax.rsqrt(var + EPS)).astype(jnp.bfloat16)


def gelu(value):
    return 0.5 * value * (1.0 + lax.erf(value * ROOT_HALF))


def dot(left, right):
    return jnp.dot(left, right, preferred_element_type=jnp.float32)


def one_hot(left, right):
    return jnp.where(left == right, 1.0, 0.0).astype(jnp.bfloat16)


def convolve(extended, taps, out_h, out_w):
    total = None
    for first in range(3):
        for second in range(3):
            term = jnp.einsum(
                "shwc,cd->shwd",
                extended[:, first : first + out_h, second : second + out_w],
                taps[first * 3 + second],
                preferred_element_type=jnp.float32,
            )
            total = term if total is None else total + term
    return total


def in_hbm(array):
    return pltpu.with_memory_space_constraint(array, pltpu.HBM)


def params(limit):
    return pltpu.CompilerParams(vmem_limit_bytes=limit * MIB)


def dispatch(my_start, cell_rank, tokens, peers):
    samples, tile, width = tokens.shape
    cap = tile // peers

    def kernel(start_ref, rank_ref, token_ref, out_ref):
        start = start_ref[pl.program_id(0)]
        slot = lax.broadcasted_iota(jnp.int32, (tile, 1), 0)
        rank = (slot % cap) * peers + ((slot // cap - start) & (peers - 1))
        chosen = one_hot(rank, rank_ref[...].reshape(1, tile))
        rows = dot(chosen, token_ref[...].reshape(tile, width)).astype(jnp.bfloat16)
        out_ref[...] = rows.reshape(peers, 1, cap, width)

    return pl.pallas_call(
        kernel,
        grid_spec=pltpu.PrefetchScalarGridSpec(
            num_scalar_prefetch=1,
            grid=(samples,),
            in_specs=[
                pl.BlockSpec((1, 1, tile), lambda s, _: (s, 0, 0)),
                pl.BlockSpec((1, tile, width), lambda s, _: (s, 0, 0)),
            ],
            out_specs=pl.BlockSpec((peers, 1, cap, width), lambda s, _: (0, s, 0, 0)),
        ),
        out_shape=jax.ShapeDtypeStruct((peers, samples, cap, width), jnp.bfloat16),
        compiler_params=params(32),
        name="dispatch",
    )(my_start, cell_rank, tokens)


def project(arrived, token_col, qkv_weight, kept):
    peers, samples, cap, width = arrived.shape
    tile = peers * cap
    lanes = 2 * HD
    groups = width // lanes
    places = peers // samples
    half = kept // 2

    def kernel(col_ref, arrived_ref, weight_hbm, x_ref, out_ref, weight, sems):
        copies = []
        for third in range(3):
            cols = pl.ds(third * width, width)
            copies.append(
                pltpu.make_async_copy(weight_hbm.at[:, cols], weight.at[third], sems.at[third])
            )
            copies[-1].start()
        token = lax.broadcasted_iota(jnp.int32, (kept, 1), 0)
        rows = []
        for sample in range(samples):
            chosen = one_hot(token, col_ref[sample])
            rows.append(dot(chosen, arrived_ref[:, sample].reshape(tile, width)))
            x_ref[sample] = rows[-1].astype(jnp.bfloat16)
        normed = normalize(jnp.concatenate(rows, 0))
        qkv = []
        for third in range(3):
            copies[third].wait()
            qkv.append(dot(normed, weight[third]))
        low = lax.broadcasted_iota(jnp.int32, (kept, lanes), 1) < HD
        low_half = lax.broadcasted_iota(jnp.int32, (half, lanes), 1) < HD
        for sample in range(samples):
            q_all, k_all, v_all = (one[sample * kept : (sample + 1) * kept] for one in qkv)
            for group in range(groups):
                at = group * lanes
                to = sample * places + 2 * group
                q = q_all[:, at : at + lanes] * (0.125 * LOG2E)
                k = k_all[:, at : at + lanes]
                v = v_all[:, at : at + lanes]
                top, bottom = v[:half], v[half:]
                first = jnp.where(low, q, pltpu.roll(k, HD, 1))
                second = jnp.where(low, pltpu.roll(q, HD, 1), k)
                first_v = jnp.where(low_half, top, pltpu.roll(bottom, HD, 1))
                second_v = jnp.where(low_half, pltpu.roll(top, HD, 1), bottom)
                out_ref[to, :kept] = first.astype(jnp.bfloat16)
                out_ref[to, kept:] = first_v.astype(jnp.bfloat16)
                out_ref[to + 1, :kept] = second.astype(jnp.bfloat16)
                out_ref[to + 1, kept:] = second_v.astype(jnp.bfloat16)
            for place in range(2 * groups, places):
                out_ref[sample * places + place] = jnp.zeros((kept + half, lanes), jnp.bfloat16)

    return pl.pallas_call(
        kernel,
        in_specs=[pl.BlockSpec(memory_space=pltpu.VMEM)] * 2 + [pl.BlockSpec(memory_space=pltpu.HBM)],
        out_specs=[pl.BlockSpec(memory_space=pltpu.VMEM)] * 2,
        out_shape=[
            jax.ShapeDtypeStruct((samples, kept, width), jnp.bfloat16),
            jax.ShapeDtypeStruct((peers, kept + half, lanes), jnp.bfloat16),
        ],
        scratch_shapes=[
            pltpu.VMEM((3, width, width), jnp.bfloat16),
            pltpu.SemaphoreType.DMA((3,)),
        ],
        compiler_params=params(20),
        name="project",
    )(token_col, arrived, in_hbm(qkv_weight))


def attention(packed, kept):
    peers, _, lanes = packed.shape
    half = kept // 2
    keys = peers * half
    step = 8
    contract = (((1,), (1,)), ((), ()))

    def kernel(packed_ref, out_ref, low_key, high_key, value, bound):
        at = pl.program_id(0)

        @pl.when(at == 0)
        def _():
            lane = lax.broadcasted_iota(jnp.int32, (kept, lanes), 1)
            most_q = jnp.zeros((kept, 1), jnp.float32)
            most_k = jnp.zeros((kept, 1), jnp.float32)
            for peer in range(peers):
                rows = pl.ds(peer * half, half)
                wide = packed_ref[peer, :kept].astype(jnp.float32)
                both = pltpu.roll(wide, HD, 1).astype(jnp.bfloat16)
                low_key[rows] = both[:half]
                high_key[rows] = both[half:]
                value[rows, :lanes] = packed_ref[peer, kept:]
                square = wide * wide
                size_q = jnp.sum(jnp.where(lane < HD, square, 0.0), -1, keepdims=True)
                size_k = jnp.sum(jnp.where(lane < HD, 0.0, square), -1, keepdims=True)
                most_q = jnp.maximum(most_q, size_q)
                most_k = jnp.maximum(most_k, size_k)
            value[:, lanes:] = jnp.ones((keys, lanes), jnp.bfloat16)
            bound[0] = jnp.max(most_q) * jnp.max(most_k)

        def finish(low, high, first, count):
            total = low[:, lanes:] + high[:, lanes:]
            mixed = (low[:, :lanes] + pltpu.roll(high[:, :lanes], HD, 1)) / total
            mixed = mixed.reshape(count, 2, half, lanes)
            lane = lax.broadcasted_iota(jnp.int32, (half, lanes), 1)
            for one in range(count):
                both = jnp.where(lane < HD, mixed[one, 0], pltpu.roll(mixed[one, 1], HD, 1))
                out_ref[first + one] = both.astype(jnp.bfloat16)

        def queries(first, count):
            query = packed_ref[pl.ds(at * step + first, count), :kept].reshape(count * kept, lanes)
            lane = lax.broadcasted_iota(jnp.int32, query.shape, 1)
            return jnp.where(lane < HD, query, jnp.zeros_like(query))

        def score(query, key):
            return lax.dot_general(query, key[...], contract, preferred_element_type=jnp.float32)

        narrow = bound[0] < SAFE * SAFE

        @pl.when(narrow)
        def _():
            query = queries(0, step)
            low = jnp.exp2(score(query, low_key)).astype(jnp.bfloat16)
            high = jnp.exp2(score(query, high_key)).astype(jnp.bfloat16)
            finish(dot(low, value[...]), dot(high, value[...]), 0, step)

        @pl.when(jnp.logical_not(narrow))
        def _():
            @pl.loop(0, step)
            def _(one):
                query = queries(one, 1)
                low, high = score(query, low_key), score(query, high_key)
                top = jnp.maximum(jnp.max(low, -1, keepdims=True), jnp.max(high, -1, keepdims=True))
                low = jnp.exp2(low - top).astype(jnp.bfloat16)
                high = jnp.exp2(high - top).astype(jnp.bfloat16)
                finish(dot(low, value[...]), dot(high, value[...]), one, 1)

    return pl.pallas_call(
        kernel,
        grid=(peers // step,),
        in_specs=[pl.BlockSpec(packed.shape, lambda i: (0, 0, 0))],
        out_specs=pl.BlockSpec((step, half, lanes), lambda i: (i, 0, 0)),
        out_shape=jax.ShapeDtypeStruct((peers, half, lanes), jnp.bfloat16),
        scratch_shapes=[
            pltpu.VMEM((keys, lanes), jnp.bfloat16),
            pltpu.VMEM((keys, lanes), jnp.bfloat16),
            pltpu.VMEM((keys, 2 * lanes), jnp.bfloat16),
            pltpu.SMEM((1,), jnp.float32),
        ],
        compiler_params=params(ATTENTION_MIB),
        name="attention",
    )(packed)


def feed_forward(mixed, x, token_col, out_weight, up, down, dec_proj, pieces, slots):
    peers, half, lanes = mixed.shape
    samples, kept, width = x.shape
    places = peers // samples
    narrow = dec_proj.shape[1]

    weights = [in_hbm(one) for one in (out_weight, up, down, *pieces, dec_proj)]
    count = len(weights)

    def kernel(mixed_ref, x_ref, col_ref, *rest):
        sources, out_ref, held, sems = rest[:count], rest[count], rest[count + 1 : -1], rest[-1]
        copies = [
            pltpu.make_async_copy(source, held[at], sems.at[at])
            for at, source in enumerate(sources)
        ]
        for copy in copies:
            copy.start()

        def ready(at):
            copies[at].wait()
            return held[at]

        low = lax.broadcasted_iota(jnp.int32, (half, lanes), 1) < HD
        attn = []
        for sample in range(samples):
            parts = []
            for group in range(width // lanes):
                one = mixed_ref[sample * places + 2 * group].astype(jnp.float32)
                two = mixed_ref[sample * places + 2 * group + 1].astype(jnp.float32)
                top = jnp.where(low, one, pltpu.roll(two, HD, 1))
                bottom = jnp.where(low, pltpu.roll(one, HD, 1), two)
                parts.append(jnp.concatenate([top, bottom], 0).astype(jnp.bfloat16))
            attn.append(jnp.concatenate(parts, 1))
        attn = jnp.concatenate(attn, 0)
        rows = x_ref[...].reshape(samples * kept, width)
        x_one = (rows.astype(jnp.float32) + dot(attn, ready(0)[...])).astype(jnp.bfloat16)
        normed = normalize(x_one.astype(jnp.float32))
        inner = gelu(dot(normed, ready(1)[...])).astype(jnp.bfloat16)
        total = dot(inner, ready(2)[...])
        for at in range(3, count - 1):
            piece = ready(at)
            part = piece.shape[1]
            inner = gelu(dot(normed, piece[:width])).astype(jnp.bfloat16)
            added = [dot(inner, piece[pl.ds(at, part)]) for at in range(width, piece.shape[0], part)]
            total = total + jnp.concatenate(added, 1)
        encoded = (x_one.astype(jnp.float32) + total).astype(jnp.bfloat16)
        field = dot(encoded, ready(count - 1)[...]).astype(jnp.bfloat16)
        for sample in range(samples):
            token = lax.broadcasted_iota(jnp.int32, (1, kept), 1)
            chosen = one_hot(col_ref[sample], token)
            sent = dot(chosen, field[sample * kept : (sample + 1) * kept])
            out_ref[:, sample] = sent.astype(jnp.bfloat16).reshape(peers, slots, narrow)

    return pl.pallas_call(
        kernel,
        in_specs=[pl.BlockSpec(memory_space=pltpu.VMEM)] * 3
        + [pl.BlockSpec(memory_space=pltpu.HBM)] * count,
        out_specs=pl.BlockSpec(memory_space=pltpu.VMEM),
        out_shape=jax.ShapeDtypeStruct((peers, samples, slots, narrow), jnp.bfloat16),
        scratch_shapes=[pltpu.VMEM(one.shape, one.dtype) for one in weights]
        + [pltpu.SemaphoreType.DMA((count,))],
        compiler_params=params(32),
        name="feed_forward",
    )(mixed, x, token_col, *weights)


def share(up_weight, down_weight):
    width, hidden = up_weight.shape
    part = hidden // 2
    at = (lax.axis_index("row") % 2) * part
    up = lax.dynamic_slice_in_dim(up_weight, at, part, axis=1)
    down = lax.dynamic_slice_in_dim(down_weight, at, part, axis=0)
    return jnp.concatenate([up] + [down[:, i : i + part] for i in range(0, width, part)], 0)


def from_dp(piece):
    count = lax.axis_size("dp")
    return [
        lax.ppermute(piece, "dp", [(i, (i + hop) % count) for i in range(count)])
        for hop in range(1, count)
    ]


def from_partner(piece):
    return lax.ppermute(piece, "row", [(i, i ^ 1) for i in range(lax.axis_size("row"))])


def place(home, cell_slot, mask_token, dec_proj, cells):
    peers, samples, slots, narrow = home.shape
    width = dec_proj.shape[0]

    def kernel(slot_ref, home_ref, token_ref, dec_ref, out_ref):
        slot = slot_ref[0]
        chosen = one_hot(slot, lax.broadcasted_iota(jnp.int32, (1, peers * slots), 1))
        rows = dot(chosen, home_ref[...].reshape(peers * slots, narrow))
        blank = dot(jnp.broadcast_to(token_ref[...], (8, width)), dec_ref[...])[:1]
        out_ref[0] = jnp.where(slot == -1, blank, rows).astype(jnp.bfloat16)

    return pl.pallas_call(
        kernel,
        grid=(samples,),
        in_specs=[
            pl.BlockSpec((1, cells, 1), lambda s: (s, 0, 0)),
            pl.BlockSpec((peers, 1, slots, narrow), lambda s: (0, s, 0, 0)),
            pl.BlockSpec((1, width), lambda s: (0, 0)),
            pl.BlockSpec((width, narrow), lambda s: (0, 0)),
        ],
        out_specs=pl.BlockSpec((1, cells, narrow), lambda s: (s, 0, 0)),
        out_shape=jax.ShapeDtypeStruct((samples, cells, narrow), jnp.bfloat16),
        compiler_params=params(16),
        name="place",
    )(cell_slot, home, mask_token.reshape(1, width), dec_proj)


def pick(which, table):
    lane = lax.broadcasted_iota(jnp.int32, (1, table.shape[1]), 1)
    found = jnp.sum(jnp.where(which == lane, table, 0.0), -1, keepdims=True)
    return found.astype(jnp.int32)


def index(me, told, rank, cuts, tiles, tile_h, tile_w, wide):
    samples, peers, width = told.shape
    marks = len(cuts)
    edge = width - marks
    tiles_h, tiles_w = tiles
    cells = rank.shape[1]
    bases = [sum(piece[4] for piece in PIECES[:number]) for number in range(len(PIECES))]

    def kernel(me_ref, told_ref, rank_ref, back_ref, slot_ref):
        me = me_ref[0]
        ahead = told_ref[0][:, :marks].astype(jnp.float32)
        bits = told_ref[0][:, marks:].astype(jnp.float32)
        tile = lax.broadcasted_iota(jnp.int32, (peers, 1), 0)
        other = lax.broadcasted_iota(jnp.int32, (1, peers), 1)
        earlier = jnp.where(other < tile, 1.0, 0.0)
        totals = jnp.broadcast_to(ahead[:, marks - 1 :], (peers, 128))
        starts = jnp.dot(
            earlier, totals, precision=lax.Precision.HIGHEST, preferred_element_type=jnp.float32
        )
        lane = lax.broadcasted_iota(jnp.int32, (1, 128), 1)
        begins = jnp.zeros((peers, 128), jnp.float32)
        ends = jnp.zeros((peers, 128), jnp.float32)
        for number, (down, right, first, last, _) in enumerate(PIECES):
            row, col = tile // tiles_w + down, tile % tiles_w + right
            there = (row >= 0) & (row < tiles_h) & (col >= 0) & (col < tiles_w) & (lane == number)
            for side, mark in enumerate((first, last)):
                value = ahead[:, mark : mark + 1] + starts
                hop = (-(down * tiles_w + right)) % peers
                if hop:
                    value = pltpu.roll(value, hop, 0)
                if side:
                    ends = jnp.where(there, value, ends)
                else:
                    begins = jnp.where(there, value, begins)

        at = lax.broadcasted_iota(jnp.int32, (peers * SLOTS, 1), 0)
        expand = jnp.where(at // SLOTS == other, 1.0, 0.0)
        at = at % SLOTS
        which = jnp.full(at.shape, len(PIECES), jnp.int32)
        nth = jnp.zeros(at.shape, jnp.int32)
        for number, base in enumerate(bases):
            here = (at >= base) & (at < base + PIECES[number][4])
            which = jnp.where(here, number, which)
            nth = jnp.where(here, at - base, nth)

        def spread(table):
            rows = jnp.dot(
                expand, table, precision=lax.Precision.HIGHEST, preferred_element_type=jnp.float32
            )
            return pick(which, rows)

        position = (spread(begins) - me + peers - 1) // peers + nth
        back_ref[0] = jnp.where(position * peers + me < spread(ends), position, -1)

        cell = lax.broadcasted_iota(jnp.int32, (cells, 1), 0)
        row, col = cell // wide, cell % wide
        side = [(col < REACH), (col >= REACH + tile_w)]
        which = jnp.where(row < REACH, 1, jnp.where(row >= REACH + tile_h, 2, 0))
        right = jnp.where(row < 2 * REACH, 5, 4)
        left = jnp.where(which == 0, 3, jnp.where(which == 1, 6, 8))
        right = jnp.where(which == 0, right, jnp.where(which == 1, 7, 9))
        which = jnp.where(side[0], left, jnp.where(side[1], right, which))
        base = jnp.zeros(cell.shape, jnp.int32)
        for number in range(1, len(bases)):
            base = jnp.where(which == number, bases[number], base)
        mine = jnp.sum(jnp.where(tile == me, begins, 0.0), 0, keepdims=True)

        one = lax.broadcasted_iota(jnp.int32, (edge, 1), 0)
        two = lax.broadcasted_iota(jnp.int32, (1, edge), 1)
        ranks = dot(bits.astype(jnp.bfloat16), jnp.where(one < two, 1.0, 0.0).astype(jnp.bfloat16))
        ranks = jnp.where(bits > 0.5, ranks + starts[:, :1] + 1.0, 0.0)
        number = lax.broadcasted_iota(jnp.int32, (128, 1), 0)
        there = jnp.full((128, 1), -1, jnp.int32)
        for at, (down, right) in enumerate(SIDES):
            there = jnp.where(number == at, me + down * tiles_w + right, there)
        chosen = jnp.where(there == other, 1.0, 0.0)
        table = jnp.dot(
            chosen, ranks, precision=lax.Precision.HIGHEST, preferred_element_type=jnp.float32
        )
        i, j = (row - REACH) % tile_h, (col - REACH) % tile_w
        down = jnp.where(row < REACH, -1, jnp.where(row >= REACH + tile_h, 1, 0))
        right = jnp.where(side[0], -1, jnp.where(side[1], 1, 0))
        place = jnp.zeros(cell.shape, jnp.int32)
        for at, (top, left) in enumerate(CORNERS):
            rows = ((i < REACH), (i >= REACH) & (i < tile_h - REACH), (i >= tile_h - REACH))[top]
            cols = ((j < REACH), (j >= REACH) & (j < tile_w - REACH), (j >= tile_w - REACH))[left]
            first_i = (0, REACH, tile_h - REACH)[top]
            first_j = (0, REACH, tile_w - REACH)[left]
            span = tile_w - 2 * REACH if left == 1 else REACH
            found = int(cuts[at]) + (i - first_i) * span + (j - first_j)
            place = jnp.where(rows & cols, found, place)
        spot = jnp.where(place == two, 1.0, 0.0)
        border = lax.dot_general(
            spot,
            table,
            (((1,), (1,)), ((), ())),
            precision=lax.Precision.HIGHEST,
            preferred_element_type=jnp.float32,
        )
        which_side = jnp.full(cell.shape, -1, jnp.int32)
        for at, (one_down, one_right) in enumerate(SIDES):
            which_side = jnp.where((down == one_down) & (right == one_right), at, which_side)
        own = jnp.sum(jnp.where(tile == me, starts[:, :1], 0.0), 0, keepdims=True).astype(jnp.int32)
        rank = jnp.where(rank_ref[0] > 0, rank_ref[0] + own, 0)
        rank = jnp.where(which_side >= 0, pick(which_side, border), rank) - 1
        peer = rank & (peers - 1)
        nth = rank // peers - (pick(which, mine) - peer + peers - 1) // peers
        row = row + (me // tiles_w) * tile_h - REACH
        col = col + (me % tiles_w) * tile_w - REACH
        within = (row >= 0) & (row < tiles_h * tile_h) & (col >= 0) & (col < tiles_w * tile_w)
        slot = jnp.where(rank >= 0, peer * SLOTS + base + nth, -1)
        slot_ref[0] = jnp.where(within, slot, -2)

    return pl.pallas_call(
        kernel,
        grid_spec=pltpu.PrefetchScalarGridSpec(
            num_scalar_prefetch=1,
            grid=(samples,),
            in_specs=[
                pl.BlockSpec((1, peers, width), lambda s, _: (s, 0, 0)),
                pl.BlockSpec((1, cells, 1), lambda s, _: (s, 0, 0)),
            ],
            out_specs=[
                pl.BlockSpec((1, peers * SLOTS, 1), lambda s, _: (s, 0, 0)),
                pl.BlockSpec((1, cells, 1), lambda s, _: (s, 0, 0)),
            ],
        ),
        out_shape=[
            jax.ShapeDtypeStruct((samples, peers * SLOTS, 1), jnp.int32),
            jax.ShapeDtypeStruct((samples, cells, 1), jnp.int32),
        ],
        compiler_params=params(16),
        name="index",
    )(me.reshape(1), told, rank)


def inside(height, width, out_h, out_w, reach):
    row = lax.axis_index("row") * height - reach + jnp.arange(out_h, dtype=jnp.int32)
    col = lax.axis_index("col") * width - reach + jnp.arange(out_w, dtype=jnp.int32)
    row_in = (row >= 0) & (row < lax.axis_size("row") * height)
    col_in = (col >= 0) & (col < lax.axis_size("col") * width)
    return row_in[:, None] & col_in[None, :]


def shards(
    patches,
    keep_mask,
    mask_token,
    qkv_weight,
    out_weight,
    up_weight,
    down_weight,
    dec_proj,
    conv_weight,
    head_weight,
):
    peers = lax.axis_size(PLANE)
    me = lax.axis_index(PLANE)
    samples, tile_h, tile_w, width = patches.shape
    tile = tile_h * tile_w
    cap = tile // peers
    kept = tile // 4
    piece = share(up_weight, down_weight)

    flat_mask = keep_mask.reshape(samples, tile)
    order, ends = ring(tile_h, tile_w)
    order = jnp.asarray(order.reshape(-1))
    marks, edge = len(ends), int(ends[-2])
    sums = order[:, None] < jnp.asarray(ends)[None, :]
    bits = order[:, None] == jnp.arange(edge, dtype=jnp.int32)[None, :]
    sums = jnp.concatenate([sums, bits], 1).astype(jnp.bfloat16)
    counts = dot(flat_mask.astype(jnp.bfloat16), sums).astype(jnp.int32)
    told_all = lax.all_to_all(
        jnp.broadcast_to(counts.reshape(1, 1, counts.size), (peers, 1, counts.size)),
        PLANE,
        split_axis=0,
        concat_axis=0,
        tiled=True,
    ).reshape(peers, samples, marks + edge)
    told = told_all[:, :, marks - 1]
    before = order[:, None] < order[None, :]
    running = dot(flat_mask.astype(jnp.bfloat16), before.astype(jnp.bfloat16)).astype(jnp.int32)
    cell_rank = jnp.where(flat_mask == 1, running, -1)

    ids = jnp.arange(peers, dtype=jnp.int32)
    earlier = ids[:, None] < ids[None, :]
    starts = jnp.sum(jnp.where(earlier[:, :, None], told[:, None, :], 0), 0)
    my_start = jnp.sum(jnp.where((ids < me)[:, None], told, 0), 0)

    outgoing = dispatch(
        my_start, cell_rank.reshape(samples, 1, tile), patches.reshape(samples, tile, width), peers
    )
    outgoing, piece = lax.optimization_barrier((outgoing, piece))
    pieces = from_dp(piece)
    arrived = lax.all_to_all(outgoing, PLANE, split_axis=0, concat_axis=0, tiled=True)

    slot = jnp.arange(cap, dtype=jnp.int32)[None, None, :]
    local = slot * peers + ((me - starts.T[:, :, None]) & (peers - 1))
    token = (starts.T[:, :, None] + local - me) // peers
    token = jnp.where(local < told.T[:, :, None], token, -1)

    tiles = lax.axis_size("row"), lax.axis_size("col")
    high, wide = tile_h + 2 * REACH, -(-(tile_w + 2 * REACH) // 8) * 8
    rank = (cell_rank + 1).reshape(samples, tile_h, tile_w)
    rank = jnp.pad(rank, ((0, 0), (REACH, REACH), (REACH, wide - tile_w - REACH)))
    back, cell_slot = index(
        me,
        told_all.transpose(1, 0, 2),
        rank.reshape(samples, high * wide, 1),
        ends,
        tiles,
        tile_h,
        tile_w,
        wide,
    )

    x, packed = project(arrived, token.reshape(samples, 1, tile), qkv_weight, kept)
    packed = lax.all_to_all(packed, PLANE, split_axis=0, concat_axis=0, tiled=True)
    mixed = attention(packed, kept)
    mixed, *pieces = lax.optimization_barrier((mixed, *pieces))
    pieces = pieces + [from_partner(one) for one in pieces]
    mixed = lax.all_to_all(mixed, PLANE, split_axis=0, concat_axis=0, tiled=True)
    returning = feed_forward(
        mixed,
        x,
        back,
        out_weight,
        up_weight,
        down_weight,
        dec_proj,
        pieces,
        SLOTS,
    )
    home = lax.all_to_all(returning, PLANE, split_axis=0, concat_axis=0, tiled=True)

    h_zero = place(home, cell_slot, mask_token, dec_proj, high * wide)
    h_zero = h_zero.reshape(samples, high, wide, h_zero.shape[-1])[:, :, : tile_w + 2 * REACH]
    conv_one = convolve(h_zero, conv_weight[0], tile_h + 2, tile_w + 2)
    h_one = h_zero[:, 1:-1, 1:-1].astype(jnp.float32) + gelu(conv_one)
    within = inside(tile_h, tile_w, tile_h + 2, tile_w + 2, 1)
    h_one = jnp.where(within[None, :, :, None], h_one, 0.0).astype(jnp.bfloat16)
    conv_two = convolve(h_one, conv_weight[1], tile_h, tile_w)
    h_two = (h_one[:, 1:-1, 1:-1].astype(jnp.float32) + gelu(conv_two)).astype(jnp.bfloat16)
    return dot(h_two, head_weight).astype(jnp.bfloat16)


def solution(mesh):
    return jax.shard_map(
        shards,
        mesh=mesh,
        in_specs=(
            P("dp", "row", "col", None),
            P("dp", "row", "col"),
            P(),
            P(),
            P(),
            P(None, "dp"),
            P("dp", None),
            P(),
            P(),
            P(),
        ),
        out_specs=P("dp", "row", "col", None),
        check_vma=False,
    )
```

```python
import jax
import jax.numpy as jnp
import numpy as np
from jax import lax
from jax.experimental import pallas as pl
from jax.experimental.pallas import tpu as pltpu
from jax.sharding import PartitionSpec as P


HD = 64
EPS = 1e-06
LOG2E = 1.4426950408889634
ROOT_HALF = 0.7071067811865476
PLANE = ("row", "col")
MIB = 1 << 20
ATTENTION_MIB = 34
SAFE = 96.0


def ring(height, width):
    bands = (slice(0, REACH), slice(REACH, -REACH), slice(-REACH, None))
    order = np.zeros((height, width), np.int32)
    ends = [0]
    for row, col in CORNERS + ((1, 1),):
        block = order[bands[row], bands[col]]
        block[...] = ends[-1] + np.arange(block.size, dtype=np.int32).reshape(block.shape)
        ends.append(ends[-1] + block.size)
    return order, np.array(ends, np.int32)


PIECES = (
    (0, 0, 0, 9, 16),
    (-1, 0, 4, 7, 2),
    (1, 0, 0, 3, 2),
    (0, -1, 2, 5, 1),
    (0, 1, 6, 8, 1),
    (0, 1, 0, 1, 1),
    (-1, -1, 4, 5, 1),
    (-1, 1, 6, 7, 1),
    (1, -1, 2, 3, 1),
    (1, 1, 0, 1, 1),
)
REACH = 2
SLOTS = 32
SIDES = ((-1, 0), (1, 0), (0, -1), (0, 1), (-1, -1), (-1, 1), (1, -1), (1, 1))
CORNERS = ((0, 0), (0, 1), (0, 2), (1, 2), (2, 2), (2, 1), (2, 0), (1, 0))


def normalize(wide):
    mean = jnp.mean(wide, -1, keepdims=True)
    centred = wide - mean
    var = jnp.mean(centred * centred, -1, keepdims=True)
    return (centred * lax.rsqrt(var + EPS)).astype(jnp.bfloat16)


def gelu(value):
    return 0.5 * value * (1.0 + lax.erf(value * ROOT_HALF))


def dot(left, right):
    return jnp.dot(left, right, preferred_element_type=jnp.float32)


def one_hot(left, right):
    return jnp.where(left == right, 1.0, 0.0).astype(jnp.bfloat16)


def convolve(extended, taps, out_h, out_w):
    beside = jnp.concatenate([extended[:, :, second : second + out_w] for second in range(3)], -1)
    taps = taps.reshape(3, beside.shape[-1], taps.shape[-1])
    total = None
    for first in range(3):
        term = jnp.einsum(
            "shwc,cd->shwd",
            beside[:, first : first + out_h],
            taps[first],
            preferred_element_type=jnp.float32,
        )
        total = term if total is None else total + term
    return total


def in_hbm(array):
    return pltpu.with_memory_space_constraint(array, pltpu.HBM)


def params(limit):
    return pltpu.CompilerParams(vmem_limit_bytes=limit * MIB)


def dispatch(my_start, cell_rank, tokens, peers):
    samples, tile, width = tokens.shape
    cap = tile // peers

    def kernel(start_ref, rank_ref, token_ref, out_ref):
        start = start_ref[pl.program_id(0)]
        slot = lax.broadcasted_iota(jnp.int32, (tile, 1), 0)
        rank = (slot % cap) * peers + ((slot // cap - start) & (peers - 1))
        chosen = one_hot(rank, rank_ref[...].reshape(1, tile))
        rows = dot(chosen, token_ref[...].reshape(tile, width)).astype(jnp.bfloat16)
        out_ref[...] = rows.reshape(peers, 1, cap, width)

    return pl.pallas_call(
        kernel,
        grid_spec=pltpu.PrefetchScalarGridSpec(
            num_scalar_prefetch=1,
            grid=(samples,),
            in_specs=[
                pl.BlockSpec((1, 1, tile), lambda s, _: (s, 0, 0)),
                pl.BlockSpec((1, tile, width), lambda s, _: (s, 0, 0)),
            ],
            out_specs=pl.BlockSpec((peers, 1, cap, width), lambda s, _: (0, s, 0, 0)),
        ),
        out_shape=jax.ShapeDtypeStruct((peers, samples, cap, width), jnp.bfloat16),
        compiler_params=params(32),
        name="dispatch",
    )(my_start, cell_rank, tokens)


def project(arrived, token_col, qkv_weight, kept):
    peers, samples, cap, width = arrived.shape
    tile = peers * cap
    lanes = 2 * HD
    groups = width // lanes
    places = peers // samples
    half = kept // 2

    def kernel(col_ref, arrived_ref, weight_hbm, x_hbm, out_ref, weight, x_ref, sems):
        copies = []
        for third in range(3):
            cols = pl.ds(third * width, width)
            copies.append(
                pltpu.make_async_copy(weight_hbm.at[:, cols], weight.at[third], sems.at[third])
            )
            copies[-1].start()
        token = lax.broadcasted_iota(jnp.int32, (kept, 1), 0)
        rows = []
        for sample in range(samples):
            chosen = one_hot(token, col_ref[sample])
            rows.append(dot(chosen, arrived_ref[:, sample].reshape(tile, width)))
            x_ref[sample] = rows[-1].astype(jnp.bfloat16)
        keep = pltpu.make_async_copy(x_ref, x_hbm, sems.at[3])
        keep.start()
        normed = normalize(jnp.concatenate(rows, 0))
        qkv = []
        for third in range(3):
            copies[third].wait()
            qkv.append(dot(normed, weight[third]))
        low = lax.broadcasted_iota(jnp.int32, (kept, lanes), 1) < HD
        low_half = lax.broadcasted_iota(jnp.int32, (half, lanes), 1) < HD
        for sample in range(samples):
            q_all, k_all, v_all = (one[sample * kept : (sample + 1) * kept] for one in qkv)
            for group in range(groups):
                at = group * lanes
                to = sample * places + 2 * group
                q = q_all[:, at : at + lanes] * (0.125 * LOG2E)
                k = k_all[:, at : at + lanes]
                v = v_all[:, at : at + lanes]
                top, bottom = v[:half], v[half:]
                first = jnp.where(low, q, pltpu.roll(k, HD, 1))
                second = jnp.where(low, pltpu.roll(q, HD, 1), k)
                first_v = jnp.where(low_half, top, pltpu.roll(bottom, HD, 1))
                second_v = jnp.where(low_half, pltpu.roll(top, HD, 1), bottom)
                out_ref[to, :kept] = first.astype(jnp.bfloat16)
                out_ref[to, kept:] = first_v.astype(jnp.bfloat16)
                out_ref[to + 1, :kept] = second.astype(jnp.bfloat16)
                out_ref[to + 1, kept:] = second_v.astype(jnp.bfloat16)
            for place in range(2 * groups, places):
                out_ref[sample * places + place] = jnp.zeros((kept + half, lanes), jnp.bfloat16)
        keep.wait()

    return pl.pallas_call(
        kernel,
        in_specs=[pl.BlockSpec(memory_space=pltpu.VMEM)] * 2 + [pl.BlockSpec(memory_space=pltpu.HBM)],
        out_specs=[pl.BlockSpec(memory_space=pltpu.HBM), pl.BlockSpec(memory_space=pltpu.VMEM)],
        out_shape=[
            pltpu.HBM((samples, kept, width), jnp.bfloat16),
            jax.ShapeDtypeStruct((peers, kept + half, lanes), jnp.bfloat16),
        ],
        scratch_shapes=[
            pltpu.VMEM((3, width, width), jnp.bfloat16),
            pltpu.VMEM((samples, kept, width), jnp.bfloat16),
            pltpu.SemaphoreType.DMA((4,)),
        ],
        compiler_params=params(20),
        name="project",
    )(token_col, arrived, in_hbm(qkv_weight))


def attention(packed, kept):
    peers, _, lanes = packed.shape
    half = kept // 2
    keys = peers * half
    step = 8
    contract = (((1,), (1,)), ((), ()))

    def kernel(packed_ref, out_ref, low_key, high_key, value, bound):
        at = pl.program_id(0)

        @pl.when(at == 0)
        def _():
            lane = lax.broadcasted_iota(jnp.int32, (kept, lanes), 1)
            most_q = jnp.zeros((kept, 1), jnp.float32)
            most_k = jnp.zeros((kept, 1), jnp.float32)
            for peer in range(peers):
                rows = pl.ds(peer * half, half)
                wide = packed_ref[peer, :kept].astype(jnp.float32)
                both = pltpu.roll(wide, HD, 1).astype(jnp.bfloat16)
                low_key[rows] = both[:half]
                high_key[rows] = both[half:]
                value[rows, :lanes] = packed_ref[peer, kept:]
                square = wide * wide
                size_q = jnp.sum(jnp.where(lane < HD, square, 0.0), -1, keepdims=True)
                size_k = jnp.sum(jnp.where(lane < HD, 0.0, square), -1, keepdims=True)
                most_q = jnp.maximum(most_q, size_q)
                most_k = jnp.maximum(most_k, size_k)
            value[:, lanes:] = jnp.ones((keys, lanes), jnp.bfloat16)
            bound[0] = jnp.max(most_q) * jnp.max(most_k)

        def finish(low, high, first, count):
            total = low[:, lanes:] + high[:, lanes:]
            mixed = (low[:, :lanes] + pltpu.roll(high[:, :lanes], HD, 1)) / total
            mixed = mixed.reshape(count, 2, half, lanes)
            lane = lax.broadcasted_iota(jnp.int32, (half, lanes), 1)
            for one in range(count):
                both = jnp.where(lane < HD, mixed[one, 0], pltpu.roll(mixed[one, 1], HD, 1))
                out_ref[first + one] = both.astype(jnp.bfloat16)

        def queries(first, count):
            query = packed_ref[pl.ds(at * step + first, count), :kept].reshape(count * kept, lanes)
            lane = lax.broadcasted_iota(jnp.int32, query.shape, 1)
            return jnp.where(lane < HD, query, jnp.zeros_like(query))

        def score(query, key):
            return lax.dot_general(query, key[...], contract, preferred_element_type=jnp.float32)

        narrow = bound[0] < SAFE * SAFE

        @pl.when(narrow)
        def _():
            query = queries(0, step)
            low = jnp.exp2(score(query, low_key)).astype(jnp.bfloat16)
            high = jnp.exp2(score(query, high_key)).astype(jnp.bfloat16)
            finish(dot(low, value[...]), dot(high, value[...]), 0, step)

        @pl.when(jnp.logical_not(narrow))
        def _():
            @pl.loop(0, step)
            def _(one):
                query = queries(one, 1)
                low, high = score(query, low_key), score(query, high_key)
                top = jnp.maximum(jnp.max(low, -1, keepdims=True), jnp.max(high, -1, keepdims=True))
                low = jnp.exp2(low - top).astype(jnp.bfloat16)
                high = jnp.exp2(high - top).astype(jnp.bfloat16)
                finish(dot(low, value[...]), dot(high, value[...]), one, 1)

    return pl.pallas_call(
        kernel,
        grid=(peers // step,),
        in_specs=[pl.BlockSpec(packed.shape, lambda i: (0, 0, 0))],
        out_specs=pl.BlockSpec((step, half, lanes), lambda i: (i, 0, 0)),
        out_shape=jax.ShapeDtypeStruct((peers, half, lanes), jnp.bfloat16),
        scratch_shapes=[
            pltpu.VMEM((keys, lanes), jnp.bfloat16),
            pltpu.VMEM((keys, lanes), jnp.bfloat16),
            pltpu.VMEM((keys, 2 * lanes), jnp.bfloat16),
            pltpu.SMEM((1,), jnp.float32),
        ],
        compiler_params=params(ATTENTION_MIB),
        name="attention",
    )(packed)


def feed_forward(mixed, x, token_col, out_weight, up, down, dec_proj, pieces, slots):
    peers, half, lanes = mixed.shape
    samples, kept, width = x.shape
    places = peers // samples
    narrow = dec_proj.shape[1]

    weights = [in_hbm(one) for one in (out_weight, up, down, *pieces, dec_proj)]
    count = len(weights)

    def kernel(mixed_ref, x_ref, col_ref, *rest):
        sources, out_ref, held, sems = rest[:count], rest[count], rest[count + 1 : -1], rest[-1]
        copies = [
            pltpu.make_async_copy(source, held[at], sems.at[at])
            for at, source in enumerate(sources)
        ]
        ahead = 3
        for copy in copies[:ahead]:
            copy.start()

        def ready(at):
            copies[at].wait()
            if at + ahead < count:
                copies[at + ahead].start()
            return held[at]

        low = lax.broadcasted_iota(jnp.int32, (half, lanes), 1) < HD
        attn = []
        for sample in range(samples):
            parts = []
            for group in range(width // lanes):
                one = mixed_ref[sample * places + 2 * group].astype(jnp.float32)
                two = mixed_ref[sample * places + 2 * group + 1].astype(jnp.float32)
                top = jnp.where(low, one, pltpu.roll(two, HD, 1))
                bottom = jnp.where(low, pltpu.roll(one, HD, 1), two)
                parts.append(jnp.concatenate([top, bottom], 0).astype(jnp.bfloat16))
            attn.append(jnp.concatenate(parts, 1))
        attn = jnp.concatenate(attn, 0)
        rows = x_ref[...].reshape(samples * kept, width)
        x_one = (rows.astype(jnp.float32) + dot(attn, ready(0)[...])).astype(jnp.bfloat16)
        normed = normalize(x_one.astype(jnp.float32))
        inner = gelu(dot(normed, ready(1)[...])).astype(jnp.bfloat16)
        total = dot(inner, ready(2)[...])
        for at in range(3, count - 1):
            piece = ready(at)
            part = piece.shape[1]
            inner = gelu(dot(normed, piece[:width])).astype(jnp.bfloat16)
            added = [dot(inner, piece[pl.ds(at, part)]) for at in range(width, piece.shape[0], part)]
            total = total + jnp.concatenate(added, 1)
        encoded = (x_one.astype(jnp.float32) + total).astype(jnp.bfloat16)
        field = dot(encoded, ready(count - 1)[...]).astype(jnp.bfloat16)
        for sample in range(samples):
            token = lax.broadcasted_iota(jnp.int32, (1, kept), 1)
            chosen = one_hot(col_ref[sample], token)
            sent = dot(chosen, field[sample * kept : (sample + 1) * kept])
            out_ref[:, sample] = sent.astype(jnp.bfloat16).reshape(peers, slots, narrow)

    return pl.pallas_call(
        kernel,
        in_specs=[pl.BlockSpec(memory_space=pltpu.VMEM)] * 3
        + [pl.BlockSpec(memory_space=pltpu.HBM)] * count,
        out_specs=pl.BlockSpec(memory_space=pltpu.VMEM),
        out_shape=jax.ShapeDtypeStruct((peers, samples, slots, narrow), jnp.bfloat16),
        scratch_shapes=[pltpu.VMEM(one.shape, one.dtype) for one in weights]
        + [pltpu.SemaphoreType.DMA((count,))],
        compiler_params=params(32),
        name="feed_forward",
    )(mixed, x, token_col, *weights)


def share(up_weight, down_weight):
    width, hidden = up_weight.shape
    part = hidden // 2
    at = (lax.axis_index("row") % 2) * part
    up = lax.dynamic_slice_in_dim(up_weight, at, part, axis=1)
    down = lax.dynamic_slice_in_dim(down_weight, at, part, axis=0)
    return jnp.concatenate([up] + [down[:, i : i + part] for i in range(0, width, part)], 0)


def from_dp(piece):
    count = lax.axis_size("dp")
    return [
        lax.ppermute(piece, "dp", [(i, (i + hop) % count) for i in range(count)])
        for hop in range(1, count)
    ]


def from_partner(piece):
    return lax.ppermute(piece, "row", [(i, i ^ 1) for i in range(lax.axis_size("row"))])


def place(home, cell_slot, mask_token, dec_proj, cells):
    peers, samples, slots, narrow = home.shape
    width = dec_proj.shape[0]

    def kernel(slot_ref, home_ref, token_ref, dec_ref, out_ref):
        slot = slot_ref[0]
        chosen = one_hot(slot, lax.broadcasted_iota(jnp.int32, (1, peers * slots), 1))
        rows = dot(chosen, home_ref[...].reshape(peers * slots, narrow))
        blank = dot(jnp.broadcast_to(token_ref[...], (8, width)), dec_ref[...])[:1]
        out_ref[0] = jnp.where(slot == -1, blank, rows).astype(jnp.bfloat16)

    return pl.pallas_call(
        kernel,
        grid=(samples,),
        in_specs=[
            pl.BlockSpec((1, cells, 1), lambda s: (s, 0, 0)),
            pl.BlockSpec((peers, 1, slots, narrow), lambda s: (0, s, 0, 0)),
            pl.BlockSpec((1, width), lambda s: (0, 0)),
            pl.BlockSpec((width, narrow), lambda s: (0, 0)),
        ],
        out_specs=pl.BlockSpec((1, cells, narrow), lambda s: (s, 0, 0)),
        out_shape=jax.ShapeDtypeStruct((samples, cells, narrow), jnp.bfloat16),
        compiler_params=params(16),
        name="place",
    )(cell_slot, home, mask_token.reshape(1, width), dec_proj)


def pick(which, table):
    lane = lax.broadcasted_iota(jnp.int32, (1, table.shape[1]), 1)
    found = jnp.sum(jnp.where(which == lane, table, 0.0), -1, keepdims=True)
    return found.astype(jnp.int32)


def index(me, told, rank, cuts, tiles, tile_h, tile_w, wide):
    samples, peers, width = told.shape
    marks = len(cuts)
    edge = width - marks
    tiles_h, tiles_w = tiles
    cells = rank.shape[1]
    bases = [sum(piece[4] for piece in PIECES[:number]) for number in range(len(PIECES))]

    def kernel(me_ref, told_ref, rank_ref, back_ref, slot_ref):
        me = me_ref[0]
        ahead = told_ref[0][:, :marks].astype(jnp.float32)
        bits = told_ref[0][:, marks:].astype(jnp.float32)
        tile = lax.broadcasted_iota(jnp.int32, (peers, 1), 0)
        other = lax.broadcasted_iota(jnp.int32, (1, peers), 1)
        earlier = jnp.where(other < tile, 1.0, 0.0)
        totals = jnp.broadcast_to(ahead[:, marks - 1 :], (peers, 128))
        starts = jnp.dot(
            earlier, totals, precision=lax.Precision.HIGHEST, preferred_element_type=jnp.float32
        )
        lane = lax.broadcasted_iota(jnp.int32, (1, 128), 1)
        begins = jnp.zeros((peers, 128), jnp.float32)
        ends = jnp.zeros((peers, 128), jnp.float32)
        for number, (down, right, first, last, _) in enumerate(PIECES):
            row, col = tile // tiles_w + down, tile % tiles_w + right
            there = (row >= 0) & (row < tiles_h) & (col >= 0) & (col < tiles_w) & (lane == number)
            for side, mark in enumerate((first, last)):
                value = ahead[:, mark : mark + 1] + starts
                hop = (-(down * tiles_w + right)) % peers
                if hop:
                    value = pltpu.roll(value, hop, 0)
                if side:
                    ends = jnp.where(there, value, ends)
                else:
                    begins = jnp.where(there, value, begins)

        at = lax.broadcasted_iota(jnp.int32, (peers * SLOTS, 1), 0)
        expand = jnp.where(at // SLOTS == other, 1.0, 0.0)
        at = at % SLOTS
        which = jnp.full(at.shape, len(PIECES), jnp.int32)
        nth = jnp.zeros(at.shape, jnp.int32)
        for number, base in enumerate(bases):
            here = (at >= base) & (at < base + PIECES[number][4])
            which = jnp.where(here, number, which)
            nth = jnp.where(here, at - base, nth)

        def spread(table):
            rows = jnp.dot(
                expand, table, precision=lax.Precision.HIGHEST, preferred_element_type=jnp.float32
            )
            return pick(which, rows)

        position = (spread(begins) - me + peers - 1) // peers + nth
        back_ref[0] = jnp.where(position * peers + me < spread(ends), position, -1)

        cell = lax.broadcasted_iota(jnp.int32, (cells, 1), 0)
        row, col = cell // wide, cell % wide
        side = [(col < REACH), (col >= REACH + tile_w)]
        which = jnp.where(row < REACH, 1, jnp.where(row >= REACH + tile_h, 2, 0))
        right = jnp.where(row < 2 * REACH, 5, 4)
        left = jnp.where(which == 0, 3, jnp.where(which == 1, 6, 8))
        right = jnp.where(which == 0, right, jnp.where(which == 1, 7, 9))
        which = jnp.where(side[0], left, jnp.where(side[1], right, which))
        base = jnp.zeros(cell.shape, jnp.int32)
        for number in range(1, len(bases)):
            base = jnp.where(which == number, bases[number], base)
        mine = jnp.sum(jnp.where(tile == me, begins, 0.0), 0, keepdims=True)

        one = lax.broadcasted_iota(jnp.int32, (edge, 1), 0)
        two = lax.broadcasted_iota(jnp.int32, (1, edge), 1)
        ranks = dot(bits.astype(jnp.bfloat16), jnp.where(one < two, 1.0, 0.0).astype(jnp.bfloat16))
        ranks = jnp.where(bits > 0.5, ranks + starts[:, :1] + 1.0, 0.0)
        number = lax.broadcasted_iota(jnp.int32, (128, 1), 0)
        there = jnp.full((128, 1), -1, jnp.int32)
        for at, (down, right) in enumerate(SIDES):
            there = jnp.where(number == at, me + down * tiles_w + right, there)
        chosen = jnp.where(there == other, 1.0, 0.0)
        table = jnp.dot(
            chosen, ranks, precision=lax.Precision.HIGHEST, preferred_element_type=jnp.float32
        )
        i, j = (row - REACH) % tile_h, (col - REACH) % tile_w
        down = jnp.where(row < REACH, -1, jnp.where(row >= REACH + tile_h, 1, 0))
        right = jnp.where(side[0], -1, jnp.where(side[1], 1, 0))
        place = jnp.zeros(cell.shape, jnp.int32)
        for at, (top, left) in enumerate(CORNERS):
            rows = ((i < REACH), (i >= REACH) & (i < tile_h - REACH), (i >= tile_h - REACH))[top]
            cols = ((j < REACH), (j >= REACH) & (j < tile_w - REACH), (j >= tile_w - REACH))[left]
            first_i = (0, REACH, tile_h - REACH)[top]
            first_j = (0, REACH, tile_w - REACH)[left]
            span = tile_w - 2 * REACH if left == 1 else REACH
            found = int(cuts[at]) + (i - first_i) * span + (j - first_j)
            place = jnp.where(rows & cols, found, place)
        spot = jnp.where(place == two, 1.0, 0.0)
        border = lax.dot_general(
            spot,
            table,
            (((1,), (1,)), ((), ())),
            precision=lax.Precision.HIGHEST,
            preferred_element_type=jnp.float32,
        )
        which_side = jnp.full(cell.shape, -1, jnp.int32)
        for at, (one_down, one_right) in enumerate(SIDES):
            which_side = jnp.where((down == one_down) & (right == one_right), at, which_side)
        own = jnp.sum(jnp.where(tile == me, starts[:, :1], 0.0), 0, keepdims=True).astype(jnp.int32)
        rank = jnp.where(rank_ref[0] > 0, rank_ref[0] + own, 0)
        rank = jnp.where(which_side >= 0, pick(which_side, border), rank) - 1
        peer = rank & (peers - 1)
        nth = rank // peers - (pick(which, mine) - peer + peers - 1) // peers
        row = row + (me // tiles_w) * tile_h - REACH
        col = col + (me % tiles_w) * tile_w - REACH
        within = (row >= 0) & (row < tiles_h * tile_h) & (col >= 0) & (col < tiles_w * tile_w)
        slot = jnp.where(rank >= 0, peer * SLOTS + base + nth, -1)
        slot_ref[0] = jnp.where(within, slot, -2)

    return pl.pallas_call(
        kernel,
        grid_spec=pltpu.PrefetchScalarGridSpec(
            num_scalar_prefetch=1,
            grid=(samples,),
            in_specs=[
                pl.BlockSpec((1, peers, width), lambda s, _: (s, 0, 0)),
                pl.BlockSpec((1, cells, 1), lambda s, _: (s, 0, 0)),
            ],
            out_specs=[
                pl.BlockSpec((1, peers * SLOTS, 1), lambda s, _: (s, 0, 0)),
                pl.BlockSpec((1, cells, 1), lambda s, _: (s, 0, 0)),
            ],
        ),
        out_shape=[
            jax.ShapeDtypeStruct((samples, peers * SLOTS, 1), jnp.int32),
            jax.ShapeDtypeStruct((samples, cells, 1), jnp.int32),
        ],
        compiler_params=params(16),
        name="index",
    )(me.reshape(1), told, rank)


def inside(height, width, out_h, out_w, reach):
    row = lax.axis_index("row") * height - reach + jnp.arange(out_h, dtype=jnp.int32)
    col = lax.axis_index("col") * width - reach + jnp.arange(out_w, dtype=jnp.int32)
    row_in = (row >= 0) & (row < lax.axis_size("row") * height)
    col_in = (col >= 0) & (col < lax.axis_size("col") * width)
    return row_in[:, None] & col_in[None, :]


def shards(
    patches,
    keep_mask,
    mask_token,
    qkv_weight,
    out_weight,
    up_weight,
    down_weight,
    dec_proj,
    conv_weight,
    head_weight,
):
    peers = lax.axis_size(PLANE)
    me = lax.axis_index(PLANE)
    samples, tile_h, tile_w, width = patches.shape
    tile = tile_h * tile_w
    cap = tile // peers
    kept = tile // 4
    piece = share(up_weight, down_weight)

    flat_mask = keep_mask.reshape(samples, tile)
    order, ends = ring(tile_h, tile_w)
    order = jnp.asarray(order.reshape(-1))
    marks, edge = len(ends), int(ends[-2])
    spots = np.arange(edge, dtype=np.int32)
    low = jnp.asarray(np.concatenate([np.zeros_like(ends), spots]))
    high = jnp.asarray(np.concatenate([ends, spots + 1]))
    sums = (order[:, None] >= low[None, :]) & (order[:, None] < high[None, :])
    sums = sums.astype(jnp.bfloat16)
    counts = dot(flat_mask.astype(jnp.bfloat16), sums).astype(jnp.int32)
    told_all = lax.all_to_all(
        jnp.broadcast_to(counts.reshape(1, 1, counts.size), (peers, 1, counts.size)),
        PLANE,
        split_axis=0,
        concat_axis=0,
        tiled=True,
    ).reshape(peers, samples, marks + edge)
    told = told_all[:, :, marks - 1]
    before = order[:, None] < order[None, :]
    running = dot(flat_mask.astype(jnp.bfloat16), before.astype(jnp.bfloat16)).astype(jnp.int32)
    cell_rank = jnp.where(flat_mask == 1, running, -1)

    ids = jnp.arange(peers, dtype=jnp.int32)
    earlier = ids[:, None] < ids[None, :]
    starts = jnp.sum(jnp.where(earlier[:, :, None], told[:, None, :], 0), 0)
    my_start = jnp.sum(jnp.where((ids < me)[:, None], told, 0), 0)

    outgoing = dispatch(
        my_start, cell_rank.reshape(samples, 1, tile), patches.reshape(samples, tile, width), peers
    )
    outgoing, piece = lax.optimization_barrier((outgoing, piece))
    pieces = from_dp(piece)
    arrived = lax.all_to_all(outgoing, PLANE, split_axis=0, concat_axis=0, tiled=True)

    slot = jnp.arange(cap, dtype=jnp.int32)[None, None, :]
    local = slot * peers + ((me - starts.T[:, :, None]) & (peers - 1))
    token = (starts.T[:, :, None] + local - me) // peers
    token = jnp.where(local < told.T[:, :, None], token, -1)

    tiles = lax.axis_size("row"), lax.axis_size("col")
    high, wide = tile_h + 2 * REACH, -(-(tile_w + 2 * REACH) // 8) * 8
    rank = (cell_rank + 1).reshape(samples, tile_h, tile_w)
    rank = jnp.pad(rank, ((0, 0), (REACH, REACH), (REACH, wide - tile_w - REACH)))
    back, cell_slot = index(
        me,
        told_all.transpose(1, 0, 2),
        rank.reshape(samples, high * wide, 1),
        ends,
        tiles,
        tile_h,
        tile_w,
        wide,
    )

    x, packed = project(arrived, token.reshape(samples, 1, tile), qkv_weight, kept)
    packed = lax.all_to_all(packed, PLANE, split_axis=0, concat_axis=0, tiled=True)
    mixed = attention(packed, kept)
    mixed, *pieces = lax.optimization_barrier((mixed, *pieces))
    pieces = pieces + [from_partner(one) for one in pieces]
    mixed = lax.all_to_all(mixed, PLANE, split_axis=0, concat_axis=0, tiled=True)
    returning = feed_forward(
        mixed,
        x,
        back,
        out_weight,
        up_weight,
        down_weight,
        dec_proj,
        pieces,
        SLOTS,
    )
    home = lax.all_to_all(returning, PLANE, split_axis=0, concat_axis=0, tiled=True)

    h_zero = place(home, cell_slot, mask_token, dec_proj, high * wide)
    h_zero = h_zero.reshape(samples, high, wide, h_zero.shape[-1])[:, :, : tile_w + 2 * REACH]
    conv_one = convolve(h_zero, conv_weight[0], tile_h + 2, tile_w + 2)
    h_one = h_zero[:, 1:-1, 1:-1].astype(jnp.float32) + gelu(conv_one)
    within = inside(tile_h, tile_w, tile_h + 2, tile_w + 2, 1)
    h_one = jnp.where(within[None, :, :, None], h_one, 0.0).astype(jnp.bfloat16)
    conv_two = convolve(h_one, conv_weight[1], tile_h, tile_w)
    h_two = (h_one[:, 1:-1, 1:-1].astype(jnp.float32) + gelu(conv_two)).astype(jnp.bfloat16)
    return dot(h_two, head_weight).astype(jnp.bfloat16)


def solution(mesh):
    return jax.shard_map(
        shards,
        mesh=mesh,
        in_specs=(
            P("dp", "row", "col", None),
            P("dp", "row", "col"),
            P(),
            P(),
            P(),
            P(None, "dp"),
            P("dp", None),
            P(),
            P(),
            P(),
        ),
        out_specs=P("dp", "row", "col", None),
        check_vma=False,
    )
```

```python
import jax
import jax.numpy as jnp
import numpy as np
from jax import lax
from jax.experimental import pallas as pl
from jax.experimental.pallas import tpu as pltpu
from jax.sharding import PartitionSpec as P


HD = 64
EPS = 1e-06
LOG2E = 1.4426950408889634
ROOT_HALF = 0.7071067811865476
PLANE = ("row", "col")
MIB = 1 << 20
ATTENTION_MIB = 34
SAFE = 96.0
EXTRA = 16


def ring(height, width):
    bands = (slice(0, REACH), slice(REACH, -REACH), slice(-REACH, None))
    order = np.zeros((height, width), np.int32)
    ends = [0]
    for row, col in CORNERS + ((1, 1),):
        block = order[bands[row], bands[col]]
        block[...] = ends[-1] + np.arange(block.size, dtype=np.int32).reshape(block.shape)
        ends.append(ends[-1] + block.size)
    return order, np.array(ends, np.int32)


PIECES = (
    (0, 0, 0, 9, 16),
    (-1, 0, 4, 7, 2),
    (1, 0, 0, 3, 2),
    (0, -1, 2, 5, 1),
    (0, 1, 6, 8, 1),
    (0, 1, 0, 1, 1),
    (-1, -1, 4, 5, 1),
    (-1, 1, 6, 7, 1),
    (1, -1, 2, 3, 1),
    (1, 1, 0, 1, 1),
)
REACH = 2
SLOTS = 32
SIDES = ((-1, 0), (1, 0), (0, -1), (0, 1), (-1, -1), (-1, 1), (1, -1), (1, 1))
CORNERS = ((0, 0), (0, 1), (0, 2), (1, 2), (2, 2), (2, 1), (2, 0), (1, 0))


def normalize(wide):
    mean = jnp.mean(wide, -1, keepdims=True)
    centred = wide - mean
    var = jnp.mean(centred * centred, -1, keepdims=True)
    return (centred * lax.rsqrt(var + EPS)).astype(jnp.bfloat16)


def gelu(value):
    return 0.5 * value * (1.0 + lax.erf(value * ROOT_HALF))


def dot(left, right):
    return jnp.dot(left, right, preferred_element_type=jnp.float32)


def one_hot(left, right):
    return jnp.where(left == right, 1.0, 0.0).astype(jnp.bfloat16)


def convolve(extended, taps, out_h, out_w):
    total = None
    for first in range(3):
        for second in range(3):
            term = jnp.einsum(
                "shwc,cd->shwd",
                extended[:, first : first + out_h, second : second + out_w],
                taps[first * 3 + second],
                preferred_element_type=jnp.float32,
            )
            total = term if total is None else total + term
    return total


def in_hbm(array):
    return pltpu.with_memory_space_constraint(array, pltpu.HBM)


def params(limit):
    return pltpu.CompilerParams(vmem_limit_bytes=limit * MIB)


def dispatch(my_start, cell_rank, tokens, peers):
    samples, tile, width = tokens.shape
    cap = tile // peers

    def kernel(start_ref, rank_ref, token_ref, out_ref):
        start = start_ref[pl.program_id(0)]
        slot = lax.broadcasted_iota(jnp.int32, (tile, 1), 0)
        rank = (slot % cap) * peers + ((slot // cap - start) & (peers - 1))
        chosen = one_hot(rank, rank_ref[...].reshape(1, tile))
        rows = dot(chosen, token_ref[...].reshape(tile, width)).astype(jnp.bfloat16)
        out_ref[...] = rows.reshape(peers, 1, cap, width)

    return pl.pallas_call(
        kernel,
        grid_spec=pltpu.PrefetchScalarGridSpec(
            num_scalar_prefetch=1,
            grid=(samples,),
            in_specs=[
                pl.BlockSpec((1, 1, tile), lambda s, _: (s, 0, 0)),
                pl.BlockSpec((1, tile, width), lambda s, _: (s, 0, 0)),
            ],
            out_specs=pl.BlockSpec((peers, 1, cap, width), lambda s, _: (0, s, 0, 0)),
        ),
        out_shape=jax.ShapeDtypeStruct((peers, samples, cap, width), jnp.bfloat16),
        compiler_params=params(32),
        name="dispatch",
    )(my_start, cell_rank, in_hbm(tokens))


def project(arrived, token_col, qkv_weight, kept):
    peers, samples, cap, width = arrived.shape
    tile = peers * cap
    lanes = 2 * HD
    groups = width // lanes
    places = peers // samples
    half = kept // 2

    def kernel(col_ref, arrived_ref, weight_hbm, x_hbm, out_ref, weight, x_ref, sems):
        copies = []
        for third in range(3):
            cols = pl.ds(third * width, width)
            copies.append(
                pltpu.make_async_copy(weight_hbm.at[:, cols], weight.at[third], sems.at[third])
            )
            copies[-1].start()
        token = lax.broadcasted_iota(jnp.int32, (kept, 1), 0)
        rows = []
        for sample in range(samples):
            chosen = one_hot(token, col_ref[sample])
            rows.append(dot(chosen, arrived_ref[:, sample].reshape(tile, width)))
            x_ref[sample] = rows[-1].astype(jnp.bfloat16)
        keep = pltpu.make_async_copy(x_ref, x_hbm, sems.at[3])
        keep.start()
        normed = normalize(jnp.concatenate(rows, 0))
        qkv = []
        for third in range(3):
            copies[third].wait()
            qkv.append(dot(normed, weight[third]))
        low = lax.broadcasted_iota(jnp.int32, (kept, lanes), 1) < HD
        low_half = lax.broadcasted_iota(jnp.int32, (half, lanes), 1) < HD
        for sample in range(samples):
            q_all, k_all, v_all = (one[sample * kept : (sample + 1) * kept] for one in qkv)
            for group in range(groups):
                at = group * lanes
                to = sample * places + 2 * group
                q = q_all[:, at : at + lanes] * (0.125 * LOG2E)
                k = k_all[:, at : at + lanes]
                v = v_all[:, at : at + lanes]
                top, bottom = v[:half], v[half:]
                first = jnp.where(low, q, pltpu.roll(k, HD, 1))
                second = jnp.where(low, pltpu.roll(q, HD, 1), k)
                first_v = jnp.where(low_half, top, pltpu.roll(bottom, HD, 1))
                second_v = jnp.where(low_half, pltpu.roll(top, HD, 1), bottom)
                out_ref[to, :kept] = first.astype(jnp.bfloat16)
                out_ref[to, kept:] = first_v.astype(jnp.bfloat16)
                out_ref[to + 1, :kept] = second.astype(jnp.bfloat16)
                out_ref[to + 1, kept:] = second_v.astype(jnp.bfloat16)
            for place in range(2 * groups, places):
                out_ref[sample * places + place] = jnp.zeros((kept + half, lanes), jnp.bfloat16)
        keep.wait()

    return pl.pallas_call(
        kernel,
        in_specs=[pl.BlockSpec(memory_space=pltpu.VMEM)] * 2 + [pl.BlockSpec(memory_space=pltpu.HBM)],
        out_specs=[pl.BlockSpec(memory_space=pltpu.HBM), pl.BlockSpec(memory_space=pltpu.VMEM)],
        out_shape=[
            pltpu.HBM((samples, kept, width), jnp.bfloat16),
            jax.ShapeDtypeStruct((peers, kept + half, lanes), jnp.bfloat16),
        ],
        scratch_shapes=[
            pltpu.VMEM((3, width, width), jnp.bfloat16),
            pltpu.VMEM((samples, kept, width), jnp.bfloat16),
            pltpu.SemaphoreType.DMA((4,)),
        ],
        compiler_params=params(20),
        name="project",
    )(token_col, arrived, in_hbm(qkv_weight))


def attention(packed, kept):
    peers, _, lanes = packed.shape
    half = kept // 2
    keys = peers * half
    step = 8
    contract = (((1,), (1,)), ((), ()))

    def kernel(packed_ref, out_ref, low_key, high_key, low_value, high_value, bound):
        at = pl.program_id(0)

        @pl.when(at == 0)
        def _():
            lane = lax.broadcasted_iota(jnp.int32, (kept, lanes), 1)
            most_q = jnp.zeros((kept, 1), jnp.float32)
            most_k = jnp.zeros((kept, 1), jnp.float32)
            for peer in range(peers):
                rows = pl.ds(peer * half, half)
                wide = packed_ref[peer, :kept].astype(jnp.float32)
                both = pltpu.roll(wide, HD, 1).astype(jnp.bfloat16)
                low_key[rows] = both[:half]
                high_key[rows] = both[half:]
                square = wide * wide
                size_q = jnp.sum(jnp.where(lane < HD, square, 0.0), -1, keepdims=True)
                size_k = jnp.sum(jnp.where(lane < HD, 0.0, square), -1, keepdims=True)
                most_q = jnp.maximum(most_q, size_q)
                most_k = jnp.maximum(most_k, size_k)
            for pair in range(peers // 2):
                cols = pl.ds(pair * 2 * half, 2 * half)
                turned = packed_ref[2 * pair : 2 * pair + 2, kept:].reshape(2 * half, lanes)
                turned = turned.astype(jnp.float32).T.astype(jnp.bfloat16)
                low_value[:HD, cols] = turned[:HD]
                high_value[:HD, cols] = turned[HD:]
            low_value[HD:] = jnp.ones((EXTRA, keys), jnp.bfloat16)
            high_value[HD:] = jnp.ones((EXTRA, keys), jnp.bfloat16)
            bound[0] = jnp.max(most_q) * jnp.max(most_k)

        def finish(low, high, first, count):
            mixed = dot(low_value[...], low) + dot(high_value[...], high)
            mixed = mixed[:HD] / mixed[HD : HD + 1]
            for one in range(count):
                here = mixed[:, one * kept : (one + 1) * kept]
                both = jnp.concatenate([here, pltpu.roll(here, half, 1)], 0).T
                out_ref[first + one] = both[:half].astype(jnp.bfloat16)

        def queries(first, count):
            query = packed_ref[pl.ds(at * step + first, count), :kept].reshape(count * kept, lanes)
            lane = lax.broadcasted_iota(jnp.int32, query.shape, 1)
            return jnp.where(lane < HD, query, jnp.zeros_like(query))

        def score(query, key):
            return lax.dot_general(key[...], query, contract, preferred_element_type=jnp.float32)

        narrow = bound[0] < SAFE * SAFE

        @pl.when(narrow)
        def _():
            query = queries(0, step)
            low = jnp.exp2(score(query, low_key)).astype(jnp.bfloat16)
            high = jnp.exp2(score(query, high_key)).astype(jnp.bfloat16)
            finish(low, high, 0, step)

        @pl.when(jnp.logical_not(narrow))
        def _():
            @pl.loop(0, step)
            def _(one):
                query = queries(one, 1)
                low, high = score(query, low_key), score(query, high_key)
                top = jnp.maximum(jnp.max(low, 0, keepdims=True), jnp.max(high, 0, keepdims=True))
                low = jnp.exp2(low - top).astype(jnp.bfloat16)
                high = jnp.exp2(high - top).astype(jnp.bfloat16)
                finish(low, high, one, 1)

    return pl.pallas_call(
        kernel,
        grid=(peers // step,),
        in_specs=[pl.BlockSpec(packed.shape, lambda i: (0, 0, 0))],
        out_specs=pl.BlockSpec((step, half, lanes), lambda i: (i, 0, 0)),
        out_shape=jax.ShapeDtypeStruct((peers, half, lanes), jnp.bfloat16),
        scratch_shapes=[
            pltpu.VMEM((keys, lanes), jnp.bfloat16),
            pltpu.VMEM((keys, lanes), jnp.bfloat16),
            pltpu.VMEM((HD + EXTRA, keys), jnp.bfloat16),
            pltpu.VMEM((HD + EXTRA, keys), jnp.bfloat16),
            pltpu.SMEM((1,), jnp.float32),
        ],
        compiler_params=params(ATTENTION_MIB),
        name="attention",
    )(packed)


def feed_forward(mixed, x, token_col, out_weight, up, down, dec_proj, pieces, slots):
    peers, half, lanes = mixed.shape
    samples, kept, width = x.shape
    places = peers // samples
    narrow = dec_proj.shape[1]

    weights = [in_hbm(one) for one in (out_weight, up, down, *pieces, dec_proj)]
    count = len(weights)

    def kernel(mixed_ref, x_ref, col_ref, *rest):
        sources, out_ref, held, sems = rest[:count], rest[count], rest[count + 1 : -1], rest[-1]
        copies = [
            pltpu.make_async_copy(source, held[at], sems.at[at])
            for at, source in enumerate(sources)
        ]
        ahead = 3
        for copy in copies[:ahead]:
            copy.start()

        def ready(at):
            copies[at].wait()
            if at + ahead < count:
                copies[at + ahead].start()
            return held[at]

        low = lax.broadcasted_iota(jnp.int32, (half, lanes), 1) < HD
        attn = []
        for sample in range(samples):
            parts = []
            for group in range(width // lanes):
                one = mixed_ref[sample * places + 2 * group].astype(jnp.float32)
                two = mixed_ref[sample * places + 2 * group + 1].astype(jnp.float32)
                top = jnp.where(low, one, pltpu.roll(two, HD, 1))
                bottom = jnp.where(low, pltpu.roll(one, HD, 1), two)
                parts.append(jnp.concatenate([top, bottom], 0).astype(jnp.bfloat16))
            attn.append(jnp.concatenate(parts, 1))
        attn = jnp.concatenate(attn, 0)
        rows = x_ref[...].reshape(samples * kept, width)
        x_one = (rows.astype(jnp.float32) + dot(attn, ready(0)[...])).astype(jnp.bfloat16)
        normed = normalize(x_one.astype(jnp.float32))
        raised = dot(normed, ready(1)[...])
        total = jnp.zeros((samples * kept, width), jnp.float32)
        lower = ready(2)
        for at in range(3, count):
            piece = ready(at)
            later = dot(normed, piece[:width]) if at < count - 1 else None
            inner = gelu(raised).astype(jnp.bfloat16)
            if at == 3:
                total = total + dot(inner, lower[...])
            else:
                part = lower.shape[1]
                ends = range(width, lower.shape[0], part)
                added = [dot(inner, lower[pl.ds(end, part)]) for end in ends]
                total = total + jnp.concatenate(added, 1)
            raised, lower = later, piece
        encoded = (x_one.astype(jnp.float32) + total).astype(jnp.bfloat16)
        field = dot(encoded, held[count - 1][...]).astype(jnp.bfloat16)
        for sample in range(samples):
            token = lax.broadcasted_iota(jnp.int32, (1, kept), 1)
            chosen = one_hot(col_ref[sample], token)
            sent = dot(chosen, field[sample * kept : (sample + 1) * kept])
            out_ref[:, sample] = sent.astype(jnp.bfloat16).reshape(peers, slots, narrow)

    return pl.pallas_call(
        kernel,
        in_specs=[pl.BlockSpec(memory_space=pltpu.VMEM)] * 3
        + [pl.BlockSpec(memory_space=pltpu.HBM)] * count,
        out_specs=pl.BlockSpec(memory_space=pltpu.VMEM),
        out_shape=jax.ShapeDtypeStruct((peers, samples, slots, narrow), jnp.bfloat16),
        scratch_shapes=[pltpu.VMEM(one.shape, one.dtype) for one in weights]
        + [pltpu.SemaphoreType.DMA((count,))],
        compiler_params=params(32),
        name="feed_forward",
    )(mixed, x, token_col, *weights)


def share(up_weight, down_weight):
    width, hidden = up_weight.shape
    part = hidden // 2
    at = (lax.axis_index("row") % 2) * part
    up = lax.dynamic_slice_in_dim(up_weight, at, part, axis=1)
    down = lax.dynamic_slice_in_dim(down_weight, at, part, axis=0)
    return jnp.concatenate([up] + [down[:, i : i + part] for i in range(0, width, part)], 0)


def from_dp(piece):
    count = lax.axis_size("dp")
    return [
        lax.ppermute(piece, "dp", [(i, (i + hop) % count) for i in range(count)])
        for hop in range(1, count)
    ]


def from_partner(piece):
    return lax.ppermute(piece, "row", [(i, i ^ 1) for i in range(lax.axis_size("row"))])


def place(home, cell_slot, mask_token, dec_proj, cells):
    peers, samples, slots, narrow = home.shape
    width = dec_proj.shape[0]

    def kernel(slot_ref, home_ref, token_ref, dec_ref, out_ref):
        slot = slot_ref[0]
        chosen = one_hot(slot, lax.broadcasted_iota(jnp.int32, (1, peers * slots), 1))
        rows = dot(chosen, home_ref[...].reshape(peers * slots, narrow))
        blank = dot(jnp.broadcast_to(token_ref[...], (8, width)), dec_ref[...])[:1]
        out_ref[0] = jnp.where(slot == -1, blank, rows).astype(jnp.bfloat16)

    return pl.pallas_call(
        kernel,
        grid=(samples,),
        in_specs=[
            pl.BlockSpec((1, cells, 1), lambda s: (s, 0, 0)),
            pl.BlockSpec((peers, 1, slots, narrow), lambda s: (0, s, 0, 0)),
            pl.BlockSpec((1, width), lambda s: (0, 0)),
            pl.BlockSpec((width, narrow), lambda s: (0, 0)),
        ],
        out_specs=pl.BlockSpec((1, cells, narrow), lambda s: (s, 0, 0)),
        out_shape=jax.ShapeDtypeStruct((samples, cells, narrow), jnp.bfloat16),
        compiler_params=params(16),
        name="place",
    )(cell_slot, home, mask_token.reshape(1, width), dec_proj)


def pick(which, table):
    lane = lax.broadcasted_iota(jnp.int32, (1, table.shape[1]), 1)
    found = jnp.sum(jnp.where(which == lane, table, 0.0), -1, keepdims=True)
    return found.astype(jnp.int32)


def index(me, told, rank, cuts, tiles, tile_h, tile_w, wide):
    samples, peers, width = told.shape
    marks = len(cuts)
    edge = width - marks
    tiles_h, tiles_w = tiles
    cells = rank.shape[1]
    bases = [sum(piece[4] for piece in PIECES[:number]) for number in range(len(PIECES))]

    def kernel(me_ref, told_ref, rank_ref, back_ref, slot_ref):
        me = me_ref[0]
        ahead = told_ref[0][:, :marks].astype(jnp.float32)
        bits = told_ref[0][:, marks:].astype(jnp.float32)
        tile = lax.broadcasted_iota(jnp.int32, (peers, 1), 0)
        other = lax.broadcasted_iota(jnp.int32, (1, peers), 1)
        earlier = jnp.where(other < tile, 1.0, 0.0)
        totals = jnp.broadcast_to(ahead[:, marks - 1 :], (peers, 128))
        starts = jnp.dot(
            earlier, totals, precision=lax.Precision.HIGHEST, preferred_element_type=jnp.float32
        )
        lane = lax.broadcasted_iota(jnp.int32, (1, 128), 1)
        begins = jnp.zeros((peers, 128), jnp.float32)
        ends = jnp.zeros((peers, 128), jnp.float32)
        for number, (down, right, first, last, _) in enumerate(PIECES):
            row, col = tile // tiles_w + down, tile % tiles_w + right
            there = (row >= 0) & (row < tiles_h) & (col >= 0) & (col < tiles_w) & (lane == number)
            for side, mark in enumerate((first, last)):
                value = ahead[:, mark : mark + 1] + starts
                hop = (-(down * tiles_w + right)) % peers
                if hop:
                    value = pltpu.roll(value, hop, 0)
                if side:
                    ends = jnp.where(there, value, ends)
                else:
                    begins = jnp.where(there, value, begins)

        at = lax.broadcasted_iota(jnp.int32, (peers * SLOTS, 1), 0)
        expand = jnp.where(at // SLOTS == other, 1.0, 0.0)
        at = at % SLOTS
        which = jnp.full(at.shape, len(PIECES), jnp.int32)
        nth = jnp.zeros(at.shape, jnp.int32)
        for number, base in enumerate(bases):
            here = (at >= base) & (at < base + PIECES[number][4])
            which = jnp.where(here, number, which)
            nth = jnp.where(here, at - base, nth)

        def spread(table):
            rows = jnp.dot(
                expand, table, precision=lax.Precision.HIGHEST, preferred_element_type=jnp.float32
            )
            return pick(which, rows)

        position = (spread(begins) - me + peers - 1) // peers + nth
        back_ref[0] = jnp.where(position * peers + me < spread(ends), position, -1)

        cell = lax.broadcasted_iota(jnp.int32, (cells, 1), 0)
        row, col = cell // wide, cell % wide
        side = [(col < REACH), (col >= REACH + tile_w)]
        which = jnp.where(row < REACH, 1, jnp.where(row >= REACH + tile_h, 2, 0))
        right = jnp.where(row < 2 * REACH, 5, 4)
        left = jnp.where(which == 0, 3, jnp.where(which == 1, 6, 8))
        right = jnp.where(which == 0, right, jnp.where(which == 1, 7, 9))
        which = jnp.where(side[0], left, jnp.where(side[1], right, which))
        base = jnp.zeros(cell.shape, jnp.int32)
        for number in range(1, len(bases)):
            base = jnp.where(which == number, bases[number], base)
        mine = jnp.sum(jnp.where(tile == me, begins, 0.0), 0, keepdims=True)

        one = lax.broadcasted_iota(jnp.int32, (edge, 1), 0)
        two = lax.broadcasted_iota(jnp.int32, (1, edge), 1)
        ranks = dot(bits.astype(jnp.bfloat16), jnp.where(one < two, 1.0, 0.0).astype(jnp.bfloat16))
        ranks = jnp.where(bits > 0.5, ranks + starts[:, :1] + 1.0, 0.0)
        number = lax.broadcasted_iota(jnp.int32, (128, 1), 0)
        there = jnp.full((128, 1), -1, jnp.int32)
        for at, (down, right) in enumerate(SIDES):
            there = jnp.where(number == at, me + down * tiles_w + right, there)
        chosen = jnp.where(there == other, 1.0, 0.0)
        table = jnp.dot(
            chosen, ranks, precision=lax.Precision.HIGHEST, preferred_element_type=jnp.float32
        )
        i, j = (row - REACH) % tile_h, (col - REACH) % tile_w
        down = jnp.where(row < REACH, -1, jnp.where(row >= REACH + tile_h, 1, 0))
        right = jnp.where(side[0], -1, jnp.where(side[1], 1, 0))
        place = jnp.zeros(cell.shape, jnp.int32)
        for at, (top, left) in enumerate(CORNERS):
            rows = ((i < REACH), (i >= REACH) & (i < tile_h - REACH), (i >= tile_h - REACH))[top]
            cols = ((j < REACH), (j >= REACH) & (j < tile_w - REACH), (j >= tile_w - REACH))[left]
            first_i = (0, REACH, tile_h - REACH)[top]
            first_j = (0, REACH, tile_w - REACH)[left]
            span = tile_w - 2 * REACH if left == 1 else REACH
            found = int(cuts[at]) + (i - first_i) * span + (j - first_j)
            place = jnp.where(rows & cols, found, place)
        spot = jnp.where(place == two, 1.0, 0.0)
        border = lax.dot_general(
            spot,
            table,
            (((1,), (1,)), ((), ())),
            precision=lax.Precision.HIGHEST,
            preferred_element_type=jnp.float32,
        )
        which_side = jnp.full(cell.shape, -1, jnp.int32)
        for at, (one_down, one_right) in enumerate(SIDES):
            which_side = jnp.where((down == one_down) & (right == one_right), at, which_side)
        own = jnp.sum(jnp.where(tile == me, starts[:, :1], 0.0), 0, keepdims=True).astype(jnp.int32)
        rank = jnp.where(rank_ref[0] > 0, rank_ref[0] + own, 0)
        rank = jnp.where(which_side >= 0, pick(which_side, border), rank) - 1
        peer = rank & (peers - 1)
        nth = rank // peers - (pick(which, mine) - peer + peers - 1) // peers
        row = row + (me // tiles_w) * tile_h - REACH
        col = col + (me % tiles_w) * tile_w - REACH
        within = (row >= 0) & (row < tiles_h * tile_h) & (col >= 0) & (col < tiles_w * tile_w)
        slot = jnp.where(rank >= 0, peer * SLOTS + base + nth, -1)
        slot_ref[0] = jnp.where(within, slot, -2)

    return pl.pallas_call(
        kernel,
        grid_spec=pltpu.PrefetchScalarGridSpec(
            num_scalar_prefetch=1,
            grid=(samples,),
            in_specs=[
                pl.BlockSpec((1, peers, width), lambda s, _: (s, 0, 0)),
                pl.BlockSpec((1, cells, 1), lambda s, _: (s, 0, 0)),
            ],
            out_specs=[
                pl.BlockSpec((1, peers * SLOTS, 1), lambda s, _: (s, 0, 0)),
                pl.BlockSpec((1, cells, 1), lambda s, _: (s, 0, 0)),
            ],
        ),
        out_shape=[
            jax.ShapeDtypeStruct((samples, peers * SLOTS, 1), jnp.int32),
            jax.ShapeDtypeStruct((samples, cells, 1), jnp.int32),
        ],
        compiler_params=params(16),
        name="index",
    )(me.reshape(1), told, rank)


def inside(height, width, out_h, out_w, reach):
    row = lax.axis_index("row") * height - reach + jnp.arange(out_h, dtype=jnp.int32)
    col = lax.axis_index("col") * width - reach + jnp.arange(out_w, dtype=jnp.int32)
    row_in = (row >= 0) & (row < lax.axis_size("row") * height)
    col_in = (col >= 0) & (col < lax.axis_size("col") * width)
    return row_in[:, None] & col_in[None, :]


def shards(
    patches,
    keep_mask,
    mask_token,
    qkv_weight,
    out_weight,
    up_weight,
    down_weight,
    dec_proj,
    conv_weight,
    head_weight,
):
    peers = lax.axis_size(PLANE)
    me = lax.axis_index(PLANE)
    samples, tile_h, tile_w, width = patches.shape
    tile = tile_h * tile_w
    cap = tile // peers
    kept = tile // 4
    flat_mask = keep_mask.reshape(samples, tile)
    order, ends = ring(tile_h, tile_w)
    order = jnp.asarray(order.reshape(-1))
    marks, edge = len(ends), int(ends[-2])
    spots = np.arange(edge, dtype=np.int32)
    low = jnp.asarray(np.concatenate([np.zeros_like(ends), spots]))
    high = jnp.asarray(np.concatenate([ends, spots + 1]))
    sums = (order[:, None] >= low[None, :]) & (order[:, None] < high[None, :])
    sums = sums.astype(jnp.bfloat16)
    counts = dot(flat_mask.astype(jnp.bfloat16), sums).astype(jnp.int32)
    told_all = lax.all_to_all(
        jnp.broadcast_to(counts.reshape(1, 1, counts.size), (peers, 1, counts.size)),
        PLANE,
        split_axis=0,
        concat_axis=0,
        tiled=True,
    ).reshape(peers, samples, marks + edge)
    told = told_all[:, :, marks - 1]
    before = order[:, None] < order[None, :]
    running = dot(flat_mask.astype(jnp.bfloat16), before.astype(jnp.bfloat16)).astype(jnp.int32)
    cell_rank = jnp.where(flat_mask == 1, running, -1)

    ids = jnp.arange(peers, dtype=jnp.int32)
    earlier = ids[:, None] < ids[None, :]
    starts = jnp.sum(jnp.where(earlier[:, :, None], told[:, None, :], 0), 0)
    my_start = jnp.sum(jnp.where((ids < me)[:, None], told, 0), 0)

    outgoing = dispatch(
        my_start, cell_rank.reshape(samples, 1, tile), patches.reshape(samples, tile, width), peers
    )
    outgoing, *halves = lax.optimization_barrier((outgoing, up_weight, down_weight))
    piece = share(*halves)
    pieces = from_dp(piece)
    arrived = lax.all_to_all(outgoing, PLANE, split_axis=0, concat_axis=0, tiled=True)

    slot = jnp.arange(cap, dtype=jnp.int32)[None, None, :]
    local = slot * peers + ((me - starts.T[:, :, None]) & (peers - 1))
    token = (starts.T[:, :, None] + local - me) // peers
    token = jnp.where(local < told.T[:, :, None], token, -1)

    tiles = lax.axis_size("row"), lax.axis_size("col")
    high, wide = tile_h + 2 * REACH, -(-(tile_w + 2 * REACH) // 8) * 8
    rank = (cell_rank + 1).reshape(samples, tile_h, tile_w)
    rank = jnp.pad(rank, ((0, 0), (REACH, REACH), (REACH, wide - tile_w - REACH)))
    back, cell_slot = index(
        me,
        told_all.transpose(1, 0, 2),
        rank.reshape(samples, high * wide, 1),
        ends,
        tiles,
        tile_h,
        tile_w,
        wide,
    )

    x, packed = project(arrived, token.reshape(samples, 1, tile), qkv_weight, kept)
    packed = lax.all_to_all(packed, PLANE, split_axis=0, concat_axis=0, tiled=True)
    mixed = attention(packed, kept)
    mixed, *pieces = lax.optimization_barrier((mixed, *pieces))
    pieces = pieces + [from_partner(one) for one in pieces]
    mixed = lax.all_to_all(mixed, PLANE, split_axis=0, concat_axis=0, tiled=True)
    returning = feed_forward(
        mixed,
        x,
        back,
        out_weight,
        up_weight,
        down_weight,
        dec_proj,
        pieces,
        SLOTS,
    )
    home = lax.all_to_all(returning, PLANE, split_axis=0, concat_axis=0, tiled=True)

    h_zero = place(home, cell_slot, mask_token, dec_proj, high * wide)
    h_zero = h_zero.reshape(samples, high, wide, h_zero.shape[-1])[:, :, : tile_w + 2 * REACH]
    conv_one = convolve(h_zero, conv_weight[0], tile_h + 2, tile_w + 2)
    h_one = h_zero[:, 1:-1, 1:-1].astype(jnp.float32) + gelu(conv_one)
    within = inside(tile_h, tile_w, tile_h + 2, tile_w + 2, 1)
    h_one = jnp.where(within[None, :, :, None], h_one, 0.0).astype(jnp.bfloat16)
    conv_two = convolve(h_one, conv_weight[1], tile_h, tile_w)
    h_two = (h_one[:, 1:-1, 1:-1].astype(jnp.float32) + gelu(conv_two)).astype(jnp.bfloat16)
    return dot(h_two, head_weight).astype(jnp.bfloat16)


def solution(mesh):
    return jax.shard_map(
        shards,
        mesh=mesh,
        in_specs=(
            P("dp", "row", "col", None),
            P("dp", "row", "col"),
            P(),
            P(),
            P(),
            P(None, "dp"),
            P("dp", None),
            P(),
            P(),
            P(),
        ),
        out_specs=P("dp", "row", "col", None),
        check_vma=False,
    )
```

```python
import jax
import jax.numpy as jnp
import numpy as np
from jax import lax
from jax.experimental import pallas as pl
from jax.experimental.pallas import tpu as pltpu
from jax.sharding import PartitionSpec as P


HD = 64
EPS = 1e-06
LOG2E = 1.4426950408889634
ROOT_HALF = 0.7071067811865476
PLANE = ("row", "col")
MIB = 1 << 20
ATTENTION_MIB = 34
SAFE = 96.0
EXTRA = 16


def ring(height, width):
    bands = (slice(0, REACH), slice(REACH, -REACH), slice(-REACH, None))
    order = np.zeros((height, width), np.int32)
    ends = [0]
    for row, col in CORNERS + ((1, 1),):
        block = order[bands[row], bands[col]]
        block[...] = ends[-1] + np.arange(block.size, dtype=np.int32).reshape(block.shape)
        ends.append(ends[-1] + block.size)
    return order, np.array(ends, np.int32)


PIECES = (
    (0, 0, 0, 9, 16),
    (-1, 0, 4, 7, 2),
    (1, 0, 0, 3, 2),
    (0, -1, 2, 5, 1),
    (0, 1, 6, 8, 1),
    (0, 1, 0, 1, 1),
    (-1, -1, 4, 5, 1),
    (-1, 1, 6, 7, 1),
    (1, -1, 2, 3, 1),
    (1, 1, 0, 1, 1),
)
REACH = 2
SLOTS = 32
SIDES = ((-1, 0), (1, 0), (0, -1), (0, 1), (-1, -1), (-1, 1), (1, -1), (1, 1))
CORNERS = ((0, 0), (0, 1), (0, 2), (1, 2), (2, 2), (2, 1), (2, 0), (1, 0))


def normalize(wide):
    mean = jnp.mean(wide, -1, keepdims=True)
    centred = wide - mean
    var = jnp.mean(centred * centred, -1, keepdims=True)
    return (centred * lax.rsqrt(var + EPS)).astype(jnp.bfloat16)


def gelu(value):
    return 0.5 * value * (1.0 + lax.erf(value * ROOT_HALF))


def dot(left, right):
    return jnp.dot(left, right, preferred_element_type=jnp.float32)


def one_hot(left, right):
    return jnp.where(left == right, 1.0, 0.0).astype(jnp.bfloat16)


def convolve(extended, taps, out_h, out_w):
    total = None
    for first in range(3):
        for second in range(3):
            term = jnp.einsum(
                "shwc,cd->shwd",
                extended[:, first : first + out_h, second : second + out_w],
                taps[first * 3 + second],
                preferred_element_type=jnp.float32,
            )
            total = term if total is None else total + term
    return total


def in_hbm(array):
    return pltpu.with_memory_space_constraint(array, pltpu.HBM)


def params(limit):
    return pltpu.CompilerParams(vmem_limit_bytes=limit * MIB)


def compact(cell_rank, tokens, peers):
    samples, tile, width = tokens.shape
    cap = tile // peers

    def kernel(rank_ref, token_ref, out_ref):
        slot = lax.broadcasted_iota(jnp.int32, (tile, 1), 0)
        rank = (slot % cap) * peers + slot // cap
        chosen = one_hot(rank, rank_ref[...].reshape(1, tile))
        rows = dot(chosen, token_ref[...].reshape(tile, width)).astype(jnp.bfloat16)
        rows = rows.reshape(peers, 1, cap, width)
        out_ref[:peers] = rows
        out_ref[peers:] = rows

    return pl.pallas_call(
        kernel,
        grid=(samples,),
        in_specs=[
            pl.BlockSpec((1, 1, tile), lambda s: (s, 0, 0)),
            pl.BlockSpec((1, tile, width), lambda s: (s, 0, 0)),
        ],
        out_specs=pl.BlockSpec((2 * peers, 1, cap, width), lambda s: (0, s, 0, 0)),
        out_shape=jax.ShapeDtypeStruct((2 * peers, samples, cap, width), jnp.bfloat16),
        compiler_params=params(20),
        name="compact",
    )(cell_rank, in_hbm(tokens))


def dispatch(my_start, twice):
    peers, samples, cap, width = twice.shape
    peers = peers // 2

    def kernel(start_ref, twice_ref, out_hbm, sems):
        copies = []
        for sample in range(samples):
            turn = (-start_ref[sample]) & (peers - 1)
            source = twice_ref.at[pl.ds(turn, peers), sample]
            copies.append(pltpu.make_async_copy(source, out_hbm.at[:, sample], sems.at[sample]))
            copies[-1].start()
        for copy in copies:
            copy.wait()

    return pl.pallas_call(
        kernel,
        in_specs=[pl.BlockSpec(memory_space=pltpu.SMEM), pl.BlockSpec(memory_space=pltpu.VMEM)],
        out_specs=pl.BlockSpec(memory_space=pltpu.HBM),
        out_shape=pltpu.HBM((peers, samples, cap, width), jnp.bfloat16),
        scratch_shapes=[pltpu.SemaphoreType.DMA((samples,))],
        compiler_params=params(8),
        name="dispatch",
    )(my_start, twice)


def project(arrived, token_col, qkv_weight, kept):
    peers, samples, cap, width = arrived.shape
    tile = peers * cap
    lanes = 2 * HD
    groups = width // lanes
    places = peers // samples
    half = kept // 2

    def kernel(col_ref, arrived_ref, weight_hbm, x_hbm, out_ref, weight, x_ref, sems):
        copies = []
        for third in range(3):
            cols = pl.ds(third * width, width)
            copies.append(
                pltpu.make_async_copy(weight_hbm.at[:, cols], weight.at[third], sems.at[third])
            )
            copies[-1].start()
        token = lax.broadcasted_iota(jnp.int32, (kept, 1), 0)
        rows = []
        for sample in range(samples):
            chosen = one_hot(token, col_ref[sample])
            rows.append(dot(chosen, arrived_ref[:, sample].reshape(tile, width)))
            x_ref[sample] = rows[-1].astype(jnp.bfloat16)
        keep = pltpu.make_async_copy(x_ref, x_hbm, sems.at[3])
        keep.start()
        normed = normalize(jnp.concatenate(rows, 0))
        qkv = []
        for third in range(3):
            copies[third].wait()
            qkv.append(dot(normed, weight[third]))
        low = lax.broadcasted_iota(jnp.int32, (kept, lanes), 1) < HD
        low_half = lax.broadcasted_iota(jnp.int32, (half, lanes), 1) < HD
        for sample in range(samples):
            q_all, k_all, v_all = (one[sample * kept : (sample + 1) * kept] for one in qkv)
            for group in range(groups):
                at = group * lanes
                to = sample * places + 2 * group
                q = q_all[:, at : at + lanes] * (0.125 * LOG2E)
                k = k_all[:, at : at + lanes]
                v = v_all[:, at : at + lanes]
                top, bottom = v[:half], v[half:]
                first = jnp.where(low, q, pltpu.roll(k, HD, 1))
                second = jnp.where(low, pltpu.roll(q, HD, 1), k)
                first_v = jnp.where(low_half, top, pltpu.roll(bottom, HD, 1))
                second_v = jnp.where(low_half, pltpu.roll(top, HD, 1), bottom)
                out_ref[to, :kept] = first.astype(jnp.bfloat16)
                out_ref[to, kept:] = first_v.astype(jnp.bfloat16)
                out_ref[to + 1, :kept] = second.astype(jnp.bfloat16)
                out_ref[to + 1, kept:] = second_v.astype(jnp.bfloat16)
            for place in range(2 * groups, places):
                out_ref[sample * places + place] = jnp.zeros((kept + half, lanes), jnp.bfloat16)
        keep.wait()

    return pl.pallas_call(
        kernel,
        in_specs=[pl.BlockSpec(memory_space=pltpu.VMEM)] * 2 + [pl.BlockSpec(memory_space=pltpu.HBM)],
        out_specs=[pl.BlockSpec(memory_space=pltpu.HBM), pl.BlockSpec(memory_space=pltpu.VMEM)],
        out_shape=[
            pltpu.HBM((samples, kept, width), jnp.bfloat16),
            jax.ShapeDtypeStruct((peers, kept + half, lanes), jnp.bfloat16),
        ],
        scratch_shapes=[
            pltpu.VMEM((3, width, width), jnp.bfloat16),
            pltpu.VMEM((samples, kept, width), jnp.bfloat16),
            pltpu.SemaphoreType.DMA((4,)),
        ],
        compiler_params=params(20),
        name="project",
    )(token_col, arrived, in_hbm(qkv_weight))


def attention(packed, kept):
    peers, _, lanes = packed.shape
    half = kept // 2
    keys = peers * half
    step = 8
    contract = (((1,), (1,)), ((), ()))

    def kernel(packed_ref, out_ref, low_key, high_key, low_value, high_value, bound):
        at = pl.program_id(0)

        @pl.when(at == 0)
        def _():
            lane = lax.broadcasted_iota(jnp.int32, (kept, lanes), 1)
            most_q = jnp.zeros((kept, 1), jnp.float32)
            most_k = jnp.zeros((kept, 1), jnp.float32)
            for peer in range(peers):
                rows = pl.ds(peer * half, half)
                wide = packed_ref[peer, :kept].astype(jnp.float32)
                both = pltpu.roll(wide, HD, 1).astype(jnp.bfloat16)
                low_key[rows] = both[:half]
                high_key[rows] = both[half:]
                square = wide * wide
                size_q = jnp.sum(jnp.where(lane < HD, square, 0.0), -1, keepdims=True)
                size_k = jnp.sum(jnp.where(lane < HD, 0.0, square), -1, keepdims=True)
                most_q = jnp.maximum(most_q, size_q)
                most_k = jnp.maximum(most_k, size_k)
            for pair in range(peers // 2):
                cols = pl.ds(pair * 2 * half, 2 * half)
                turned = packed_ref[2 * pair : 2 * pair + 2, kept:].reshape(2 * half, lanes)
                turned = turned.astype(jnp.float32).T.astype(jnp.bfloat16)
                low_value[:HD, cols] = turned[:HD]
                high_value[:HD, cols] = turned[HD:]
            low_value[HD:] = jnp.ones((EXTRA, keys), jnp.bfloat16)
            high_value[HD:] = jnp.ones((EXTRA, keys), jnp.bfloat16)
            bound[0] = jnp.max(most_q) * jnp.max(most_k)

        def finish(low, high, first, count):
            mixed = dot(low_value[...], low) + dot(high_value[...], high)
            mixed = mixed[:HD] / mixed[HD : HD + 1]
            for one in range(count):
                here = mixed[:, one * kept : (one + 1) * kept]
                both = jnp.concatenate([here, pltpu.roll(here, half, 1)], 0).T
                out_ref[first + one] = both[:half].astype(jnp.bfloat16)

        def queries(first, count):
            query = packed_ref[pl.ds(at * step + first, count), :kept].reshape(count * kept, lanes)
            lane = lax.broadcasted_iota(jnp.int32, query.shape, 1)
            return jnp.where(lane < HD, query, jnp.zeros_like(query))

        def score(query, key):
            return lax.dot_general(key[...], query, contract, preferred_element_type=jnp.float32)

        narrow = bound[0] < SAFE * SAFE

        @pl.when(narrow)
        def _():
            query = queries(0, step)
            low = jnp.exp2(score(query, low_key)).astype(jnp.bfloat16)
            high = jnp.exp2(score(query, high_key)).astype(jnp.bfloat16)
            finish(low, high, 0, step)

        @pl.when(jnp.logical_not(narrow))
        def _():
            @pl.loop(0, step)
            def _(one):
                query = queries(one, 1)
                low, high = score(query, low_key), score(query, high_key)
                top = jnp.maximum(jnp.max(low, 0, keepdims=True), jnp.max(high, 0, keepdims=True))
                low = jnp.exp2(low - top).astype(jnp.bfloat16)
                high = jnp.exp2(high - top).astype(jnp.bfloat16)
                finish(low, high, one, 1)

    return pl.pallas_call(
        kernel,
        grid=(peers // step,),
        in_specs=[pl.BlockSpec(packed.shape, lambda i: (0, 0, 0))],
        out_specs=pl.BlockSpec((step, half, lanes), lambda i: (i, 0, 0)),
        out_shape=jax.ShapeDtypeStruct((peers, half, lanes), jnp.bfloat16),
        scratch_shapes=[
            pltpu.VMEM((keys, lanes), jnp.bfloat16),
            pltpu.VMEM((keys, lanes), jnp.bfloat16),
            pltpu.VMEM((HD + EXTRA, keys), jnp.bfloat16),
            pltpu.VMEM((HD + EXTRA, keys), jnp.bfloat16),
            pltpu.SMEM((1,), jnp.float32),
        ],
        compiler_params=params(ATTENTION_MIB),
        name="attention",
    )(packed)


def fetch(arrays):
    count = len(arrays)

    def kernel(*refs):
        sources, held, sems = refs[:count], refs[count : 2 * count], refs[-1]
        copies = [
            pltpu.make_async_copy(source, kept, sems.at[at])
            for at, (source, kept) in enumerate(zip(sources, held))
        ]
        for copy in copies:
            copy.start()
        for copy in copies:
            copy.wait()

    return pl.pallas_call(
        kernel,
        in_specs=[pl.BlockSpec(memory_space=pltpu.HBM)] * count,
        out_specs=[pl.BlockSpec(memory_space=pltpu.VMEM)] * count,
        out_shape=[pltpu.VMEM(one.shape, one.dtype) for one in arrays],
        scratch_shapes=[pltpu.SemaphoreType.DMA((count,))],
        compiler_params=params(2),
        name="fetch",
    )(*[in_hbm(one) for one in arrays])


def feed_forward(mixed, x, token_col, out_weight, up, down, dec_proj, pieces, slots):
    peers, half, lanes = mixed.shape
    samples, kept, width = x.shape
    places = peers // samples
    narrow = dec_proj.shape[1]

    weights = [in_hbm(one) for one in (down, *pieces, dec_proj)]
    count = len(weights)

    def kernel(mixed_ref, x_ref, col_hbm, out_w, up_ref, *rest):
        sources, out_ref, held = rest[:count], rest[count], rest[count + 1 : -2]
        col_ref, sems = rest[-2:]
        slots_in = pltpu.make_async_copy(col_hbm, col_ref, sems.at[count])
        copies = [
            pltpu.make_async_copy(source, held[at], sems.at[at])
            for at, source in enumerate(sources)
        ]
        slots_in.start()
        ahead = 4
        for copy in copies[:ahead]:
            copy.start()

        def ready(at):
            copies[at].wait()
            if at + ahead < count:
                copies[at + ahead].start()
            return held[at]

        low = lax.broadcasted_iota(jnp.int32, (half, lanes), 1) < HD
        attn = []
        for sample in range(samples):
            parts = []
            for group in range(width // lanes):
                one = mixed_ref[sample * places + 2 * group].astype(jnp.float32)
                two = mixed_ref[sample * places + 2 * group + 1].astype(jnp.float32)
                top = jnp.where(low, one, pltpu.roll(two, HD, 1))
                bottom = jnp.where(low, pltpu.roll(one, HD, 1), two)
                parts.append(jnp.concatenate([top, bottom], 0).astype(jnp.bfloat16))
            attn.append(jnp.concatenate(parts, 1))
        attn = jnp.concatenate(attn, 0)
        rows = x_ref[...].reshape(samples * kept, width)
        x_one = (rows.astype(jnp.float32) + dot(attn, out_w[...])).astype(jnp.bfloat16)
        normed = normalize(x_one.astype(jnp.float32))
        raised = dot(normed, up_ref[...])
        total = jnp.zeros((samples * kept, width), jnp.float32)
        lower = ready(0)
        for at in range(1, count):
            piece = ready(at)
            later = dot(normed, piece[:width]) if at < count - 1 else None
            inner = gelu(raised).astype(jnp.bfloat16)
            if at == 1:
                total = total + dot(inner, lower[...])
            else:
                part = lower.shape[1]
                ends = range(width, lower.shape[0], part)
                added = [dot(inner, lower[pl.ds(end, part)]) for end in ends]
                total = total + jnp.concatenate(added, 1)
            raised, lower = later, piece
        encoded = (x_one.astype(jnp.float32) + total).astype(jnp.bfloat16)
        field = dot(encoded, held[count - 1][...]).astype(jnp.bfloat16)
        slots_in.wait()
        for sample in range(samples):
            token = lax.broadcasted_iota(jnp.int32, (1, kept), 1)
            chosen = one_hot(col_ref[sample], token)
            sent = dot(chosen, field[sample * kept : (sample + 1) * kept])
            out_ref[:, sample] = sent.astype(jnp.bfloat16).reshape(peers, slots, narrow)

    return pl.pallas_call(
        kernel,
        in_specs=[pl.BlockSpec(memory_space=pltpu.VMEM)] * 2
        + [pl.BlockSpec(memory_space=pltpu.HBM)]
        + [pl.BlockSpec(memory_space=pltpu.VMEM)] * 2
        + [pl.BlockSpec(memory_space=pltpu.HBM)] * count,
        out_specs=pl.BlockSpec(memory_space=pltpu.VMEM),
        out_shape=jax.ShapeDtypeStruct((peers, samples, slots, narrow), jnp.bfloat16),
        scratch_shapes=[pltpu.VMEM(one.shape, one.dtype) for one in weights]
        + [pltpu.VMEM(token_col.shape, jnp.int32), pltpu.SemaphoreType.DMA((count + 1,))],
        compiler_params=params(32),
        name="feed_forward",
    )(mixed, x, in_hbm(token_col), out_weight, up, *weights)


def share(up_weight, down_weight):
    width, hidden = up_weight.shape
    part = hidden // 2
    at = (lax.axis_index("row") % 2) * part
    up = lax.dynamic_slice_in_dim(up_weight, at, part, axis=1)
    down = lax.dynamic_slice_in_dim(down_weight, at, part, axis=0)
    return jnp.concatenate([up] + [down[:, i : i + part] for i in range(0, width, part)], 0)


def from_dp(piece):
    count = lax.axis_size("dp")
    return [
        lax.ppermute(piece, "dp", [(i, (i + hop) % count) for i in range(count)])
        for hop in range(1, count)
    ]


def from_partner(piece):
    return lax.ppermute(piece, "row", [(i, i ^ 1) for i in range(lax.axis_size("row"))])


def place(home, cell_slot, mask_token, dec_proj, cells):
    peers, samples, slots, narrow = home.shape
    width = dec_proj.shape[0]

    def kernel(slot_ref, home_ref, token_ref, dec_ref, out_ref):
        slot = slot_ref[0]
        chosen = one_hot(slot, lax.broadcasted_iota(jnp.int32, (1, peers * slots), 1))
        rows = dot(chosen, home_ref[...].reshape(peers * slots, narrow))
        blank = dot(jnp.broadcast_to(token_ref[...], (8, width)), dec_ref[...])[:1]
        out_ref[0] = jnp.where(slot == -1, blank, rows).astype(jnp.bfloat16)

    return pl.pallas_call(
        kernel,
        grid=(samples,),
        in_specs=[
            pl.BlockSpec((1, cells, 1), lambda s: (s, 0, 0)),
            pl.BlockSpec((peers, 1, slots, narrow), lambda s: (0, s, 0, 0)),
            pl.BlockSpec((1, width), lambda s: (0, 0)),
            pl.BlockSpec((width, narrow), lambda s: (0, 0)),
        ],
        out_specs=pl.BlockSpec((1, cells, narrow), lambda s: (s, 0, 0)),
        out_shape=jax.ShapeDtypeStruct((samples, cells, narrow), jnp.bfloat16),
        compiler_params=params(16),
        name="place",
    )(cell_slot, home, mask_token.reshape(1, width), dec_proj)


def pick(which, table):
    lane = lax.broadcasted_iota(jnp.int32, (1, table.shape[1]), 1)
    found = jnp.sum(jnp.where(which == lane, table, 0.0), -1, keepdims=True)
    return found.astype(jnp.int32)


def index(me, told, rank, cuts, tiles, tile_h, tile_w, wide):
    samples, peers, width = told.shape
    marks = len(cuts)
    edge = width - marks
    tiles_h, tiles_w = tiles
    cells = rank.shape[1]
    bases = [sum(piece[4] for piece in PIECES[:number]) for number in range(len(PIECES))]

    def kernel(me_ref, told_ref, rank_ref, back_ref, slot_ref):
        me = me_ref[0]
        ahead = told_ref[0][:, :marks].astype(jnp.float32)
        bits = told_ref[0][:, marks:].astype(jnp.float32)
        tile = lax.broadcasted_iota(jnp.int32, (peers, 1), 0)
        other = lax.broadcasted_iota(jnp.int32, (1, peers), 1)
        earlier = jnp.where(other < tile, 1.0, 0.0)
        totals = jnp.broadcast_to(ahead[:, marks - 1 :], (peers, 128))
        starts = jnp.dot(
            earlier, totals, precision=lax.Precision.HIGHEST, preferred_element_type=jnp.float32
        )
        lane = lax.broadcasted_iota(jnp.int32, (1, 128), 1)
        begins = jnp.zeros((peers, 128), jnp.float32)
        ends = jnp.zeros((peers, 128), jnp.float32)
        for number, (down, right, first, last, _) in enumerate(PIECES):
            row, col = tile // tiles_w + down, tile % tiles_w + right
            there = (row >= 0) & (row < tiles_h) & (col >= 0) & (col < tiles_w) & (lane == number)
            for side, mark in enumerate((first, last)):
                value = ahead[:, mark : mark + 1] + starts
                hop = (-(down * tiles_w + right)) % peers
                if hop:
                    value = pltpu.roll(value, hop, 0)
                if side:
                    ends = jnp.where(there, value, ends)
                else:
                    begins = jnp.where(there, value, begins)

        at = lax.broadcasted_iota(jnp.int32, (peers * SLOTS, 1), 0)
        expand = jnp.where(at // SLOTS == other, 1.0, 0.0)
        at = at % SLOTS
        which = jnp.full(at.shape, len(PIECES), jnp.int32)
        nth = jnp.zeros(at.shape, jnp.int32)
        for number, base in enumerate(bases):
            here = (at >= base) & (at < base + PIECES[number][4])
            which = jnp.where(here, number, which)
            nth = jnp.where(here, at - base, nth)

        def spread(table):
            rows = jnp.dot(
                expand, table, precision=lax.Precision.HIGHEST, preferred_element_type=jnp.float32
            )
            return pick(which, rows)

        position = (spread(begins) - me + peers - 1) // peers + nth
        back_ref[0] = jnp.where(position * peers + me < spread(ends), position, -1)

        cell = lax.broadcasted_iota(jnp.int32, (cells, 1), 0)
        row, col = cell // wide, cell % wide
        side = [(col < REACH), (col >= REACH + tile_w)]
        which = jnp.where(row < REACH, 1, jnp.where(row >= REACH + tile_h, 2, 0))
        right = jnp.where(row < 2 * REACH, 5, 4)
        left = jnp.where(which == 0, 3, jnp.where(which == 1, 6, 8))
        right = jnp.where(which == 0, right, jnp.where(which == 1, 7, 9))
        which = jnp.where(side[0], left, jnp.where(side[1], right, which))
        base = jnp.zeros(cell.shape, jnp.int32)
        for number in range(1, len(bases)):
            base = jnp.where(which == number, bases[number], base)
        mine = jnp.sum(jnp.where(tile == me, begins, 0.0), 0, keepdims=True)

        one = lax.broadcasted_iota(jnp.int32, (edge, 1), 0)
        two = lax.broadcasted_iota(jnp.int32, (1, edge), 1)
        ranks = dot(bits.astype(jnp.bfloat16), jnp.where(one < two, 1.0, 0.0).astype(jnp.bfloat16))
        ranks = jnp.where(bits > 0.5, ranks + starts[:, :1] + 1.0, 0.0)
        number = lax.broadcasted_iota(jnp.int32, (128, 1), 0)
        there = jnp.full((128, 1), -1, jnp.int32)
        for at, (down, right) in enumerate(SIDES):
            there = jnp.where(number == at, me + down * tiles_w + right, there)
        chosen = jnp.where(there == other, 1.0, 0.0)
        table = jnp.dot(
            chosen, ranks, precision=lax.Precision.HIGHEST, preferred_element_type=jnp.float32
        )
        i, j = (row - REACH) % tile_h, (col - REACH) % tile_w
        down = jnp.where(row < REACH, -1, jnp.where(row >= REACH + tile_h, 1, 0))
        right = jnp.where(side[0], -1, jnp.where(side[1], 1, 0))
        place = jnp.zeros(cell.shape, jnp.int32)
        for at, (top, left) in enumerate(CORNERS):
            rows = ((i < REACH), (i >= REACH) & (i < tile_h - REACH), (i >= tile_h - REACH))[top]
            cols = ((j < REACH), (j >= REACH) & (j < tile_w - REACH), (j >= tile_w - REACH))[left]
            first_i = (0, REACH, tile_h - REACH)[top]
            first_j = (0, REACH, tile_w - REACH)[left]
            span = tile_w - 2 * REACH if left == 1 else REACH
            found = int(cuts[at]) + (i - first_i) * span + (j - first_j)
            place = jnp.where(rows & cols, found, place)
        spot = jnp.where(place == two, 1.0, 0.0)
        border = lax.dot_general(
            spot,
            table,
            (((1,), (1,)), ((), ())),
            precision=lax.Precision.HIGHEST,
            preferred_element_type=jnp.float32,
        )
        which_side = jnp.full(cell.shape, -1, jnp.int32)
        for at, (one_down, one_right) in enumerate(SIDES):
            which_side = jnp.where((down == one_down) & (right == one_right), at, which_side)
        own = jnp.sum(jnp.where(tile == me, starts[:, :1], 0.0), 0, keepdims=True).astype(jnp.int32)
        rank = jnp.where(rank_ref[0] > 0, rank_ref[0] + own, 0)
        rank = jnp.where(which_side >= 0, pick(which_side, border), rank) - 1
        peer = rank & (peers - 1)
        nth = rank // peers - (pick(which, mine) - peer + peers - 1) // peers
        row = row + (me // tiles_w) * tile_h - REACH
        col = col + (me % tiles_w) * tile_w - REACH
        within = (row >= 0) & (row < tiles_h * tile_h) & (col >= 0) & (col < tiles_w * tile_w)
        slot = jnp.where(rank >= 0, peer * SLOTS + base + nth, -1)
        slot_ref[0] = jnp.where(within, slot, -2)

    return pl.pallas_call(
        kernel,
        grid_spec=pltpu.PrefetchScalarGridSpec(
            num_scalar_prefetch=1,
            grid=(samples,),
            in_specs=[
                pl.BlockSpec((1, peers, width), lambda s, _: (s, 0, 0)),
                pl.BlockSpec((1, cells, 1), lambda s, _: (s, 0, 0)),
            ],
            out_specs=[
                pl.BlockSpec((1, peers * SLOTS, 1), lambda s, _: (s, 0, 0)),
                pl.BlockSpec((1, cells, 1), lambda s, _: (s, 0, 0)),
            ],
        ),
        out_shape=[
            jax.ShapeDtypeStruct((samples, peers * SLOTS, 1), jnp.int32),
            jax.ShapeDtypeStruct((samples, cells, 1), jnp.int32),
        ],
        compiler_params=params(16),
        name="index",
    )(me.reshape(1), told, rank)


def inside(height, width, out_h, out_w, reach):
    row = lax.axis_index("row") * height - reach + jnp.arange(out_h, dtype=jnp.int32)
    col = lax.axis_index("col") * width - reach + jnp.arange(out_w, dtype=jnp.int32)
    row_in = (row >= 0) & (row < lax.axis_size("row") * height)
    col_in = (col >= 0) & (col < lax.axis_size("col") * width)
    return row_in[:, None] & col_in[None, :]


def shards(
    patches,
    keep_mask,
    mask_token,
    qkv_weight,
    out_weight,
    up_weight,
    down_weight,
    dec_proj,
    conv_weight,
    head_weight,
):
    peers = lax.axis_size(PLANE)
    me = lax.axis_index(PLANE)
    samples, tile_h, tile_w, width = patches.shape
    tile = tile_h * tile_w
    cap = tile // peers
    kept = tile // 4
    flat_mask = keep_mask.reshape(samples, tile)
    order, ends = ring(tile_h, tile_w)
    order = jnp.asarray(order.reshape(-1))
    marks, edge = len(ends), int(ends[-2])
    spots = np.arange(edge, dtype=np.int32)
    low = jnp.asarray(np.concatenate([np.zeros_like(ends), spots]))
    high = jnp.asarray(np.concatenate([ends, spots + 1]))
    sums = (order[:, None] >= low[None, :]) & (order[:, None] < high[None, :])
    sums = sums.astype(jnp.bfloat16)
    counts = dot(flat_mask.astype(jnp.bfloat16), sums).astype(jnp.int32)
    told_all = lax.all_to_all(
        jnp.broadcast_to(counts.reshape(1, 1, counts.size), (peers, 1, counts.size)),
        PLANE,
        split_axis=0,
        concat_axis=0,
        tiled=True,
    )
    told_all = told_all.reshape(peers, samples, marks + edge)
    told = told_all[:, :, marks - 1]
    before = order[:, None] < order[None, :]
    running = dot(flat_mask.astype(jnp.bfloat16), before.astype(jnp.bfloat16)).astype(jnp.int32)
    cell_rank = jnp.where(flat_mask == 1, running, -1)
    twice = compact(
        cell_rank.reshape(samples, 1, tile), patches.reshape(samples, tile, width), peers
    )

    ids = jnp.arange(peers, dtype=jnp.int32)
    earlier = ids[:, None] < ids[None, :]
    starts = jnp.sum(jnp.where(earlier[:, :, None], told[:, None, :], 0), 0)
    my_start = jnp.sum(jnp.where((ids < me)[:, None], told, 0), 0)

    outgoing = dispatch(my_start, twice)
    outgoing, *halves = lax.optimization_barrier((outgoing, up_weight, down_weight))
    piece = share(*halves)
    pieces = from_dp(piece)
    arrived = lax.all_to_all(outgoing, PLANE, split_axis=0, concat_axis=0, tiled=True)

    slot = jnp.arange(cap, dtype=jnp.int32)[None, None, :]
    local = slot * peers + ((me - starts.T[:, :, None]) & (peers - 1))
    token = (starts.T[:, :, None] + local - me) // peers
    token = jnp.where(local < told.T[:, :, None], token, -1)

    tiles = lax.axis_size("row"), lax.axis_size("col")
    high, wide = tile_h + 2 * REACH, -(-(tile_w + 2 * REACH) // 8) * 8
    rank = (cell_rank + 1).reshape(samples, tile_h, tile_w)
    rank = jnp.pad(rank, ((0, 0), (REACH, REACH), (REACH, wide - tile_w - REACH)))
    back, cell_slot = index(
        me,
        told_all.transpose(1, 0, 2),
        rank.reshape(samples, high * wide, 1),
        ends,
        tiles,
        tile_h,
        tile_w,
        wide,
    )

    x, packed = project(arrived, token.reshape(samples, 1, tile), qkv_weight, kept)
    packed = lax.all_to_all(packed, PLANE, split_axis=0, concat_axis=0, tiled=True)
    mixed = attention(packed, kept)
    mixed, *pieces = lax.optimization_barrier((mixed, *pieces))
    pieces = pieces + [from_partner(one) for one in pieces]
    out_near, up_near = fetch([out_weight, up_weight])
    mixed = lax.all_to_all(mixed, PLANE, split_axis=0, concat_axis=0, tiled=True)
    returning = feed_forward(
        mixed,
        x,
        back,
        out_near,
        up_near,
        down_weight,
        dec_proj,
        pieces,
        SLOTS,
    )
    home = lax.all_to_all(returning, PLANE, split_axis=0, concat_axis=0, tiled=True)

    h_zero = place(home, cell_slot, mask_token, dec_proj, high * wide)
    h_zero = h_zero.reshape(samples, high, wide, h_zero.shape[-1])[:, :, : tile_w + 2 * REACH]
    conv_one = convolve(h_zero, conv_weight[0], tile_h + 2, tile_w + 2)
    h_one = h_zero[:, 1:-1, 1:-1].astype(jnp.float32) + gelu(conv_one)
    within = inside(tile_h, tile_w, tile_h + 2, tile_w + 2, 1)
    h_one = jnp.where(within[None, :, :, None], h_one, 0.0).astype(jnp.bfloat16)
    conv_two = convolve(h_one, conv_weight[1], tile_h, tile_w)
    h_two = (h_one[:, 1:-1, 1:-1].astype(jnp.float32) + gelu(conv_two)).astype(jnp.bfloat16)
    return dot(h_two, head_weight).astype(jnp.bfloat16)


def solution(mesh):
    return jax.shard_map(
        shards,
        mesh=mesh,
        in_specs=(
            P("dp", "row", "col", None),
            P("dp", "row", "col"),
            P(),
            P(),
            P(),
            P(None, "dp"),
            P("dp", None),
            P(),
            P(),
            P(),
        ),
        out_specs=P("dp", "row", "col", None),
        check_vma=False,
    )
```

```python
import jax
import jax.numpy as jnp
import numpy as np
from jax import lax
from jax.experimental import pallas as pl
from jax.experimental.pallas import tpu as pltpu
from jax.sharding import PartitionSpec as P


HD = 64
EPS = 1e-06
LOG2E = 1.4426950408889634
ROOT_HALF = 0.7071067811865476
PLANE = ("row", "col")
MIB = 1 << 20
ATTENTION_MIB = 34
SAFE = 96.0
EXTRA = 16


def ring(height, width):
    bands = (slice(0, REACH), slice(REACH, -REACH), slice(-REACH, None))
    order = np.zeros((height, width), np.int32)
    ends = [0]
    for row, col in CORNERS + ((1, 1),):
        block = order[bands[row], bands[col]]
        block[...] = ends[-1] + np.arange(block.size, dtype=np.int32).reshape(block.shape)
        ends.append(ends[-1] + block.size)
    return order, np.array(ends, np.int32)


PIECES = (
    (0, 0, 0, 9, 16),
    (-1, 0, 4, 7, 2),
    (1, 0, 0, 3, 2),
    (0, -1, 2, 5, 1),
    (0, 1, 6, 8, 1),
    (0, 1, 0, 1, 1),
    (-1, -1, 4, 5, 1),
    (-1, 1, 6, 7, 1),
    (1, -1, 2, 3, 1),
    (1, 1, 0, 1, 1),
)
REACH = 2
SLOTS = 32
SIDES = ((-1, 0), (1, 0), (0, -1), (0, 1), (-1, -1), (-1, 1), (1, -1), (1, 1))
CORNERS = ((0, 0), (0, 1), (0, 2), (1, 2), (2, 2), (2, 1), (2, 0), (1, 0))


def normalize(wide):
    mean = jnp.mean(wide, -1, keepdims=True)
    centred = wide - mean
    var = jnp.mean(centred * centred, -1, keepdims=True)
    return (centred * lax.rsqrt(var + EPS)).astype(jnp.bfloat16)


def gelu(value):
    return 0.5 * value * (1.0 + lax.erf(value * ROOT_HALF))


def dot(left, right):
    return jnp.dot(left, right, preferred_element_type=jnp.float32)


def one_hot(left, right):
    return jnp.where(left == right, 1.0, 0.0).astype(jnp.bfloat16)


def convolve(extended, taps, out_h, out_w):
    total = None
    for first in range(3):
        for second in range(3):
            term = jnp.einsum(
                "shwc,cd->shwd",
                extended[:, first : first + out_h, second : second + out_w],
                taps[first * 3 + second],
                preferred_element_type=jnp.float32,
            )
            total = term if total is None else total + term
    return total


def in_hbm(array):
    return pltpu.with_memory_space_constraint(array, pltpu.HBM)


def params(limit):
    return pltpu.CompilerParams(vmem_limit_bytes=limit * MIB)


def compact(cell_rank, tokens, peers):
    samples, tile, width = tokens.shape
    cap = tile // peers

    def kernel(rank_ref, token_ref, out_ref):
        slot = lax.broadcasted_iota(jnp.int32, (tile, 1), 0)
        rank = (slot % cap) * peers + slot // cap
        chosen = one_hot(rank, rank_ref[...].reshape(1, tile))
        rows = dot(chosen, token_ref[...].reshape(tile, width)).astype(jnp.bfloat16)
        rows = rows.reshape(peers, 1, cap, width)
        out_ref[:peers] = rows
        out_ref[peers:] = rows

    return pl.pallas_call(
        kernel,
        grid=(samples,),
        in_specs=[
            pl.BlockSpec((1, 1, tile), lambda s: (s, 0, 0)),
            pl.BlockSpec((1, tile, width), lambda s: (s, 0, 0)),
        ],
        out_specs=pl.BlockSpec((2 * peers, 1, cap, width), lambda s: (0, s, 0, 0)),
        out_shape=jax.ShapeDtypeStruct((2 * peers, samples, cap, width), jnp.bfloat16),
        compiler_params=params(20),
        name="compact",
    )(cell_rank, in_hbm(tokens))


def dispatch(my_start, twice):
    peers, samples, cap, width = twice.shape
    peers = peers // 2

    def kernel(start_ref, twice_ref, out_hbm, sems):
        copies = []
        for sample in range(samples):
            turn = (-start_ref[sample]) & (peers - 1)
            source = twice_ref.at[pl.ds(turn, peers), sample]
            copies.append(pltpu.make_async_copy(source, out_hbm.at[:, sample], sems.at[sample]))
            copies[-1].start()
        for copy in copies:
            copy.wait()

    return pl.pallas_call(
        kernel,
        in_specs=[pl.BlockSpec(memory_space=pltpu.SMEM), pl.BlockSpec(memory_space=pltpu.VMEM)],
        out_specs=pl.BlockSpec(memory_space=pltpu.HBM),
        out_shape=pltpu.HBM((peers, samples, cap, width), jnp.bfloat16),
        scratch_shapes=[pltpu.SemaphoreType.DMA((samples,))],
        compiler_params=params(8),
        name="dispatch",
    )(my_start, twice)


def project(arrived, token_col, q_weight, qkv_weight, kept):
    peers, samples, cap, width = arrived.shape
    tile = peers * cap
    lanes = 2 * HD
    groups = width // lanes
    places = peers // samples
    half = kept // 2

    def kernel(col_ref, arrived_ref, weight_ref, weight_hbm, x_hbm, out_ref, weight, x_ref, sems):
        copies = []
        for third in (1, 2):
            cols = pl.ds(third * width, width)
            copies.append(
                pltpu.make_async_copy(weight_hbm.at[:, cols], weight.at[third - 1], sems.at[third])
            )
            copies[-1].start()
        token = lax.broadcasted_iota(jnp.int32, (kept, 1), 0)
        rows = []
        for sample in range(samples):
            chosen = one_hot(token, col_ref[sample])
            rows.append(dot(chosen, arrived_ref[:, sample].reshape(tile, width)))
            x_ref[sample] = rows[-1].astype(jnp.bfloat16)
        keep = pltpu.make_async_copy(x_ref, x_hbm, sems.at[0])
        keep.start()
        normed = normalize(jnp.concatenate(rows, 0))
        qkv = [dot(normed, weight_ref[...])]
        for at, copy in enumerate(copies):
            copy.wait()
            qkv.append(dot(normed, weight[at]))
        low = lax.broadcasted_iota(jnp.int32, (kept, lanes), 1) < HD
        low_half = lax.broadcasted_iota(jnp.int32, (half, lanes), 1) < HD
        for sample in range(samples):
            q_all, k_all, v_all = (one[sample * kept : (sample + 1) * kept] for one in qkv)
            for group in range(groups):
                at = group * lanes
                to = sample * places + 2 * group
                q = q_all[:, at : at + lanes] * (0.125 * LOG2E)
                k = k_all[:, at : at + lanes]
                v = v_all[:, at : at + lanes]
                top, bottom = v[:half], v[half:]
                first = jnp.where(low, q, pltpu.roll(k, HD, 1))
                second = jnp.where(low, pltpu.roll(q, HD, 1), k)
                first_v = jnp.where(low_half, top, pltpu.roll(bottom, HD, 1))
                second_v = jnp.where(low_half, pltpu.roll(top, HD, 1), bottom)
                out_ref[to, :kept] = first.astype(jnp.bfloat16)
                out_ref[to, kept:] = first_v.astype(jnp.bfloat16)
                out_ref[to + 1, :kept] = second.astype(jnp.bfloat16)
                out_ref[to + 1, kept:] = second_v.astype(jnp.bfloat16)
            for place in range(2 * groups, places):
                out_ref[sample * places + place] = jnp.zeros((kept + half, lanes), jnp.bfloat16)
        keep.wait()

    return pl.pallas_call(
        kernel,
        in_specs=[pl.BlockSpec(memory_space=pltpu.VMEM)] * 3 + [pl.BlockSpec(memory_space=pltpu.HBM)],
        out_specs=[
            pl.BlockSpec(memory_space=pltpu.HBM),
            pl.BlockSpec((peers, kept + half, lanes), lambda: (0, 0, 0)),
        ],
        out_shape=[
            pltpu.HBM((samples, kept, width), jnp.bfloat16),
            pltpu.HBM((peers, kept + half, lanes), jnp.bfloat16),
        ],
        scratch_shapes=[
            pltpu.VMEM((2, width, width), jnp.bfloat16),
            pltpu.VMEM((samples, kept, width), jnp.bfloat16),
            pltpu.SemaphoreType.DMA((3,)),
        ],
        compiler_params=params(20),
        name="project",
    )(token_col, arrived, q_weight, in_hbm(qkv_weight))


def attention(packed, kept):
    peers, _, lanes = packed.shape
    half = kept // 2
    keys = peers * half
    step = 8
    contract = (((1,), (1,)), ((), ()))

    def kernel(packed_ref, out_ref, low_key, high_key, low_value, high_value, bound):
        at = pl.program_id(0)

        @pl.when(at == 0)
        def _():
            lane = lax.broadcasted_iota(jnp.int32, (kept, lanes), 1)
            most_q = jnp.zeros((kept, 1), jnp.float32)
            most_k = jnp.zeros((kept, 1), jnp.float32)
            for peer in range(peers):
                rows = pl.ds(peer * half, half)
                wide = packed_ref[peer, :kept].astype(jnp.float32)
                both = pltpu.roll(wide, HD, 1).astype(jnp.bfloat16)
                low_key[rows] = both[:half]
                high_key[rows] = both[half:]
                square = wide * wide
                size_q = jnp.sum(jnp.where(lane < HD, square, 0.0), -1, keepdims=True)
                size_k = jnp.sum(jnp.where(lane < HD, 0.0, square), -1, keepdims=True)
                most_q = jnp.maximum(most_q, size_q)
                most_k = jnp.maximum(most_k, size_k)
            for pair in range(peers // 2):
                cols = pl.ds(pair * 2 * half, 2 * half)
                turned = packed_ref[2 * pair : 2 * pair + 2, kept:].reshape(2 * half, lanes)
                turned = turned.astype(jnp.float32).T.astype(jnp.bfloat16)
                low_value[:HD, cols] = turned[:HD]
                high_value[:HD, cols] = turned[HD:]
            low_value[HD:] = jnp.ones((EXTRA, keys), jnp.bfloat16)
            high_value[HD:] = jnp.ones((EXTRA, keys), jnp.bfloat16)
            bound[0] = jnp.max(most_q) * jnp.max(most_k)

        def finish(low, high, first, count):
            mixed = dot(low_value[...], low) + dot(high_value[...], high)
            mixed = mixed[:HD] / mixed[HD : HD + 1]
            for one in range(count):
                here = mixed[:, one * kept : (one + 1) * kept]
                both = jnp.concatenate([here, pltpu.roll(here, half, 1)], 0).T
                out_ref[first + one] = both[:half].astype(jnp.bfloat16)

        def queries(first, count):
            query = packed_ref[pl.ds(at * step + first, count), :kept].reshape(count * kept, lanes)
            lane = lax.broadcasted_iota(jnp.int32, query.shape, 1)
            return jnp.where(lane < HD, query, jnp.zeros_like(query))

        def score(query, key):
            return lax.dot_general(key[...], query, contract, preferred_element_type=jnp.float32)

        narrow = bound[0] < SAFE * SAFE

        @pl.when(narrow)
        def _():
            query = queries(0, step)
            low = jnp.exp2(score(query, low_key)).astype(jnp.bfloat16)
            high = jnp.exp2(score(query, high_key)).astype(jnp.bfloat16)
            finish(low, high, 0, step)

        @pl.when(jnp.logical_not(narrow))
        def _():
            @pl.loop(0, step)
            def _(one):
                query = queries(one, 1)
                low, high = score(query, low_key), score(query, high_key)
                top = jnp.maximum(jnp.max(low, 0, keepdims=True), jnp.max(high, 0, keepdims=True))
                low = jnp.exp2(low - top).astype(jnp.bfloat16)
                high = jnp.exp2(high - top).astype(jnp.bfloat16)
                finish(low, high, one, 1)

    return pl.pallas_call(
        kernel,
        grid=(peers // step,),
        in_specs=[pl.BlockSpec(packed.shape, lambda i: (0, 0, 0))],
        out_specs=pl.BlockSpec((step, half, lanes), lambda i: (i, 0, 0)),
        out_shape=jax.ShapeDtypeStruct((peers, half, lanes), jnp.bfloat16),
        scratch_shapes=[
            pltpu.VMEM((keys, lanes), jnp.bfloat16),
            pltpu.VMEM((keys, lanes), jnp.bfloat16),
            pltpu.VMEM((HD + EXTRA, keys), jnp.bfloat16),
            pltpu.VMEM((HD + EXTRA, keys), jnp.bfloat16),
            pltpu.SMEM((1,), jnp.float32),
        ],
        compiler_params=params(ATTENTION_MIB),
        name="attention",
    )(packed)


def fetch(arrays, columns):
    count = len(arrays)

    def kernel(*refs):
        sources, held, sems = refs[:count], refs[count : 2 * count], refs[-1]
        copies = [
            pltpu.make_async_copy(source.at[:, pl.ds(0, columns)], kept, sems.at[at])
            for at, (source, kept) in enumerate(zip(sources, held))
        ]
        for copy in copies:
            copy.start()
        for copy in copies:
            copy.wait()

    return pl.pallas_call(
        kernel,
        in_specs=[pl.BlockSpec(memory_space=pltpu.HBM)] * count,
        out_specs=[pl.BlockSpec(memory_space=pltpu.VMEM)] * count,
        out_shape=[pltpu.VMEM((one.shape[0], columns), one.dtype) for one in arrays],
        scratch_shapes=[pltpu.SemaphoreType.DMA((count,))],
        compiler_params=params(2),
        name="fetch",
    )(*[in_hbm(one) for one in arrays])


def feed_forward(mixed, x, token_col, out_weight, up, down, dec_proj, pieces, slots):
    peers, half, lanes = mixed.shape
    samples, kept, width = x.shape
    places = peers // samples
    narrow = dec_proj.shape[1]

    weights = [in_hbm(one) for one in (down, *pieces, dec_proj)]
    count = len(weights)

    def kernel(mixed_ref, x_ref, col_ref, out_w, up_ref, *rest):
        sources, out_ref, held = rest[:count], rest[count], rest[count + 1 : -1]
        sems = rest[-1]
        copies = [
            pltpu.make_async_copy(source, held[at], sems.at[at])
            for at, source in enumerate(sources)
        ]
        ahead = count
        for copy in copies[:ahead]:
            copy.start()

        def ready(at):
            copies[at].wait()
            if at + ahead < count:
                copies[at + ahead].start()
            return held[at]

        low = lax.broadcasted_iota(jnp.int32, (half, lanes), 1) < HD
        attn = []
        for sample in range(samples):
            parts = []
            for group in range(width // lanes):
                one = mixed_ref[sample * places + 2 * group].astype(jnp.float32)
                two = mixed_ref[sample * places + 2 * group + 1].astype(jnp.float32)
                top = jnp.where(low, one, pltpu.roll(two, HD, 1))
                bottom = jnp.where(low, pltpu.roll(one, HD, 1), two)
                parts.append(jnp.concatenate([top, bottom], 0).astype(jnp.bfloat16))
            attn.append(jnp.concatenate(parts, 1))
        attn = jnp.concatenate(attn, 0)
        rows = x_ref[...].reshape(samples * kept, width)
        x_one = (rows.astype(jnp.float32) + dot(attn, out_w[...])).astype(jnp.bfloat16)
        normed = normalize(x_one.astype(jnp.float32))
        raised = dot(normed, up_ref[...])
        total = jnp.zeros((samples * kept, width), jnp.float32)
        lower = ready(0)
        for at in range(1, count):
            piece = ready(at)
            later = dot(normed, piece[:width]) if at < count - 1 else None
            inner = gelu(raised).astype(jnp.bfloat16)
            if at == 1:
                total = total + dot(inner, lower[...])
            else:
                part = lower.shape[1]
                ends = range(width, lower.shape[0], part)
                added = [dot(inner, lower[pl.ds(end, part)]) for end in ends]
                total = total + jnp.concatenate(added, 1)
            raised, lower = later, piece
        encoded = (x_one.astype(jnp.float32) + total).astype(jnp.bfloat16)
        field = dot(encoded, held[count - 1][...]).astype(jnp.bfloat16)
        for sample in range(samples):
            token = lax.broadcasted_iota(jnp.int32, (1, kept), 1)
            turned = jnp.broadcast_to(col_ref[sample].astype(jnp.float32), (kept, peers * slots)).T
            chosen = one_hot(turned.astype(jnp.int32), token)
            sent = dot(chosen, field[sample * kept : (sample + 1) * kept])
            out_ref[:, sample] = sent.astype(jnp.bfloat16).reshape(peers, slots, narrow)

    return pl.pallas_call(
        kernel,
        in_specs=[pl.BlockSpec(memory_space=pltpu.VMEM)] * 5
        + [pl.BlockSpec(memory_space=pltpu.HBM)] * count,
        out_specs=pl.BlockSpec(memory_space=pltpu.VMEM),
        out_shape=jax.ShapeDtypeStruct((peers, samples, slots, narrow), jnp.bfloat16),
        scratch_shapes=[pltpu.VMEM(one.shape, one.dtype) for one in weights]
        + [pltpu.SemaphoreType.DMA((count,))],
        compiler_params=params(32),
        name="feed_forward",
    )(mixed, x, token_col, out_weight, up, *weights)


def share(up_weight, down_weight):
    width, hidden = up_weight.shape
    part = hidden // 2
    at = (lax.axis_index("row") % 2) * part
    up = lax.dynamic_slice_in_dim(up_weight, at, part, axis=1)
    down = lax.dynamic_slice_in_dim(down_weight, at, part, axis=0)
    return jnp.concatenate([up] + [down[:, i : i + part] for i in range(0, width, part)], 0)


def from_dp(piece):
    count = lax.axis_size("dp")
    return [
        lax.ppermute(piece, "dp", [(i, (i + hop) % count) for i in range(count)])
        for hop in range(1, count)
    ]


def from_partner(piece):
    return lax.ppermute(piece, "row", [(i, i ^ 1) for i in range(lax.axis_size("row"))])


def place(home, cell_slot, mask_token, dec_proj, cells):
    peers, samples, slots, narrow = home.shape
    width = dec_proj.shape[0]

    def kernel(slot_ref, home_ref, token_ref, dec_ref, out_ref):
        slot = slot_ref[0]
        chosen = one_hot(slot, lax.broadcasted_iota(jnp.int32, (1, peers * slots), 1))
        rows = dot(chosen, home_ref[...].reshape(peers * slots, narrow))
        blank = dot(jnp.broadcast_to(token_ref[...], (8, width)), dec_ref[...])[:1]
        out_ref[0] = jnp.where(slot == -1, blank, rows).astype(jnp.bfloat16)

    return pl.pallas_call(
        kernel,
        grid=(samples,),
        in_specs=[
            pl.BlockSpec((1, cells, 1), lambda s: (s, 0, 0)),
            pl.BlockSpec((peers, 1, slots, narrow), lambda s: (0, s, 0, 0)),
            pl.BlockSpec((1, width), lambda s: (0, 0)),
            pl.BlockSpec((width, narrow), lambda s: (0, 0)),
        ],
        out_specs=pl.BlockSpec((1, cells, narrow), lambda s: (s, 0, 0)),
        out_shape=jax.ShapeDtypeStruct((samples, cells, narrow), jnp.bfloat16),
        compiler_params=params(16),
        name="place",
    )(cell_slot, home, mask_token.reshape(1, width), dec_proj)


def pick(which, table):
    lane = lax.broadcasted_iota(jnp.int32, (1, table.shape[1]), 1)
    found = jnp.sum(jnp.where(which == lane, table, 0.0), -1, keepdims=True)
    return found.astype(jnp.int32)


def index(me, told, rank, cuts, tiles, tile_h, tile_w, wide):
    samples, peers, width = told.shape
    marks = len(cuts)
    edge = width - marks
    tiles_h, tiles_w = tiles
    cells = rank.shape[1]
    bases = [sum(piece[4] for piece in PIECES[:number]) for number in range(len(PIECES))]

    def kernel(me_ref, told_ref, rank_ref, back_ref, slot_ref):
        me = me_ref[0]
        ahead = told_ref[0][:, :marks].astype(jnp.float32)
        bits = told_ref[0][:, marks:].astype(jnp.float32)
        tile = lax.broadcasted_iota(jnp.int32, (peers, 1), 0)
        other = lax.broadcasted_iota(jnp.int32, (1, peers), 1)
        earlier = jnp.where(other < tile, 1.0, 0.0)
        totals = jnp.broadcast_to(ahead[:, marks - 1 :], (peers, 128))
        starts = jnp.dot(
            earlier, totals, precision=lax.Precision.HIGHEST, preferred_element_type=jnp.float32
        )
        lane = lax.broadcasted_iota(jnp.int32, (1, 128), 1)
        begins = jnp.zeros((peers, 128), jnp.float32)
        ends = jnp.zeros((peers, 128), jnp.float32)
        for number, (down, right, first, last, _) in enumerate(PIECES):
            row, col = tile // tiles_w + down, tile % tiles_w + right
            there = (row >= 0) & (row < tiles_h) & (col >= 0) & (col < tiles_w) & (lane == number)
            for side, mark in enumerate((first, last)):
                value = ahead[:, mark : mark + 1] + starts
                hop = (-(down * tiles_w + right)) % peers
                if hop:
                    value = pltpu.roll(value, hop, 0)
                if side:
                    ends = jnp.where(there, value, ends)
                else:
                    begins = jnp.where(there, value, begins)

        at = lax.broadcasted_iota(jnp.int32, (peers * SLOTS, 1), 0)
        expand = jnp.where(at // SLOTS == other, 1.0, 0.0)
        at = at % SLOTS
        which = jnp.full(at.shape, len(PIECES), jnp.int32)
        nth = jnp.zeros(at.shape, jnp.int32)
        for number, base in enumerate(bases):
            here = (at >= base) & (at < base + PIECES[number][4])
            which = jnp.where(here, number, which)
            nth = jnp.where(here, at - base, nth)

        def spread(table):
            rows = jnp.dot(
                expand, table, precision=lax.Precision.HIGHEST, preferred_element_type=jnp.float32
            )
            return pick(which, rows)

        position = (spread(begins) - me + peers - 1) // peers + nth
        back = jnp.where(position * peers + me < spread(ends), position, -1)
        back = jnp.broadcast_to(back.astype(jnp.float32), (peers * SLOTS, 128)).T
        back_ref[0] = back[:1].astype(jnp.int32)

        cell = lax.broadcasted_iota(jnp.int32, (cells, 1), 0)
        row, col = cell // wide, cell % wide
        side = [(col < REACH), (col >= REACH + tile_w)]
        which = jnp.where(row < REACH, 1, jnp.where(row >= REACH + tile_h, 2, 0))
        right = jnp.where(row < 2 * REACH, 5, 4)
        left = jnp.where(which == 0, 3, jnp.where(which == 1, 6, 8))
        right = jnp.where(which == 0, right, jnp.where(which == 1, 7, 9))
        which = jnp.where(side[0], left, jnp.where(side[1], right, which))
        base = jnp.zeros(cell.shape, jnp.int32)
        for number in range(1, len(bases)):
            base = jnp.where(which == number, bases[number], base)
        mine = jnp.sum(jnp.where(tile == me, begins, 0.0), 0, keepdims=True)

        one = lax.broadcasted_iota(jnp.int32, (edge, 1), 0)
        two = lax.broadcasted_iota(jnp.int32, (1, edge), 1)
        ranks = dot(bits.astype(jnp.bfloat16), jnp.where(one < two, 1.0, 0.0).astype(jnp.bfloat16))
        ranks = jnp.where(bits > 0.5, ranks + starts[:, :1] + 1.0, 0.0)
        number = lax.broadcasted_iota(jnp.int32, (128, 1), 0)
        there = jnp.full((128, 1), -1, jnp.int32)
        for at, (down, right) in enumerate(SIDES):
            there = jnp.where(number == at, me + down * tiles_w + right, there)
        chosen = jnp.where(there == other, 1.0, 0.0)
        table = jnp.dot(
            chosen, ranks, precision=lax.Precision.HIGHEST, preferred_element_type=jnp.float32
        )
        i, j = (row - REACH) % tile_h, (col - REACH) % tile_w
        down = jnp.where(row < REACH, -1, jnp.where(row >= REACH + tile_h, 1, 0))
        right = jnp.where(side[0], -1, jnp.where(side[1], 1, 0))
        place = jnp.zeros(cell.shape, jnp.int32)
        for at, (top, left) in enumerate(CORNERS):
            rows = ((i < REACH), (i >= REACH) & (i < tile_h - REACH), (i >= tile_h - REACH))[top]
            cols = ((j < REACH), (j >= REACH) & (j < tile_w - REACH), (j >= tile_w - REACH))[left]
            first_i = (0, REACH, tile_h - REACH)[top]
            first_j = (0, REACH, tile_w - REACH)[left]
            span = tile_w - 2 * REACH if left == 1 else REACH
            found = int(cuts[at]) + (i - first_i) * span + (j - first_j)
            place = jnp.where(rows & cols, found, place)
        spot = jnp.where(place == two, 1.0, 0.0)
        border = lax.dot_general(
            spot,
            table,
            (((1,), (1,)), ((), ())),
            precision=lax.Precision.HIGHEST,
            preferred_element_type=jnp.float32,
        )
        which_side = jnp.full(cell.shape, -1, jnp.int32)
        for at, (one_down, one_right) in enumerate(SIDES):
            which_side = jnp.where((down == one_down) & (right == one_right), at, which_side)
        own = jnp.sum(jnp.where(tile == me, starts[:, :1], 0.0), 0, keepdims=True).astype(jnp.int32)
        rank = jnp.where(rank_ref[0] > 0, rank_ref[0] + own, 0)
        rank = jnp.where(which_side >= 0, pick(which_side, border), rank) - 1
        peer = rank & (peers - 1)
        nth = rank // peers - (pick(which, mine) - peer + peers - 1) // peers
        row = row + (me // tiles_w) * tile_h - REACH
        col = col + (me % tiles_w) * tile_w - REACH
        within = (row >= 0) & (row < tiles_h * tile_h) & (col >= 0) & (col < tiles_w * tile_w)
        slot = jnp.where(rank >= 0, peer * SLOTS + base + nth, -1)
        slot_ref[0] = jnp.where(within, slot, -2)

    return pl.pallas_call(
        kernel,
        grid_spec=pltpu.PrefetchScalarGridSpec(
            num_scalar_prefetch=1,
            grid=(samples,),
            in_specs=[
                pl.BlockSpec((1, peers, width), lambda s, _: (s, 0, 0)),
                pl.BlockSpec((1, cells, 1), lambda s, _: (s, 0, 0)),
            ],
            out_specs=[
                pl.BlockSpec((1, 1, peers * SLOTS), lambda s, _: (s, 0, 0)),
                pl.BlockSpec((1, cells, 1), lambda s, _: (s, 0, 0)),
            ],
        ),
        out_shape=[
            jax.ShapeDtypeStruct((samples, 1, peers * SLOTS), jnp.int32),
            jax.ShapeDtypeStruct((samples, cells, 1), jnp.int32),
        ],
        compiler_params=params(16),
        name="index",
    )(me.reshape(1), told, rank)


def inside(height, width, out_h, out_w, reach):
    row = lax.axis_index("row") * height - reach + jnp.arange(out_h, dtype=jnp.int32)
    col = lax.axis_index("col") * width - reach + jnp.arange(out_w, dtype=jnp.int32)
    row_in = (row >= 0) & (row < lax.axis_size("row") * height)
    col_in = (col >= 0) & (col < lax.axis_size("col") * width)
    return row_in[:, None] & col_in[None, :]


def shards(
    patches,
    keep_mask,
    mask_token,
    qkv_weight,
    out_weight,
    up_weight,
    down_weight,
    dec_proj,
    conv_weight,
    head_weight,
):
    peers = lax.axis_size(PLANE)
    me = lax.axis_index(PLANE)
    samples, tile_h, tile_w, width = patches.shape
    tile = tile_h * tile_w
    cap = tile // peers
    kept = tile // 4
    flat_mask = keep_mask.reshape(samples, tile)
    order, ends = ring(tile_h, tile_w)
    order = jnp.asarray(order.reshape(-1))
    marks, edge = len(ends), int(ends[-2])
    spots = np.arange(edge, dtype=np.int32)
    low = jnp.asarray(np.concatenate([np.zeros_like(ends), spots]))
    high = jnp.asarray(np.concatenate([ends, spots + 1]))
    sums = (order[:, None] >= low[None, :]) & (order[:, None] < high[None, :])
    sums = sums.astype(jnp.bfloat16)
    counts = dot(flat_mask.astype(jnp.bfloat16), sums).astype(jnp.int32)
    told_all = lax.all_to_all(
        jnp.broadcast_to(counts.reshape(1, 1, counts.size), (peers, 1, counts.size)),
        PLANE,
        split_axis=0,
        concat_axis=0,
        tiled=True,
    )
    told_all = told_all.reshape(peers, samples, marks + edge)
    told = told_all[:, :, marks - 1]
    before = order[:, None] < order[None, :]
    running = dot(flat_mask.astype(jnp.bfloat16), before.astype(jnp.bfloat16)).astype(jnp.int32)
    cell_rank = jnp.where(flat_mask == 1, running, -1)
    twice = compact(
        cell_rank.reshape(samples, 1, tile), patches.reshape(samples, tile, width), peers
    )

    ids = jnp.arange(peers, dtype=jnp.int32)
    earlier = ids[:, None] < ids[None, :]
    starts = jnp.sum(jnp.where(earlier[:, :, None], told[:, None, :], 0), 0)
    my_start = jnp.sum(jnp.where((ids < me)[:, None], told, 0), 0)

    outgoing = dispatch(my_start, twice)
    outgoing, *halves = lax.optimization_barrier((outgoing, up_weight, down_weight))
    piece = share(*halves)
    pieces = from_dp(piece)
    arrived = lax.all_to_all(outgoing, PLANE, split_axis=0, concat_axis=0, tiled=True)

    slot = jnp.arange(cap, dtype=jnp.int32)[None, None, :]
    local = slot * peers + ((me - starts.T[:, :, None]) & (peers - 1))
    token = (starts.T[:, :, None] + local - me) // peers
    token = jnp.where(local < told.T[:, :, None], token, -1)

    tiles = lax.axis_size("row"), lax.axis_size("col")
    high, wide = tile_h + 2 * REACH, -(-(tile_w + 2 * REACH) // 8) * 8
    rank = (cell_rank + 1).reshape(samples, tile_h, tile_w)
    rank = jnp.pad(rank, ((0, 0), (REACH, REACH), (REACH, wide - tile_w - REACH)))
    back, cell_slot = index(
        me,
        told_all.transpose(1, 0, 2),
        rank.reshape(samples, high * wide, 1),
        ends,
        tiles,
        tile_h,
        tile_w,
        wide,
    )

    (q_near,) = fetch([qkv_weight], width)
    x, packed = project(arrived, token.reshape(samples, 1, tile), q_near, qkv_weight, kept)
    packed = lax.all_to_all(packed, PLANE, split_axis=0, concat_axis=0, tiled=True)
    mixed = attention(packed, kept)
    mixed, *pieces = lax.optimization_barrier((mixed, *pieces))
    pieces = pieces + [from_partner(one) for one in pieces]
    out_near, up_near = fetch([out_weight, up_weight], width)
    mixed = lax.all_to_all(mixed, PLANE, split_axis=0, concat_axis=0, tiled=True)
    returning = feed_forward(
        mixed,
        x,
        back,
        out_near,
        up_near,
        down_weight,
        dec_proj,
        pieces,
        SLOTS,
    )
    home = lax.all_to_all(returning, PLANE, split_axis=0, concat_axis=0, tiled=True)

    h_zero = place(home, cell_slot, mask_token, dec_proj, high * wide)
    h_zero = h_zero.reshape(samples, high, wide, h_zero.shape[-1])[:, :, : tile_w + 2 * REACH]
    conv_one = convolve(h_zero, conv_weight[0], tile_h + 2, tile_w + 2)
    h_one = h_zero[:, 1:-1, 1:-1].astype(jnp.float32) + gelu(conv_one)
    within = inside(tile_h, tile_w, tile_h + 2, tile_w + 2, 1)
    h_one = jnp.where(within[None, :, :, None], h_one, 0.0).astype(jnp.bfloat16)
    conv_two = convolve(h_one, conv_weight[1], tile_h, tile_w)
    h_two = (h_one[:, 1:-1, 1:-1].astype(jnp.float32) + gelu(conv_two)).astype(jnp.bfloat16)
    return dot(h_two, head_weight).astype(jnp.bfloat16)


def solution(mesh):
    return jax.shard_map(
        shards,
        mesh=mesh,
        in_specs=(
            P("dp", "row", "col", None),
            P("dp", "row", "col"),
            P(),
            P(),
            P(),
            P(None, "dp"),
            P("dp", None),
            P(),
            P(),
            P(),
        ),
        out_specs=P("dp", "row", "col", None),
        check_vma=False,
    )
```
